128 devices in a mesh: tm: 16 (over x_hi, y, core), height: 8 (over x_lo, z).
Axes of the slice: x: 4 (x_hi: 2, x_lo: 2; x = x_hi * 2 + x_lo), y: 4, z: 4, core: 2. Of those that a mesh axis runs over, the one named last changes fastest.
Arguments:
- tokens: bfloat16 [32, 32, 80, 3072], P('tm', 'height'), may hold values from -6 to 6
- mod_scale: float32 [3072], replicated, may hold values from -3 to 3
- mod_shift: float32 [3072], replicated, may hold values from -3 to 3
- w_qkv: bfloat16 [3072, 4608], P(('tm', 'height')), may hold values from -0.109375 to 0.109375
- q_gain: float32 [128], replicated, may hold values from 0.25 to 1.75
- k_gain: float32 [128], replicated, may hold values from 0.25 to 1.75
- window: int32 [12, 3], replicated, may hold values from 0 to 2, as said below
- valid: int32 [32, 32, 80], replicated, may hold values from 0 to 1, as said below
Outputs:
- attended: bfloat16 [32, 32, 80, 1536], P('tm', 'height')
The draws below stay inside these ranges and needn't reach their ends.
Inputs may be any that keep to these rules, and one draw needn't show every extreme that they name: `window`: column 0 is at most 1, column 1 at most 1, column 2 at most 2; some head has all three at these most values. `valid`: the last frames, rows and columns of the grid may be padding with 0; scattered tokens elsewhere are 0 too.
All inputs are finite; a program needn't handle non-finite values.
Results may differ from the reference program's by a relative error of at most 0.0055.
Values may be sent and summed in bfloat16 or wider, within the bound.
A program may use at most 128 MiB of HBM per device.

```python
import jax
import jax.numpy as jnp
from jax import lax

D = 3072
HDIM = 128
HEADS = 12
TT = 1
TH = 2
TW = 8
WT = 1
WH = 1
WW = 2
FH = 4
W = 80
NT = 32
NH = 32


def draw_window(key, part):
    keys = jax.random.split(jax.random.fold_in(key, 11), 4)
    frames = jax.random.randint(keys[0], (HEADS,), 0, WT + 1)
    rows = jax.random.randint(keys[1], (HEADS,), 0, WH + 1)
    columns = jax.random.randint(keys[2], (HEADS,), 0, WW + 1)
    widest = jax.random.randint(keys[3], (), 0, HEADS)
    chosen = jnp.arange(HEADS) == widest
    frames = jnp.where(chosen, WT, frames)
    rows = jnp.where(chosen, WH, rows)
    columns = jnp.where(chosen, WW, columns)
    return jnp.stack([frames, rows, columns], axis=1).astype(jnp.int32)


def draw_valid(key, part):
    keys = jax.random.split(jax.random.fold_in(key, 23), 4)
    pad_frames = jax.random.randint(keys[0], (), 0, TT + 1)
    pad_rows = jax.random.randint(keys[1], (), 0, TH + 1)
    pad_columns = jax.random.randint(keys[2], (), 0, TW)
    scattered = jax.random.randint(keys[3], (NT, NH, W), 0, 16) != 0
    frame_ok = (jnp.arange(NT) < NT - pad_frames)[:, None, None]
    row_ok = (jnp.arange(NH) < NH - pad_rows)[None, :, None]
    column_ok = (jnp.arange(W) < W - pad_columns)[None, None, :]
    return (scattered & frame_ok & row_ok & column_ok).astype(jnp.int32)


def block_scale(key, shape, cuts, low, high):
    loudness, own = 1.0, jax.random.fold_in(key, 6)
    for position, shards_of in cuts:
        steps = jnp.exp(jax.random.uniform(jax.random.fold_in(own, position), (shards_of,), jnp.float32, low / len(cuts), high / len(cuts)))
        loudness = loudness * jnp.repeat(steps, shape[position] // shards_of).reshape([-1 if axis == position else 1 for axis in range(len(shape))])
    return loudness


def normal_values(stream_key, dims, scale, most, shards=(), kind=jnp.bfloat16):
    drawn = scale * jax.random.normal(stream_key, dims, jnp.float32)
    if shards:
        drawn = drawn * block_scale(stream_key, dims, shards, -0.22, 0.18)
    return jnp.clip(drawn, -most, most).astype(kind)


def setup_inputs(seed: int = 0) -> dict:
    seeds = jax.random.split(jax.random.key(seed), 9)
    tokens = normal_values(seeds[0], (NT, NH, W, D), 1.0, 6.0, ((0, 16), (1, 8)))
    mod_scale = normal_values(seeds[1], (D,), 0.5, 3.0, (), jnp.float32)
    mod_shift = normal_values(seeds[2], (D,), 0.5, 3.0, (), jnp.float32)
    w_qkv = normal_values(seeds[3], (D, 3 * HEADS * HDIM), D ** -0.5, 0.109375, ((0, 128),))
    q_gain = jnp.clip(1.0 + 0.15 * jax.random.normal(seeds[4], (HDIM,), jnp.float32), 0.25, 1.75)
    k_gain = jnp.clip(1.0 + 0.15 * jax.random.normal(seeds[5], (HDIM,), jnp.float32), 0.25, 1.75)
    window = draw_window(jax.random.fold_in(seeds[8], 71), 0)
    valid = draw_valid(jax.random.fold_in(seeds[8], 71), 0)
    return dict(tokens=tokens, mod_scale=mod_scale, mod_shift=mod_shift, w_qkv=w_qkv, q_gain=q_gain, k_gain=k_gain, window=window, valid=valid)


EPS = 1e-06

def modulate(tokens, mod_scale, mod_shift):
    values = tokens.astype(jnp.float32)
    mean = lax.optimization_barrier(jnp.mean(values, axis=-1, keepdims=True))
    centred = values - mean
    variance = lax.optimization_barrier(jnp.mean(centred * centred, axis=-1, keepdims=True))
    normed = centred * lax.rsqrt(variance + EPS)
    return (normed * (1.0 + mod_scale) + mod_shift).astype(jnp.bfloat16)

def head_norm(values, gain):
    power = lax.optimization_barrier(jnp.mean(values * values, axis=-1, keepdims=True))
    return (values * lax.rsqrt(power + EPS) * gain).astype(jnp.bfloat16)

def project(flat, mod_scale, mod_shift, w_qkv, q_gain, k_gain):
    count = flat.shape[0]
    modulated = modulate(flat, mod_scale, mod_shift)
    qkv = jnp.dot(modulated, w_qkv, preferred_element_type=jnp.float32)
    inner = qkv.shape[1] // 3
    query = head_norm(qkv[:, :inner].reshape(count, HEADS, HDIM), q_gain)
    key = head_norm(qkv[:, inner:2 * inner].reshape(count, HEADS, HDIM), k_gain)
    value = qkv[:, 2 * inner:].reshape(count, HEADS, HDIM).astype(jnp.bfloat16)
    return (query, key, value)

def tile_coords(frames, rows, width):
    shape = (frames.shape[0], rows.shape[0], width)
    columns = jnp.arange(width, dtype=jnp.int32)
    frame_tiles = jnp.broadcast_to((frames // TT)[:, None, None], shape).reshape(-1)
    row_tiles = jnp.broadcast_to((rows // TH)[None, :, None], shape).reshape(-1)
    column_tiles = jnp.broadcast_to((columns // TW)[None, None, :], shape).reshape(-1)
    return (frame_tiles, row_tiles, column_tiles)

def distances(query_coords, key_coords):
    return tuple((jnp.abs(qa[:, None] - ka[None, :]) for qa, ka in zip(query_coords, key_coords)))

def reference(tokens, mod_scale, mod_shift, w_qkv, q_gain, k_gain, window, valid):

    def per_frame(frame_tokens):
        query, key, value = project(frame_tokens.reshape(NH * W, D), mod_scale, mod_shift, w_qkv, q_gain, k_gain)
        shape = (NH, W, HEADS, HDIM)
        return (query.reshape(shape), key.reshape(shape), value.reshape(shape))
    query_grid, key_grid, value_grid = lax.map(per_frame, tokens)
    padding = ((TT, TT), (TH, TH), (0, 0), (0, 0), (0, 0))
    key_pad = jnp.pad(key_grid, padding)
    value_pad = jnp.pad(value_grid, padding)
    valid_pad = jnp.pad(valid, ((TT, TT), (TH, TH), (0, 0)))
    bands = NH // FH
    zero = jnp.int32(0)

    def block(index):
        frame = (index // bands).astype(jnp.int32)
        first_row = (index % bands * FH).astype(jnp.int32)
        query = lax.dynamic_slice(query_grid, (frame, first_row, zero, zero, zero), (1, FH, W, HEADS, HDIM)).reshape(-1, HEADS, HDIM)
        key_size = (1 + 2 * TT, FH + 2 * TH, W, HEADS, HDIM)
        key = lax.dynamic_slice(key_pad, (frame, first_row, zero, zero, zero), key_size).reshape(-1, HEADS, HDIM)
        value = lax.dynamic_slice(value_pad, (frame, first_row, zero, zero, zero), key_size).reshape(-1, HEADS, HDIM)
        key_valid = lax.dynamic_slice(valid_pad, (frame, first_row, zero), (1 + 2 * TT, FH + 2 * TH, W)).reshape(-1) > 0
        query_valid = lax.dynamic_slice(valid, (frame, first_row, zero), (1, FH, W)).reshape(-1) > 0
        query_coords = tile_coords(frame + jnp.arange(1, dtype=jnp.int32), first_row + jnp.arange(FH, dtype=jnp.int32), W)
        key_coords = tile_coords(frame - TT + jnp.arange(1 + 2 * TT, dtype=jnp.int32), first_row - TH + jnp.arange(FH + 2 * TH, dtype=jnp.int32), W)
        apart_t, apart_h, apart_w = distances(query_coords, key_coords)
        allowed = (apart_t[None] <= window[:, 0, None, None]) & (apart_h[None] <= window[:, 1, None, None])
        allowed = allowed & (apart_w[None] <= window[:, 2, None, None]) & key_valid[None, None, :]
        scores = jnp.einsum('qhd,khd->hqk', query.astype(jnp.float32), key.astype(jnp.float32)) / jnp.sqrt(jnp.float32(HDIM))
        terms = jnp.where(allowed, jnp.exp(scores), jnp.float32(0.0))
        total = lax.optimization_barrier(jnp.sum(terms, axis=-1, keepdims=True))
        total = jnp.where(query_valid[None, :, None], total, jnp.float32(1.0))
        weights = (terms / total).astype(jnp.bfloat16)
        result = jnp.einsum('hqk,khd->qhd', weights.astype(jnp.float32), value.astype(jnp.float32))
        result = jnp.where(query_valid[:, None, None], result, jnp.float32(0.0)).astype(jnp.bfloat16)
        return result.reshape(FH, W, HEADS * HDIM)
    blocks = lax.map(block, jnp.arange(NT * bands, dtype=jnp.int32))
    return blocks.reshape(NT, NH, W, HEADS * HDIM)
```

```python
import jax
import jax.numpy as jnp
from jax import lax
from jax.sharding import PartitionSpec as P

HDIM = 128
HEADS = 12
TT = 1
TH = 2
TW = 8


EPS = 1e-06


def with_halo(cells, sides, width):
    for axis, dim in sides:
        count = lax.axis_size(axis)
        ends = count - 1
        head = lax.slice_in_dim(cells, 0, width, axis=dim)
        tail = lax.slice_in_dim(cells, cells.shape[dim] - width, cells.shape[dim], axis=dim)
        cells = jnp.concatenate(
            [
                lax.ppermute(tail, axis, [(i, (i + 1) % count) for i in range(ends)]),
                cells,
                lax.ppermute(head, axis, [((i + 1) % count, i) for i in range(ends)]),
            ],
            axis=dim,
        )
    return cells


def modulate(tokens, mod_scale, mod_shift):
    values = tokens.astype(jnp.float32)
    mean = jnp.mean(values, axis=-1, keepdims=True)
    centred = values - mean
    variance = jnp.mean(centred * centred, axis=-1, keepdims=True)
    normed = centred * lax.rsqrt(variance + EPS)
    return (normed * (1.0 + mod_scale) + mod_shift).astype(jnp.bfloat16)


def head_norm(values, gain):
    power = jnp.mean(values * values, axis=-1, keepdims=True)
    return (values * lax.rsqrt(power + EPS) * gain).astype(jnp.bfloat16)


def tile_coords(frames, rows, width):
    shape = (frames.shape[0], rows.shape[0], width)
    columns = jnp.arange(width, dtype=jnp.int32)
    frame_tiles = jnp.broadcast_to((frames // TT)[:, None, None], shape).reshape(-1)
    row_tiles = jnp.broadcast_to((rows // TH)[None, :, None], shape).reshape(-1)
    column_tiles = jnp.broadcast_to((columns // TW)[None, None, :], shape).reshape(-1)
    return (frame_tiles, row_tiles, column_tiles)


def per_device(tokens, mod_scale, mod_shift, w_qkv, q_gain, k_gain, window, valid):
    frame_count, row_count, width, features = tokens.shape
    token_count = frame_count * row_count * width
    modulated = modulate(tokens.reshape(token_count, features), mod_scale, mod_shift)
    band_weight = lax.all_gather(w_qkv, "height", axis=0, tiled=True)
    full_weight = lax.all_gather(band_weight, "tm", axis=0, tiled=True)
    qkv = jnp.dot(modulated, full_weight, preferred_element_type=jnp.float32)
    inner = qkv.shape[1] // 3
    query = head_norm(qkv[:, :inner].reshape(token_count, HEADS, HDIM), q_gain)
    key = head_norm(qkv[:, inner : 2 * inner].reshape(token_count, HEADS, HDIM), k_gain)
    value = qkv[:, 2 * inner :].astype(jnp.bfloat16)
    tiled = (frame_count // TT, TT, row_count // TH, TH, width, inner)
    stacked = jnp.stack([key.reshape(tiled), value.reshape(tiled)])
    extended = with_halo(stacked, (("tm", 1), ("height", 3)), 1)
    frames_ext = frame_count + 2 * TT
    rows_ext = row_count + 2 * TH
    key_count = frames_ext * rows_ext * width
    extended = extended.reshape(2, key_count, HEADS, HDIM)
    key_heads = jnp.transpose(extended[0], (1, 0, 2))
    value_heads = jnp.transpose(extended[1], (1, 0, 2))
    query_heads = jnp.transpose(query, (1, 0, 2))
    frame_block = lax.axis_index("tm")
    row_block = lax.axis_index("height")
    first_frame = frame_block * frame_count
    first_row = row_block * row_count
    zero = jnp.int32(0)
    valid_pad = jnp.pad(valid, ((TT, TT), (TH, TH), (0, 0)))
    key_valid = (
        lax.dynamic_slice(
            valid_pad, (first_frame, first_row, zero), (frames_ext, rows_ext, width)
        ).reshape(-1)
        > 0
    )
    query_valid = (
        lax.dynamic_slice(
            valid, (first_frame, first_row, zero), (frame_count, row_count, width)
        ).reshape(-1)
        > 0
    )
    query_coords = tile_coords(
        first_frame + jnp.arange(frame_count, dtype=jnp.int32),
        first_row + jnp.arange(row_count, dtype=jnp.int32),
        width,
    )
    key_coords = tile_coords(
        first_frame - TT + jnp.arange(frames_ext, dtype=jnp.int32),
        first_row - TH + jnp.arange(rows_ext, dtype=jnp.int32),
        width,
    )
    apart_t, apart_h, apart_w = (
        jnp.abs(qa[:, None] - ka[None, :]) for qa, ka in zip(query_coords, key_coords)
    )
    seen = key_valid[None, :]
    scale = 1.0 / jnp.sqrt(jnp.float32(HDIM))

    def per_head(inputs):
        query_one, key_one, value_one, reach = inputs
        allowed = (apart_t <= reach[0]) & (apart_h <= reach[1]) & (apart_w <= reach[2]) & seen
        scores = (
            jnp.einsum("qd,kd->qk", query_one, key_one, preferred_element_type=jnp.float32) * scale
        )
        terms = jnp.where(allowed, jnp.exp(scores), jnp.float32(0.0))
        total = jnp.sum(terms, axis=-1, keepdims=True)
        total = jnp.where(query_valid[:, None], total, jnp.float32(1.0))
        weights = (terms / total).astype(jnp.bfloat16)
        result = jnp.dot(weights, value_one, preferred_element_type=jnp.float32)
        return jnp.where(query_valid[:, None], result, jnp.float32(0.0)).astype(jnp.bfloat16)

    heads_out = lax.map(per_head, (query_heads, key_heads, value_heads, window))
    attended = jnp.transpose(heads_out, (1, 0, 2)).reshape(frame_count, row_count, width, inner)
    return attended


def solution(mesh):
    in_specs = (
        P("tm", "height", None, None),
        P(),
        P(),
        P(("tm", "height"), None),
        P(),
        P(),
        P(),
        P(),
    )
    out_specs = P("tm", "height", None, None)
    return jax.shard_map(
        per_device, mesh=mesh, in_specs=in_specs, out_specs=out_specs, check_vma=False
    )
```

```python
import jax
import jax.numpy as jnp
from jax import lax
from jax.sharding import PartitionSpec as P
from jax.experimental import pallas as pl
from jax.experimental.pallas import tpu as pltpu

HDIM = 128
HEADS = 12
TT = 1
TH = 2
TW = 8


EPS = 1e-06


def with_halo(cells, sides, width):
    for axis, dim in sides:
        count = lax.axis_size(axis)
        ends = count - 1
        head = lax.slice_in_dim(cells, 0, width, axis=dim)
        tail = lax.slice_in_dim(cells, cells.shape[dim] - width, cells.shape[dim], axis=dim)
        cells = jnp.concatenate(
            [
                lax.ppermute(tail, axis, [(i, (i + 1) % count) for i in range(ends)]),
                cells,
                lax.ppermute(head, axis, [((i + 1) % count, i) for i in range(ends)]),
            ],
            axis=dim,
        )
    return cells


def modulate(tokens, mod_scale, mod_shift):
    values = tokens.astype(jnp.float32)
    mean = jnp.mean(values, axis=-1, keepdims=True)
    centred = values - mean
    variance = jnp.mean(centred * centred, axis=-1, keepdims=True)
    normed = centred * lax.rsqrt(variance + EPS)
    return (normed * (1.0 + mod_scale) + mod_shift).astype(jnp.bfloat16)


def head_norm(values, gain):
    power = jnp.mean(values * values, axis=-1, keepdims=True)
    return (values * lax.rsqrt(power + EPS) * gain).astype(jnp.bfloat16)


def tile_coords(frames, rows, width):
    shape = (frames.shape[0], rows.shape[0], width)
    columns = jnp.arange(width, dtype=jnp.int32)
    frame_tiles = jnp.broadcast_to((frames // TT)[:, None, None], shape).reshape(-1)
    row_tiles = jnp.broadcast_to((rows // TH)[None, :, None], shape).reshape(-1)
    column_tiles = jnp.broadcast_to((columns // TW)[None, None, :], shape).reshape(-1)
    return (frame_tiles, row_tiles, column_tiles)


def per_device(tokens, mod_scale, mod_shift, w_qkv, q_gain, k_gain, window, valid):
    frame_count, row_count, width, features = tokens.shape
    token_count = frame_count * row_count * width
    modulated = modulate(tokens.reshape(token_count, features), mod_scale, mod_shift)
    band_weight = lax.all_gather(w_qkv, "height", axis=0, tiled=True)
    full_weight = lax.all_gather(band_weight, "tm", axis=0, tiled=True)
    qkv = jnp.dot(modulated, full_weight, preferred_element_type=jnp.float32)
    inner = qkv.shape[1] // 3
    query = head_norm(qkv[:, :inner].reshape(token_count, HEADS, HDIM), q_gain)
    key = head_norm(qkv[:, inner : 2 * inner].reshape(token_count, HEADS, HDIM), k_gain)
    value = qkv[:, 2 * inner :].astype(jnp.bfloat16)
    tiled = (frame_count // TT, TT, row_count // TH, TH, width, inner)
    stacked = jnp.stack([key.reshape(tiled), value.reshape(tiled)])
    extended = with_halo(stacked, (("tm", 1), ("height", 3)), 1)
    frames_ext = frame_count + 2 * TT
    rows_ext = row_count + 2 * TH
    extended = extended.reshape(2, frames_ext, rows_ext, width, inner)
    frame_block = lax.axis_index("tm")
    row_block = lax.axis_index("height")
    first_frame = frame_block * frame_count
    first_row = row_block * row_count
    zero = jnp.int32(0)
    valid_pad = jnp.pad(valid, ((TT, TT), (TH, TH), (0, 0)))
    key_valid = lax.dynamic_slice(
        valid_pad, (first_frame, first_row, zero), (frames_ext, rows_ext, width)
    )
    query_valid = lax.dynamic_slice(
        valid, (first_frame, first_row, zero), (frame_count, row_count, width)
    )
    row_tiles = row_count // TH
    blocks = frame_count * row_tiles
    span_t = 2 * TT + 1
    span_h = 3 * TH
    query_n = TH * width
    key_n = span_t * span_h * width
    block_valid = jnp.stack(
        [
            key_valid[f : f + span_t, TH * rt : TH * rt + span_h].reshape(-1)
            for f in range(frame_count)
            for rt in range(row_tiles)
        ]
    )
    apart_t = jnp.abs(jnp.arange(span_t, dtype=jnp.int32) - TT)
    apart_h = jnp.abs(jnp.arange(span_h, dtype=jnp.int32) // TH - 1)
    near = (apart_t[None, :, None, None] <= window[:, 0, None, None, None]) & (
        apart_h[None, None, :, None] <= window[:, 1, None, None, None]
    )
    near = jnp.broadcast_to(near, (HEADS, span_t, span_h, width)).reshape(HEADS, 1, key_n)
    key_mask = (near & (block_valid[None] > 0)).astype(jnp.float32).reshape(HEADS, blocks, 1, key_n)
    column_tiles = jnp.arange(width, dtype=jnp.int32) // TW
    key_cols = jnp.tile(column_tiles, span_t * span_h).reshape(1, key_n)
    query_cols = jnp.tile(column_tiles, TH)
    query_lo = (query_cols[None, :] - window[:, 2, None]).reshape(HEADS, query_n, 1)
    query_hi = (query_cols[None, :] + window[:, 2, None]).reshape(HEADS, query_n, 1)
    query_ok = query_valid.reshape(blocks, query_n, 1).astype(jnp.float32)
    query_grid = query.reshape(frame_count, row_count, width, inner)
    return tile_attention(query_grid, extended, key_mask, query_lo, query_hi, key_cols, query_ok)


def attention_kernel(q_ref, k_ref, v_ref, km_ref, lo_ref, hi_ref, kc_ref, qv_ref, o_ref):
    block = pl.program_id(1)
    span_t = 2 * TT + 1
    span_h = 3 * TH
    frame = block // ROW_TILES
    row = (block % ROW_TILES) * TH
    width = q_ref.shape[2]
    query = q_ref[0].reshape(TH * width, HDIM)
    key = k_ref[0, pl.ds(frame, span_t), pl.ds(row, span_h)].reshape(-1, HDIM)
    value = v_ref[0, pl.ds(frame, span_t), pl.ds(row, span_h)].reshape(-1, HDIM)
    scores = lax.dot_general(
        query, key, (((1,), (1,)), ((), ())), preferred_element_type=jnp.float32
    ) * (1.0 / float(HDIM) ** 0.5)
    key_cols = kc_ref[...]
    allowed = (key_cols >= lo_ref[0]) & (key_cols <= hi_ref[0]) & (km_ref[0, 0] > 0.0)
    terms = jnp.where(allowed, jnp.exp(scores), jnp.float32(0.0))
    total = jnp.sum(terms, axis=-1, keepdims=True)
    seen = qv_ref[0] > 0.0
    total = jnp.where(seen, total, jnp.float32(1.0))
    weights = (terms / total).astype(jnp.bfloat16)
    result = jnp.dot(weights, value, preferred_element_type=jnp.float32)
    result = jnp.where(seen, result, jnp.float32(0.0)).astype(jnp.bfloat16)
    o_ref[0] = result.reshape(TH, width, HDIM)


ROW_TILES = 2


def tile_attention(query, extended, key_mask, query_lo, query_hi, key_cols, query_ok):
    frames, rows, width, inner = query.shape
    heads = inner // HDIM
    row_tiles = rows // TH
    assert row_tiles == ROW_TILES
    blocks = frames * row_tiles
    _, frames_ext, rows_ext, _, _ = extended.shape
    key_n = key_mask.shape[-1]
    query_n = TH * width
    q_spec = pl.BlockSpec(
        (1, TH, width, HDIM), lambda h, b: (b // row_tiles, b % row_tiles, 0, h)
    )
    return pl.pallas_call(
        attention_kernel,
        grid=(heads, blocks),
        in_specs=[
            q_spec,
            pl.BlockSpec((1, frames_ext, rows_ext, width, HDIM), lambda h, b: (0, 0, 0, 0, h)),
            pl.BlockSpec((1, frames_ext, rows_ext, width, HDIM), lambda h, b: (1, 0, 0, 0, h)),
            pl.BlockSpec((1, 1, 1, key_n), lambda h, b: (h, b, 0, 0)),
            pl.BlockSpec((1, query_n, 1), lambda h, b: (h, 0, 0)),
            pl.BlockSpec((1, query_n, 1), lambda h, b: (h, 0, 0)),
            pl.BlockSpec((1, key_n), lambda h, b: (0, 0)),
            pl.BlockSpec((1, query_n, 1), lambda h, b: (b, 0, 0)),
        ],
        out_specs=q_spec,
        out_shape=jax.ShapeDtypeStruct(query.shape, jnp.bfloat16),
    )(query, extended, extended, key_mask, query_lo, query_hi, key_cols, query_ok)


def solution(mesh):
    in_specs = (
        P("tm", "height", None, None),
        P(),
        P(),
        P(("tm", "height"), None),
        P(),
        P(),
        P(),
        P(),
    )
    out_specs = P("tm", "height", None, None)
    return jax.shard_map(
        per_device, mesh=mesh, in_specs=in_specs, out_specs=out_specs, check_vma=False
    )
```

```python
import functools

import jax
import jax.numpy as jnp
from jax import lax
from jax.sharding import PartitionSpec as P
from jax.experimental import pallas as pl
from jax.experimental.pallas import tpu as pltpu

HDIM = 128
HEADS = 12
TT = 1
TH = 2
TW = 8
GROUPS = 2


EPS = 1e-06


def with_halo(cells, sides, width):
    for axis, dim in sides:
        count = lax.axis_size(axis)
        ends = count - 1
        head = lax.slice_in_dim(cells, 0, width, axis=dim)
        tail = lax.slice_in_dim(cells, cells.shape[dim] - width, cells.shape[dim], axis=dim)
        cells = jnp.concatenate(
            [
                lax.ppermute(tail, axis, [(i, (i + 1) % count) for i in range(ends)]),
                cells,
                lax.ppermute(head, axis, [((i + 1) % count, i) for i in range(ends)]),
            ],
            axis=dim,
        )
    return cells


def modulate(tokens, mod_scale, mod_shift):
    values = tokens.astype(jnp.float32)
    mean = jnp.mean(values, axis=-1, keepdims=True)
    centred = values - mean
    variance = jnp.mean(centred * centred, axis=-1, keepdims=True)
    normed = centred * lax.rsqrt(variance + EPS)
    return (normed * (1.0 + mod_scale) + mod_shift).astype(jnp.bfloat16)


def head_norm(values, gain):
    power = jnp.mean(values * values, axis=-1, keepdims=True)
    return (values * lax.rsqrt(power + EPS) * gain).astype(jnp.bfloat16)


def tile_coords(frames, rows, width):
    shape = (frames.shape[0], rows.shape[0], width)
    columns = jnp.arange(width, dtype=jnp.int32)
    frame_tiles = jnp.broadcast_to((frames // TT)[:, None, None], shape).reshape(-1)
    row_tiles = jnp.broadcast_to((rows // TH)[None, :, None], shape).reshape(-1)
    column_tiles = jnp.broadcast_to((columns // TW)[None, None, :], shape).reshape(-1)
    return (frame_tiles, row_tiles, column_tiles)


def per_device(tokens, mod_scale, mod_shift, w_qkv, q_gain, k_gain, window, valid):
    frame_count, row_count, width, features = tokens.shape
    token_count = frame_count * row_count * width
    modulated = modulate(tokens.reshape(token_count, features), mod_scale, mod_shift)
    band_weight = lax.all_gather(w_qkv, "height", axis=0, tiled=True)
    full_weight = lax.all_gather(band_weight, "tm", axis=0, tiled=True)
    inner = full_weight.shape[1] // 3
    group_cols = inner // GROUPS
    tiled = (frame_count // TT, TT, row_count // TH, TH, width, group_cols)
    groups = []
    for group in range(GROUPS):
        start = group * group_cols
        key = project(modulated, full_weight, inner + start, group_cols, k_gain)
        value = project(modulated, full_weight, 2 * inner + start, group_cols, None)
        stacked = jnp.stack([key.reshape(tiled), value.reshape(tiled)])
        groups.append(with_halo(stacked, (("tm", 1), ("height", 3)), 1))
    query = project(modulated, full_weight, 0, inner, q_gain)
    frames_ext = frame_count + 2 * TT
    rows_ext = row_count + 2 * TH
    groups = [g.reshape(2, frames_ext, rows_ext, width, group_cols) for g in groups]
    frame_block = lax.axis_index("tm")
    row_block = lax.axis_index("height")
    first_frame = frame_block * frame_count
    first_row = row_block * row_count
    zero = jnp.int32(0)
    valid_pad = jnp.pad(valid, ((TT, TT), (TH, TH), (0, 0)))
    key_valid = lax.dynamic_slice(
        valid_pad, (first_frame, first_row, zero), (frames_ext, rows_ext, width)
    )
    query_valid = lax.dynamic_slice(
        valid, (first_frame, first_row, zero), (frame_count, row_count, width)
    )
    row_tiles = row_count // TH
    blocks = frame_count * row_tiles
    span_t = 2 * TT + 1
    span_h = 3 * TH
    query_n = TH * width
    key_n = span_t * span_h * width
    block_valid = jnp.stack(
        [
            key_valid[f : f + span_t, TH * rt : TH * rt + span_h].reshape(-1)
            for f in range(frame_count)
            for rt in range(row_tiles)
        ]
    )
    apart_t = jnp.abs(jnp.arange(span_t, dtype=jnp.int32) - TT)
    apart_h = jnp.abs(jnp.arange(span_h, dtype=jnp.int32) // TH - 1)
    near = (apart_t[None, :, None, None] <= window[:, 0, None, None, None]) & (
        apart_h[None, None, :, None] <= window[:, 1, None, None, None]
    )
    near = jnp.broadcast_to(near, (HEADS, span_t, span_h, width)).reshape(HEADS, 1, key_n)
    key_mask = (near & (block_valid[None] > 0)).astype(jnp.float32).reshape(HEADS, blocks, 1, key_n)
    column_tiles = jnp.arange(width, dtype=jnp.int32) // TW
    key_cols = jnp.tile(column_tiles, span_t * span_h).reshape(1, key_n)
    query_cols = jnp.tile(column_tiles, TH)
    query_lo = (query_cols[None, :] - window[:, 2, None]).reshape(HEADS, query_n, 1)
    query_hi = (query_cols[None, :] + window[:, 2, None]).reshape(HEADS, query_n, 1)
    query_ok = query_valid.reshape(blocks, query_n, 1).astype(jnp.float32)
    query_grid = query.reshape(frame_count, row_count, width, inner)
    out = None
    for group, extended in enumerate(groups):
        out = tile_attention(
            query_grid, extended, key_mask, query_lo, query_hi, key_cols, query_ok, group, out
        )
    return out


def attention_kernel(q_ref, k_ref, v_ref, km_ref, lo_ref, hi_ref, kc_ref, qv_ref, o_ref):
    block = pl.program_id(1)
    span_t = 2 * TT + 1
    span_h = 3 * TH
    frame = block // ROW_TILES
    row = (block % ROW_TILES) * TH
    width = q_ref.shape[2]
    query = q_ref[0].reshape(TH * width, HDIM)
    key = k_ref[0, pl.ds(frame, span_t), pl.ds(row, span_h)].reshape(-1, HDIM)
    value = v_ref[0, pl.ds(frame, span_t), pl.ds(row, span_h)].reshape(-1, HDIM)
    scores = lax.dot_general(
        query, key, (((1,), (1,)), ((), ())), preferred_element_type=jnp.float32
    ) * (1.0 / float(HDIM) ** 0.5)
    key_cols = kc_ref[...]
    allowed = (key_cols >= lo_ref[0]) & (key_cols <= hi_ref[0]) & (km_ref[0, 0] > 0.0)
    terms = jnp.where(allowed, jnp.exp(scores), jnp.float32(0.0))
    total = jnp.sum(terms, axis=-1, keepdims=True)
    seen = qv_ref[0] > 0.0
    total = jnp.where(seen, total, jnp.float32(1.0))
    weights = (terms / total).astype(jnp.bfloat16)
    result = jnp.dot(weights, value, preferred_element_type=jnp.float32)
    result = jnp.where(seen, result, jnp.float32(0.0)).astype(jnp.bfloat16)
    o_ref[0] = result.reshape(TH, width, HDIM)


ROW_TILES = 2


def tile_attention(query, extended, key_mask, query_lo, query_hi, key_cols, query_ok, group, out):
    frames, rows, width, inner = query.shape
    heads = extended.shape[-1] // HDIM
    first = group * heads
    row_tiles = rows // TH
    assert row_tiles == ROW_TILES
    blocks = frames * row_tiles
    _, frames_ext, rows_ext, _, _ = extended.shape
    key_n = key_mask.shape[-1]
    query_n = TH * width
    q_spec = pl.BlockSpec(
        (1, TH, width, HDIM), lambda h, b: (b // row_tiles, b % row_tiles, 0, first + h)
    )
    in_specs = [
        q_spec,
        pl.BlockSpec((1, frames_ext, rows_ext, width, HDIM), lambda h, b: (0, 0, 0, 0, h)),
        pl.BlockSpec((1, frames_ext, rows_ext, width, HDIM), lambda h, b: (1, 0, 0, 0, h)),
        pl.BlockSpec((1, 1, 1, key_n), lambda h, b: (first + h, b, 0, 0)),
        pl.BlockSpec((1, query_n, 1), lambda h, b: (first + h, 0, 0)),
        pl.BlockSpec((1, query_n, 1), lambda h, b: (first + h, 0, 0)),
        pl.BlockSpec((1, key_n), lambda h, b: (0, 0)),
        pl.BlockSpec((1, query_n, 1), lambda h, b: (b, 0, 0)),
    ]
    operands = [query, extended, extended, key_mask, query_lo, query_hi, key_cols, query_ok]
    aliases = {}
    kernel = attention_kernel
    if out is not None:
        in_specs.append(pl.BlockSpec(memory_space=pl.ANY))
        operands.append(out)
        aliases = {len(operands) - 1: 0}
        kernel = lambda *refs: attention_kernel(*refs[:8], refs[9])
    return pl.pallas_call(
        kernel,
        grid=(heads, blocks),
        in_specs=in_specs,
        out_specs=q_spec,
        out_shape=jax.ShapeDtypeStruct(query.shape, jnp.bfloat16),
        input_output_aliases=aliases,
    )(*operands)


PROJECT_COLS = 256


def projection_kernel(x_ref, w_ref, g_ref, o_ref, *, normalize):
    acc = jnp.dot(x_ref[...], w_ref[...], preferred_element_type=jnp.float32)
    for part in range(acc.shape[1] // HDIM):
        piece = acc[:, part * HDIM : (part + 1) * HDIM]
        if normalize:
            power = jnp.mean(piece * piece, axis=-1, keepdims=True)
            piece = piece * lax.rsqrt(power + EPS) * g_ref[...]
        o_ref[:, part * HDIM : (part + 1) * HDIM] = piece.astype(o_ref.dtype)


def project(x, w, start, count, gain):
    tokens, features = x.shape
    cols = PROJECT_COLS
    normalize = gain is not None
    gain = gain.reshape(1, HDIM) if normalize else jnp.ones((1, HDIM), jnp.float32)
    first = start // cols
    return pl.pallas_call(
        functools.partial(projection_kernel, normalize=normalize),
        grid=(count // cols,),
        in_specs=[
            pl.BlockSpec((tokens, features), lambda j: (0, 0)),
            pl.BlockSpec((features, cols), lambda j: (0, first + j)),
            pl.BlockSpec((1, HDIM), lambda j: (0, 0)),
        ],
        out_specs=pl.BlockSpec((tokens, cols), lambda j: (0, j)),
        out_shape=jax.ShapeDtypeStruct((tokens, count), jnp.bfloat16),
    )(x, w, gain)


def solution(mesh):
    in_specs = (
        P("tm", "height", None, None),
        P(),
        P(),
        P(("tm", "height"), None),
        P(),
        P(),
        P(),
        P(),
    )
    out_specs = P("tm", "height", None, None)
    return jax.shard_map(
        per_device, mesh=mesh, in_specs=in_specs, out_specs=out_specs, check_vma=False
    )
```

```python
import functools

import jax
import jax.numpy as jnp
from jax import lax
from jax.sharding import PartitionSpec as P
from jax.experimental import pallas as pl
from jax.experimental.pallas import tpu as pltpu

HDIM = 128
HEADS = 12
TT = 1
TH = 2
TW = 8
GROUPS = 2


EPS = 1e-06


def with_halo(cells, sides, width):
    for axis, dim in sides:
        count = lax.axis_size(axis)
        ends = count - 1
        head = lax.slice_in_dim(cells, 0, width, axis=dim)
        tail = lax.slice_in_dim(cells, cells.shape[dim] - width, cells.shape[dim], axis=dim)
        cells = jnp.concatenate(
            [
                lax.ppermute(tail, axis, [(i, (i + 1) % count) for i in range(ends)]),
                cells,
                lax.ppermute(head, axis, [((i + 1) % count, i) for i in range(ends)]),
            ],
            axis=dim,
        )
    return cells


def modulate(tokens, mod_scale, mod_shift):
    values = tokens.astype(jnp.float32)
    mean = jnp.mean(values, axis=-1, keepdims=True)
    centred = values - mean
    variance = jnp.mean(centred * centred, axis=-1, keepdims=True)
    normed = centred * lax.rsqrt(variance + EPS)
    return (normed * (1.0 + mod_scale) + mod_shift).astype(jnp.bfloat16)


def head_norm(values, gain):
    power = jnp.mean(values * values, axis=-1, keepdims=True)
    return (values * lax.rsqrt(power + EPS) * gain).astype(jnp.bfloat16)


def tile_coords(frames, rows, width):
    shape = (frames.shape[0], rows.shape[0], width)
    columns = jnp.arange(width, dtype=jnp.int32)
    frame_tiles = jnp.broadcast_to((frames // TT)[:, None, None], shape).reshape(-1)
    row_tiles = jnp.broadcast_to((rows // TH)[None, :, None], shape).reshape(-1)
    column_tiles = jnp.broadcast_to((columns // TW)[None, None, :], shape).reshape(-1)
    return (frame_tiles, row_tiles, column_tiles)


def per_device(tokens, mod_scale, mod_shift, w_qkv, q_gain, k_gain, window, valid):
    frame_count, row_count, width, features = tokens.shape
    token_count = frame_count * row_count * width
    modulated = modulate(tokens.reshape(token_count, features), mod_scale, mod_shift)
    band_weight = lax.all_gather(w_qkv, "height", axis=0, tiled=True)
    band_rows = band_weight.shape[0]
    inner = band_weight.shape[1] // 3
    group_cols = inner // GROUPS
    band_parts = (
        band_weight.reshape(band_rows, 3, GROUPS, group_cols)
        .transpose(2, 0, 1, 3)
        .reshape(GROUPS, band_rows, 3 * group_cols)
    )
    frames_ext = frame_count + 2 * TT
    rows_ext = row_count + 2 * TH
    frame_block = lax.axis_index("tm")
    row_block = lax.axis_index("height")
    first_frame = frame_block * frame_count
    first_row = row_block * row_count
    zero = jnp.int32(0)
    valid_pad = jnp.pad(valid, ((TT, TT), (TH, TH), (0, 0)))
    key_valid = lax.dynamic_slice(
        valid_pad, (first_frame, first_row, zero), (frames_ext, rows_ext, width)
    )
    query_valid = lax.dynamic_slice(
        valid, (first_frame, first_row, zero), (frame_count, row_count, width)
    )
    row_tiles = row_count // TH
    blocks = frame_count * row_tiles
    span_t = 2 * TT + 1
    span_h = 3 * TH
    query_n = TH * width
    key_n = span_t * span_h * width
    block_valid = jnp.stack(
        [
            key_valid[f : f + span_t, TH * rt : TH * rt + span_h].reshape(-1)
            for f in range(frame_count)
            for rt in range(row_tiles)
        ]
    )
    apart_t = jnp.abs(jnp.arange(span_t, dtype=jnp.int32) - TT)
    apart_h = jnp.abs(jnp.arange(span_h, dtype=jnp.int32) // TH - 1)
    near = (apart_t[None, :, None, None] <= window[:, 0, None, None, None]) & (
        apart_h[None, None, :, None] <= window[:, 1, None, None, None]
    )
    near = jnp.broadcast_to(near, (HEADS, span_t, span_h, width)).reshape(HEADS, 1, key_n)
    key_mask = (near & (block_valid[None] > 0)).astype(jnp.float32).reshape(HEADS, blocks, 1, key_n)
    column_tiles = jnp.arange(width, dtype=jnp.int32) // TW
    key_cols = jnp.tile(column_tiles, span_t * span_h).reshape(1, key_n)
    query_cols = jnp.tile(column_tiles, TH)
    query_lo = (query_cols[None, :] - window[:, 2, None]).reshape(HEADS, query_n, 1)
    query_hi = (query_cols[None, :] + window[:, 2, None]).reshape(HEADS, query_n, 1)
    query_ok = query_valid.reshape(blocks, query_n, 1).astype(jnp.float32)
    tiled = (frame_count // TT, TT, row_count // TH, TH, width, group_cols)
    out = None
    for group in range(GROUPS):
        group_weight = lax.all_gather(band_parts[group], "tm", axis=0, tiled=True)
        if out is not None:
            group_weight, out = lax.optimization_barrier((group_weight, out))
        key = project(modulated, group_weight, group_cols, group_cols, k_gain)
        value = project(modulated, group_weight, 2 * group_cols, group_cols, None)
        stacked = jnp.stack([key.reshape(tiled), value.reshape(tiled)])
        extended = with_halo(stacked, (("tm", 1), ("height", 3)), 1)
        extended = extended.reshape(2, frames_ext, rows_ext, width, group_cols)
        query = project(modulated, group_weight, 0, group_cols, q_gain)
        query = query.reshape(frame_count, row_count, width, group_cols)
        out = tile_attention(
            query, extended, key_mask, query_lo, query_hi, key_cols, query_ok, group, out
        )
    return out


def attention_kernel(q_ref, k_ref, v_ref, km_ref, lo_ref, hi_ref, kc_ref, qv_ref, o_ref):
    block = pl.program_id(1)
    span_t = 2 * TT + 1
    span_h = 3 * TH
    frame = block // ROW_TILES
    row = (block % ROW_TILES) * TH
    width = q_ref.shape[2]
    query = q_ref[0].reshape(TH * width, HDIM)
    key = k_ref[0, pl.ds(frame, span_t), pl.ds(row, span_h)].reshape(-1, HDIM)
    value = v_ref[0, pl.ds(frame, span_t), pl.ds(row, span_h)].reshape(-1, HDIM)
    scores = lax.dot_general(
        query, key, (((1,), (1,)), ((), ())), preferred_element_type=jnp.float32
    ) * (1.0 / float(HDIM) ** 0.5)
    key_cols = kc_ref[...]
    allowed = (key_cols >= lo_ref[0]) & (key_cols <= hi_ref[0]) & (km_ref[0, 0] > 0.0)
    terms = jnp.where(allowed, jnp.exp(scores), jnp.float32(0.0))
    total = jnp.sum(terms, axis=-1, keepdims=True)
    seen = qv_ref[0] > 0.0
    total = jnp.where(seen, total, jnp.float32(1.0))
    weights = (terms / total).astype(jnp.bfloat16)
    result = jnp.dot(weights, value, preferred_element_type=jnp.float32)
    result = jnp.where(seen, result, jnp.float32(0.0)).astype(jnp.bfloat16)
    o_ref[0] = result.reshape(TH, width, HDIM)


ROW_TILES = 2


def tile_attention(query, extended, key_mask, query_lo, query_hi, key_cols, query_ok, group, out):
    frames, rows, width, group_cols = query.shape
    heads = group_cols // HDIM
    out_shape = (frames, rows, width, key_mask.shape[0] * HDIM)
    first = group * heads
    row_tiles = rows // TH
    assert row_tiles == ROW_TILES
    blocks = frames * row_tiles
    _, frames_ext, rows_ext, _, _ = extended.shape
    key_n = key_mask.shape[-1]
    query_n = TH * width
    q_spec = pl.BlockSpec(
        (1, TH, width, HDIM), lambda h, b: (b // row_tiles, b % row_tiles, 0, h)
    )
    o_spec = pl.BlockSpec(
        (1, TH, width, HDIM), lambda h, b: (b // row_tiles, b % row_tiles, 0, first + h)
    )
    in_specs = [
        q_spec,
        pl.BlockSpec((1, frames_ext, rows_ext, width, HDIM), lambda h, b: (0, 0, 0, 0, h)),
        pl.BlockSpec((1, frames_ext, rows_ext, width, HDIM), lambda h, b: (1, 0, 0, 0, h)),
        pl.BlockSpec((1, 1, 1, key_n), lambda h, b: (first + h, b, 0, 0)),
        pl.BlockSpec((1, query_n, 1), lambda h, b: (first + h, 0, 0)),
        pl.BlockSpec((1, query_n, 1), lambda h, b: (first + h, 0, 0)),
        pl.BlockSpec((1, key_n), lambda h, b: (0, 0)),
        pl.BlockSpec((1, query_n, 1), lambda h, b: (b, 0, 0)),
    ]
    operands = [query, extended, extended, key_mask, query_lo, query_hi, key_cols, query_ok]
    aliases = {}
    kernel = attention_kernel
    if out is not None:
        in_specs.append(pl.BlockSpec(memory_space=pl.ANY))
        operands.append(out)
        aliases = {len(operands) - 1: 0}
        kernel = lambda *refs: attention_kernel(*refs[:8], refs[9])
    return pl.pallas_call(
        kernel,
        grid=(heads, blocks),
        in_specs=in_specs,
        out_specs=o_spec,
        out_shape=jax.ShapeDtypeStruct(out_shape, jnp.bfloat16),
        input_output_aliases=aliases,
    )(*operands)


PROJECT_COLS = 256


def projection_kernel(x_ref, w_ref, g_ref, o_ref, *, normalize):
    acc = jnp.dot(x_ref[...], w_ref[...], preferred_element_type=jnp.float32)
    for part in range(acc.shape[1] // HDIM):
        piece = acc[:, part * HDIM : (part + 1) * HDIM]
        if normalize:
            power = jnp.mean(piece * piece, axis=-1, keepdims=True)
            piece = piece * lax.rsqrt(power + EPS) * g_ref[...]
        o_ref[:, part * HDIM : (part + 1) * HDIM] = piece.astype(o_ref.dtype)


def project(x, w, start, count, gain):
    tokens, features = x.shape
    cols = PROJECT_COLS
    normalize = gain is not None
    gain = gain.reshape(1, HDIM) if normalize else jnp.ones((1, HDIM), jnp.float32)
    first = start // cols
    return pl.pallas_call(
        functools.partial(projection_kernel, normalize=normalize),
        grid=(count // cols,),
        in_specs=[
            pl.BlockSpec((tokens, features), lambda j: (0, 0)),
            pl.BlockSpec((features, cols), lambda j: (0, first + j)),
            pl.BlockSpec((1, HDIM), lambda j: (0, 0)),
        ],
        out_specs=pl.BlockSpec((tokens, cols), lambda j: (0, j)),
        out_shape=jax.ShapeDtypeStruct((tokens, count), jnp.bfloat16),
    )(x, w, gain)


def solution(mesh):
    in_specs = (
        P("tm", "height", None, None),
        P(),
        P(),
        P(("tm", "height"), None),
        P(),
        P(),
        P(),
        P(),
    )
    out_specs = P("tm", "height", None, None)
    return jax.shard_map(
        per_device, mesh=mesh, in_specs=in_specs, out_specs=out_specs, check_vma=False
    )
```

```python
import functools

import jax
import jax.numpy as jnp
from jax import lax
from jax.sharding import PartitionSpec as P
from jax.experimental import pallas as pl
from jax.experimental.pallas import tpu as pltpu

HDIM = 128
HEADS = 12
TT = 1
TH = 2
TW = 8
GROUPS = 2


EPS = 1e-06


def with_halo(cells, sides, width):
    for axis, dim in sides:
        count = lax.axis_size(axis)
        ends = count - 1
        head = lax.slice_in_dim(cells, 0, width, axis=dim)
        tail = lax.slice_in_dim(cells, cells.shape[dim] - width, cells.shape[dim], axis=dim)
        cells = jnp.concatenate(
            [
                lax.ppermute(tail, axis, [(i, (i + 1) % count) for i in range(ends)]),
                cells,
                lax.ppermute(head, axis, [((i + 1) % count, i) for i in range(ends)]),
            ],
            axis=dim,
        )
    return cells


def modulate(tokens, mod_scale, mod_shift):
    values = tokens.astype(jnp.float32)
    mean = jnp.mean(values, axis=-1, keepdims=True)
    centred = values - mean
    variance = jnp.mean(centred * centred, axis=-1, keepdims=True)
    normed = centred * lax.rsqrt(variance + EPS)
    return (normed * (1.0 + mod_scale) + mod_shift).astype(jnp.bfloat16)


def head_norm(values, gain):
    power = jnp.mean(values * values, axis=-1, keepdims=True)
    return (values * lax.rsqrt(power + EPS) * gain).astype(jnp.bfloat16)


def tile_coords(frames, rows, width):
    shape = (frames.shape[0], rows.shape[0], width)
    columns = jnp.arange(width, dtype=jnp.int32)
    frame_tiles = jnp.broadcast_to((frames // TT)[:, None, None], shape).reshape(-1)
    row_tiles = jnp.broadcast_to((rows // TH)[None, :, None], shape).reshape(-1)
    column_tiles = jnp.broadcast_to((columns // TW)[None, None, :], shape).reshape(-1)
    return (frame_tiles, row_tiles, column_tiles)


def per_device(tokens, mod_scale, mod_shift, w_qkv, q_gain, k_gain, window, valid):
    frame_count, row_count, width, features = tokens.shape
    token_count = frame_count * row_count * width
    modulated = modulate(tokens.reshape(token_count, features), mod_scale, mod_shift)
    band_weight = band_gather(w_qkv)
    full_weight = lax.all_gather(band_weight, "tm", axis=0, tiled=True)
    inner = full_weight.shape[1] // 3
    group_cols = inner // GROUPS
    tiled = (frame_count // TT, TT, row_count // TH, TH, width, group_cols)
    groups = []
    for group in range(GROUPS):
        start = group * group_cols
        key = project(modulated, full_weight, inner + start, group_cols, k_gain)
        value = project(modulated, full_weight, 2 * inner + start, group_cols, None)
        stacked = jnp.stack([key.reshape(tiled), value.reshape(tiled)])
        groups.append(with_halo(stacked, (("tm", 1), ("height", 3)), 1))
    query = project(modulated, full_weight, 0, inner, q_gain)
    frames_ext = frame_count + 2 * TT
    rows_ext = row_count + 2 * TH
    groups = [g.reshape(2, frames_ext, rows_ext, width, group_cols) for g in groups]
    frame_block = lax.axis_index("tm")
    row_block = lax.axis_index("height")
    first_frame = frame_block * frame_count
    first_row = row_block * row_count
    zero = jnp.int32(0)
    valid_pad = jnp.pad(valid, ((TT, TT), (TH, TH), (0, 0)))
    key_valid = lax.dynamic_slice(
        valid_pad, (first_frame, first_row, zero), (frames_ext, rows_ext, width)
    )
    query_valid = lax.dynamic_slice(
        valid, (first_frame, first_row, zero), (frame_count, row_count, width)
    )
    row_tiles = row_count // TH
    blocks = frame_count * row_tiles
    span_t = 2 * TT + 1
    span_h = 3 * TH
    query_n = TH * width
    key_n = span_t * span_h * width
    block_valid = jnp.stack(
        [
            key_valid[f : f + span_t, TH * rt : TH * rt + span_h].reshape(-1)
            for f in range(frame_count)
            for rt in range(row_tiles)
        ]
    )
    apart_t = jnp.abs(jnp.arange(span_t, dtype=jnp.int32) - TT)
    apart_h = jnp.abs(jnp.arange(span_h, dtype=jnp.int32) // TH - 1)
    near = (apart_t[None, :, None, None] <= window[:, 0, None, None, None]) & (
        apart_h[None, None, :, None] <= window[:, 1, None, None, None]
    )
    near = jnp.broadcast_to(near, (HEADS, span_t, span_h, width)).reshape(HEADS, 1, key_n)
    key_mask = (near & (block_valid[None] > 0)).astype(jnp.float32).reshape(HEADS, blocks, 1, key_n)
    column_tiles = jnp.arange(width, dtype=jnp.int32) // TW
    key_cols = jnp.tile(column_tiles, span_t * span_h).reshape(1, key_n)
    query_cols = jnp.tile(column_tiles, TH)
    query_lo = (query_cols[None, :] - window[:, 2, None]).reshape(HEADS, query_n, 1)
    query_hi = (query_cols[None, :] + window[:, 2, None]).reshape(HEADS, query_n, 1)
    query_ok = query_valid.reshape(blocks, query_n, 1).astype(jnp.float32)
    query_grid = query.reshape(frame_count, row_count, width, inner)
    out = None
    for group, extended in enumerate(groups):
        out = tile_attention(
            query_grid, extended, key_mask, query_lo, query_hi, key_cols, query_ok, group, out
        )
    return out


def attention_kernel(q_ref, k_ref, v_ref, km_ref, lo_ref, hi_ref, kc_ref, qv_ref, o_ref):
    block = pl.program_id(1)
    span_t = 2 * TT + 1
    span_h = 3 * TH
    frame = block // ROW_TILES
    row = (block % ROW_TILES) * TH
    width = q_ref.shape[2]
    query = q_ref[0].reshape(TH * width, HDIM)
    key = k_ref[0, pl.ds(frame, span_t), pl.ds(row, span_h)].reshape(-1, HDIM)
    value = v_ref[0, pl.ds(frame, span_t), pl.ds(row, span_h)].reshape(-1, HDIM)
    scores = lax.dot_general(
        query, key, (((1,), (1,)), ((), ())), preferred_element_type=jnp.float32
    ) * (1.0 / float(HDIM) ** 0.5)
    key_cols = kc_ref[...]
    allowed = (key_cols >= lo_ref[0]) & (key_cols <= hi_ref[0]) & (km_ref[0, 0] > 0.0)
    terms = jnp.where(allowed, jnp.exp(scores), jnp.float32(0.0))
    total = jnp.sum(terms, axis=-1, keepdims=True)
    seen = qv_ref[0] > 0.0
    total = jnp.where(seen, total, jnp.float32(1.0))
    weights = (terms / total).astype(jnp.bfloat16)
    result = jnp.dot(weights, value, preferred_element_type=jnp.float32)
    result = jnp.where(seen, result, jnp.float32(0.0)).astype(jnp.bfloat16)
    o_ref[0] = result.reshape(TH, width, HDIM)


ROW_TILES = 2


def tile_attention(query, extended, key_mask, query_lo, query_hi, key_cols, query_ok, group, out):
    frames, rows, width, inner = query.shape
    heads = extended.shape[-1] // HDIM
    first = group * heads
    row_tiles = rows // TH
    assert row_tiles == ROW_TILES
    blocks = frames * row_tiles
    _, frames_ext, rows_ext, _, _ = extended.shape
    key_n = key_mask.shape[-1]
    query_n = TH * width
    q_spec = pl.BlockSpec(
        (1, TH, width, HDIM), lambda h, b: (b // row_tiles, b % row_tiles, 0, first + h)
    )
    in_specs = [
        q_spec,
        pl.BlockSpec((1, frames_ext, rows_ext, width, HDIM), lambda h, b: (0, 0, 0, 0, h)),
        pl.BlockSpec((1, frames_ext, rows_ext, width, HDIM), lambda h, b: (1, 0, 0, 0, h)),
        pl.BlockSpec((1, 1, 1, key_n), lambda h, b: (first + h, b, 0, 0)),
        pl.BlockSpec((1, query_n, 1), lambda h, b: (first + h, 0, 0)),
        pl.BlockSpec((1, query_n, 1), lambda h, b: (first + h, 0, 0)),
        pl.BlockSpec((1, key_n), lambda h, b: (0, 0)),
        pl.BlockSpec((1, query_n, 1), lambda h, b: (b, 0, 0)),
    ]
    operands = [query, extended, extended, key_mask, query_lo, query_hi, key_cols, query_ok]
    aliases = {}
    kernel = attention_kernel
    if out is not None:
        in_specs.append(pl.BlockSpec(memory_space=pl.ANY))
        operands.append(out)
        aliases = {len(operands) - 1: 0}
        kernel = lambda *refs: attention_kernel(*refs[:8], refs[9])
    return pl.pallas_call(
        kernel,
        grid=(heads, blocks),
        in_specs=in_specs,
        out_specs=q_spec,
        out_shape=jax.ShapeDtypeStruct(query.shape, jnp.bfloat16),
        input_output_aliases=aliases,
    )(*operands)


PROJECT_COLS = 256


def projection_kernel(x_ref, w_ref, g_ref, o_ref, *, normalize):
    acc = jnp.dot(x_ref[...], w_ref[...], preferred_element_type=jnp.float32)
    for part in range(acc.shape[1] // HDIM):
        piece = acc[:, part * HDIM : (part + 1) * HDIM]
        if normalize:
            power = jnp.mean(piece * piece, axis=-1, keepdims=True)
            piece = piece * lax.rsqrt(power + EPS) * g_ref[...]
        o_ref[:, part * HDIM : (part + 1) * HDIM] = piece.astype(o_ref.dtype)


def project(x, w, start, count, gain):
    tokens, features = x.shape
    cols = PROJECT_COLS
    normalize = gain is not None
    gain = gain.reshape(1, HDIM) if normalize else jnp.ones((1, HDIM), jnp.float32)
    first = start // cols
    return pl.pallas_call(
        functools.partial(projection_kernel, normalize=normalize),
        grid=(count // cols,),
        in_specs=[
            pl.BlockSpec((tokens, features), lambda j: (0, 0)),
            pl.BlockSpec((features, cols), lambda j: (0, first + j)),
            pl.BlockSpec((1, HDIM), lambda j: (0, 0)),
        ],
        out_specs=pl.BlockSpec((tokens, cols), lambda j: (0, j)),
        out_shape=jax.ShapeDtypeStruct((tokens, count), jnp.bfloat16),
    )(x, w, gain)


MESH = pl.DeviceIdType.MESH


def band_gather_kernel(w_ref, out_ref, local_sem, send_sem, recv_sem):
    count = lax.axis_size("height")
    me = lax.axis_index("height")
    frame_block = lax.axis_index("tm")
    barrier = pltpu.get_barrier_semaphore()
    for step in range(1, count):
        peer = lax.rem(me + step, count)
        pl.semaphore_signal(barrier, inc=1, device_id=(frame_block, peer), device_id_type=MESH)
    pl.semaphore_wait(barrier, count - 1)
    own = pltpu.make_async_copy(w_ref, out_ref.at[me], local_sem)
    own.start()
    copies = []
    for step in range(1, count):
        peer = lax.rem(me + step, count)
        copy = pltpu.make_async_remote_copy(
            src_ref=w_ref,
            dst_ref=out_ref.at[me],
            send_sem=send_sem.at[step],
            recv_sem=recv_sem.at[me],
            device_id=(frame_block, peer),
            device_id_type=MESH,
        )
        copy.start()
        copies.append(copy)
    for copy in copies:
        copy.wait_send()
    for step in range(1, count):
        source = lax.rem(me + count - step, count)
        incoming = pltpu.make_async_remote_copy(
            src_ref=w_ref,
            dst_ref=out_ref.at[source],
            send_sem=send_sem.at[step],
            recv_sem=recv_sem.at[source],
            device_id=(frame_block, source),
            device_id_type=MESH,
        )
        incoming.wait_recv()
    own.wait()


def band_gather(w):
    rows, cols = w.shape
    count = lax.axis_size("height")
    gathered = pl.pallas_call(
        band_gather_kernel,
        in_specs=[pl.BlockSpec(memory_space=pl.ANY)],
        out_specs=pl.BlockSpec(memory_space=pl.ANY),
        out_shape=jax.ShapeDtypeStruct((count, rows, cols), w.dtype),
        scratch_shapes=[
            pltpu.SemaphoreType.DMA(()),
            pltpu.SemaphoreType.DMA((count,)),
            pltpu.SemaphoreType.DMA((count,)),
        ],
        compiler_params=pltpu.CompilerParams(collective_id=0, has_side_effects=True),
    )(w)
    return gathered.reshape(count * rows, cols)


def solution(mesh):
    in_specs = (
        P("tm", "height", None, None),
        P(),
        P(),
        P(("tm", "height"), None),
        P(),
        P(),
        P(),
        P(),
    )
    out_specs = P("tm", "height", None, None)
    return jax.shard_map(
        per_device, mesh=mesh, in_specs=in_specs, out_specs=out_specs, check_vma=False
    )
```

```python
import functools

import jax
import jax.numpy as jnp
from jax import lax
from jax.sharding import PartitionSpec as P
from jax.experimental import pallas as pl
from jax.experimental.pallas import tpu as pltpu

HDIM = 128
HEADS = 12
TT = 1
TH = 2
TW = 8
GROUPS = 2


EPS = 1e-06


def with_halo(cells, sides, width):
    for axis, dim in sides:
        count = lax.axis_size(axis)
        ends = count - 1
        head = lax.slice_in_dim(cells, 0, width, axis=dim)
        tail = lax.slice_in_dim(cells, cells.shape[dim] - width, cells.shape[dim], axis=dim)
        cells = jnp.concatenate(
            [
                lax.ppermute(tail, axis, [(i, (i + 1) % count) for i in range(ends)]),
                cells,
                lax.ppermute(head, axis, [((i + 1) % count, i) for i in range(ends)]),
            ],
            axis=dim,
        )
    return cells


def modulate(tokens, mod_scale, mod_shift):
    values = tokens.astype(jnp.float32)
    mean = jnp.mean(values, axis=-1, keepdims=True)
    centred = values - mean
    variance = jnp.mean(centred * centred, axis=-1, keepdims=True)
    normed = centred * lax.rsqrt(variance + EPS)
    return (normed * (1.0 + mod_scale) + mod_shift).astype(jnp.bfloat16)


def head_norm(values, gain):
    power = jnp.mean(values * values, axis=-1, keepdims=True)
    return (values * lax.rsqrt(power + EPS) * gain).astype(jnp.bfloat16)


def tile_coords(frames, rows, width):
    shape = (frames.shape[0], rows.shape[0], width)
    columns = jnp.arange(width, dtype=jnp.int32)
    frame_tiles = jnp.broadcast_to((frames // TT)[:, None, None], shape).reshape(-1)
    row_tiles = jnp.broadcast_to((rows // TH)[None, :, None], shape).reshape(-1)
    column_tiles = jnp.broadcast_to((columns // TW)[None, None, :], shape).reshape(-1)
    return (frame_tiles, row_tiles, column_tiles)


def per_device(tokens, mod_scale, mod_shift, w_qkv, q_gain, k_gain, window, valid):
    frame_count, row_count, width, features = tokens.shape
    token_count = frame_count * row_count * width
    modulated = modulate(tokens.reshape(token_count, features), mod_scale, mod_shift)
    band_weight = band_gather(w_qkv)
    full_weight = lax.all_gather(band_weight, "tm", axis=0, tiled=True)
    inner = full_weight.shape[1] // 3
    group_cols = inner // GROUPS
    tiled = (frame_count // TT, TT, row_count // TH, TH, width, group_cols)
    groups = []
    for group in range(GROUPS):
        start = group * group_cols
        key = project(modulated, full_weight, inner + start, group_cols, k_gain)
        value = project(modulated, full_weight, 2 * inner + start, group_cols, None)
        stacked = jnp.stack([key.reshape(tiled), value.reshape(tiled)])
        groups.append(with_halo(stacked, (("tm", 1), ("height", 3)), 1))
    query = project(modulated, full_weight, 0, inner, q_gain)
    frames_ext = frame_count + 2 * TT
    rows_ext = row_count + 2 * TH
    groups = [g.reshape(2, frames_ext, rows_ext, width, group_cols) for g in groups]
    frame_block = lax.axis_index("tm")
    row_block = lax.axis_index("height")
    first_frame = frame_block * frame_count
    first_row = row_block * row_count
    zero = jnp.int32(0)
    valid_pad = jnp.pad(valid, ((TT, TT), (TH, TH), (0, 0)))
    key_valid = lax.dynamic_slice(
        valid_pad, (first_frame, first_row, zero), (frames_ext, rows_ext, width)
    )
    query_valid = lax.dynamic_slice(
        valid, (first_frame, first_row, zero), (frame_count, row_count, width)
    )
    row_tiles = row_count // TH
    blocks = frame_count * row_tiles
    span_t = 2 * TT + 1
    span_h = 3 * TH
    apart_t = jnp.abs(jnp.arange(span_t, dtype=jnp.int32) - TT)
    apart_h = jnp.abs(jnp.arange(span_h, dtype=jnp.int32) // TH - 1)
    near = (apart_t[None, :, None, None] <= window[:, 0, None, None, None]) & (
        apart_h[None, None, :, None] <= window[:, 1, None, None, None]
    )
    column_tiles = jnp.arange(width, dtype=jnp.int32) // TW
    masks = []
    for q0, q1, k0, k1 in COLUMN_PARTS:
        key_n = span_t * span_h * (k1 - k0)
        query_n = TH * (q1 - q0)
        block_valid = jnp.stack(
            [
                key_valid[f : f + span_t, TH * rt : TH * rt + span_h, k0:k1].reshape(-1)
                for f in range(frame_count)
                for rt in range(row_tiles)
            ]
        )
        part_near = jnp.broadcast_to(near, (HEADS, span_t, span_h, k1 - k0)).reshape(HEADS, 1, key_n)
        key_mask = (part_near & (block_valid[None] > 0)).astype(jnp.float32)
        key_mask = key_mask.reshape(HEADS, blocks, 1, key_n)
        key_cols = jnp.tile(column_tiles[k0:k1], span_t * span_h).reshape(1, key_n)
        query_cols = jnp.tile(column_tiles[q0:q1], TH)
        query_lo = (query_cols[None, :] - window[:, 2, None]).reshape(HEADS, query_n, 1)
        query_hi = (query_cols[None, :] + window[:, 2, None]).reshape(HEADS, query_n, 1)
        query_ok = query_valid[:, :, q0:q1].reshape(blocks, query_n, 1).astype(jnp.float32)
        masks.append((key_mask, query_lo, query_hi, key_cols, query_ok))
    query_grid = query.reshape(frame_count, row_count, width, inner)
    out = None
    for group, extended in enumerate(groups):
        out = tile_attention(
            query_grid, extended, masks, group, out
        )
    return out


def attention_kernel(q_ref, k_ref, v_ref, *refs):
    o_ref = refs[-1]
    block = pl.program_id(1)
    span_t = 2 * TT + 1
    span_h = 3 * TH
    frame = block // ROW_TILES
    row = (block % ROW_TILES) * TH
    for part, (q0, q1, k0, k1) in enumerate(COLUMN_PARTS):
        km_ref, lo_ref, hi_ref, kc_ref, qv_ref = refs[5 * part : 5 * part + 5]
        query = q_ref[0, :, q0:q1].reshape(TH * (q1 - q0), HDIM)
        key = k_ref[0, pl.ds(frame, span_t), pl.ds(row, span_h), k0:k1].reshape(-1, HDIM)
        value = v_ref[0, pl.ds(frame, span_t), pl.ds(row, span_h), k0:k1].reshape(-1, HDIM)
        scores = lax.dot_general(
            query, key, (((1,), (1,)), ((), ())), preferred_element_type=jnp.float32
        ) * (1.0 / float(HDIM) ** 0.5)
        key_cols = kc_ref[...]
        allowed = (key_cols >= lo_ref[0]) & (key_cols <= hi_ref[0]) & (km_ref[0, 0] > 0.0)
        terms = jnp.where(allowed, jnp.exp(scores), jnp.float32(0.0))
        total = jnp.sum(terms, axis=-1, keepdims=True)
        seen = qv_ref[0] > 0.0
        total = jnp.where(seen, total, jnp.float32(1.0))
        weights = (terms / total).astype(jnp.bfloat16)
        result = jnp.dot(weights, value, preferred_element_type=jnp.float32)
        result = jnp.where(seen, result, jnp.float32(0.0)).astype(jnp.bfloat16)
        o_ref[0, :, q0:q1] = result.reshape(TH, q1 - q0, HDIM)


COLUMN_PARTS = ((0, 48, 0, 64), (48, 80, 32, 80))
ROW_TILES = 2


def tile_attention(query, extended, masks, group, out):
    frames, rows, width, inner = query.shape
    heads = extended.shape[-1] // HDIM
    out_shape = query.shape
    first = group * heads
    row_tiles = rows // TH
    assert row_tiles == ROW_TILES
    assert COLUMN_PARTS[-1][1] == width
    blocks = frames * row_tiles
    _, frames_ext, rows_ext, _, _ = extended.shape
    q_spec = pl.BlockSpec(
        (1, TH, width, HDIM), lambda h, b: (b // row_tiles, b % row_tiles, 0, first + h)
    )
    o_spec = q_spec
    in_specs = [
        q_spec,
        pl.BlockSpec((1, frames_ext, rows_ext, width, HDIM), lambda h, b: (0, 0, 0, 0, h)),
        pl.BlockSpec((1, frames_ext, rows_ext, width, HDIM), lambda h, b: (1, 0, 0, 0, h)),
    ]
    operands = [query, extended, extended]
    for key_mask, query_lo, query_hi, key_cols, query_ok in masks:
        key_n = key_mask.shape[-1]
        query_n = query_lo.shape[1]
        in_specs += [
            pl.BlockSpec((1, 1, 1, key_n), lambda h, b: (first + h, b, 0, 0)),
            pl.BlockSpec((1, query_n, 1), lambda h, b: (first + h, 0, 0)),
            pl.BlockSpec((1, query_n, 1), lambda h, b: (first + h, 0, 0)),
            pl.BlockSpec((1, key_n), lambda h, b: (0, 0)),
            pl.BlockSpec((1, query_n, 1), lambda h, b: (b, 0, 0)),
        ]
        operands += [key_mask, query_lo, query_hi, key_cols, query_ok]
    aliases = {}
    kernel = attention_kernel
    if out is not None:
        in_specs.append(pl.BlockSpec(memory_space=pl.ANY))
        operands.append(out)
        aliases = {len(operands) - 1: 0}
        count = len(operands)
        kernel = lambda *refs: attention_kernel(*refs[: count - 1], refs[count])
    return pl.pallas_call(
        kernel,
        grid=(heads, blocks),
        in_specs=in_specs,
        out_specs=o_spec,
        out_shape=jax.ShapeDtypeStruct(out_shape, jnp.bfloat16),
        input_output_aliases=aliases,
    )(*operands)


PROJECT_COLS = 256


def projection_kernel(x_ref, w_ref, g_ref, o_ref, *, normalize):
    acc = jnp.dot(x_ref[...], w_ref[...], preferred_element_type=jnp.float32)
    for part in range(acc.shape[1] // HDIM):
        piece = acc[:, part * HDIM : (part + 1) * HDIM]
        if normalize:
            power = jnp.mean(piece * piece, axis=-1, keepdims=True)
            piece = piece * lax.rsqrt(power + EPS) * g_ref[...]
        o_ref[:, part * HDIM : (part + 1) * HDIM] = piece.astype(o_ref.dtype)


def project(x, w, start, count, gain):
    tokens, features = x.shape
    cols = PROJECT_COLS
    normalize = gain is not None
    gain = gain.reshape(1, HDIM) if normalize else jnp.ones((1, HDIM), jnp.float32)
    first = start // cols
    return pl.pallas_call(
        functools.partial(projection_kernel, normalize=normalize),
        grid=(count // cols,),
        in_specs=[
            pl.BlockSpec((tokens, features), lambda j: (0, 0)),
            pl.BlockSpec((features, cols), lambda j: (0, first + j)),
            pl.BlockSpec((1, HDIM), lambda j: (0, 0)),
        ],
        out_specs=pl.BlockSpec((tokens, cols), lambda j: (0, j)),
        out_shape=jax.ShapeDtypeStruct((tokens, count), jnp.bfloat16),
    )(x, w, gain)


MESH = pl.DeviceIdType.MESH


def band_gather_kernel(w_ref, out_ref, local_sem, send_sem, recv_sem):
    count = lax.axis_size("height")
    me = lax.axis_index("height")
    frame_block = lax.axis_index("tm")
    barrier = pltpu.get_barrier_semaphore()
    for step in range(1, count):
        peer = lax.rem(me + step, count)
        pl.semaphore_signal(barrier, inc=1, device_id=(frame_block, peer), device_id_type=MESH)
    pl.semaphore_wait(barrier, count - 1)
    own = pltpu.make_async_copy(w_ref, out_ref.at[me], local_sem)
    own.start()
    copies = []
    for step in range(1, count):
        peer = lax.rem(me + step, count)
        copy = pltpu.make_async_remote_copy(
            src_ref=w_ref,
            dst_ref=out_ref.at[me],
            send_sem=send_sem.at[step],
            recv_sem=recv_sem.at[me],
            device_id=(frame_block, peer),
            device_id_type=MESH,
        )
        copy.start()
        copies.append(copy)
    for copy in copies:
        copy.wait_send()
    for step in range(1, count):
        source = lax.rem(me + count - step, count)
        incoming = pltpu.make_async_remote_copy(
            src_ref=w_ref,
            dst_ref=out_ref.at[source],
            send_sem=send_sem.at[step],
            recv_sem=recv_sem.at[source],
            device_id=(frame_block, source),
            device_id_type=MESH,
        )
        incoming.wait_recv()
    own.wait()


def band_gather(w):
    rows, cols = w.shape
    count = lax.axis_size("height")
    gathered = pl.pallas_call(
        band_gather_kernel,
        in_specs=[pl.BlockSpec(memory_space=pl.ANY)],
        out_specs=pl.BlockSpec(memory_space=pl.ANY),
        out_shape=jax.ShapeDtypeStruct((count, rows, cols), w.dtype),
        scratch_shapes=[
            pltpu.SemaphoreType.DMA(()),
            pltpu.SemaphoreType.DMA((count,)),
            pltpu.SemaphoreType.DMA((count,)),
        ],
        compiler_params=pltpu.CompilerParams(collective_id=0, has_side_effects=True),
    )(w)
    return gathered.reshape(count * rows, cols)


def solution(mesh):
    in_specs = (
        P("tm", "height", None, None),
        P(),
        P(),
        P(("tm", "height"), None),
        P(),
        P(),
        P(),
        P(),
    )
    out_specs = P("tm", "height", None, None)
    return jax.shard_map(
        per_device, mesh=mesh, in_specs=in_specs, out_specs=out_specs, check_vma=False
    )
```

```python
import functools

import jax
import jax.numpy as jnp
from jax import lax
from jax.sharding import PartitionSpec as P
from jax.experimental import pallas as pl
from jax.experimental.pallas import tpu as pltpu

HDIM = 128
HEADS = 12
TT = 1
TH = 2
TW = 8
GROUPS = 2


EPS = 1e-06


def with_halo(cells, sides, width):
    for axis, dim in sides:
        count = lax.axis_size(axis)
        ends = count - 1
        head = lax.slice_in_dim(cells, 0, width, axis=dim)
        tail = lax.slice_in_dim(cells, cells.shape[dim] - width, cells.shape[dim], axis=dim)
        cells = jnp.concatenate(
            [
                lax.ppermute(tail, axis, [(i, (i + 1) % count) for i in range(ends)]),
                cells,
                lax.ppermute(head, axis, [((i + 1) % count, i) for i in range(ends)]),
            ],
            axis=dim,
        )
    return cells


def modulate(tokens, mod_scale, mod_shift):
    values = tokens.astype(jnp.float32)
    mean = jnp.mean(values, axis=-1, keepdims=True)
    centred = values - mean
    variance = jnp.mean(centred * centred, axis=-1, keepdims=True)
    normed = centred * lax.rsqrt(variance + EPS)
    return (normed * (1.0 + mod_scale) + mod_shift).astype(jnp.bfloat16)


def head_norm(values, gain):
    power = jnp.mean(values * values, axis=-1, keepdims=True)
    return (values * lax.rsqrt(power + EPS) * gain).astype(jnp.bfloat16)


def tile_coords(frames, rows, width):
    shape = (frames.shape[0], rows.shape[0], width)
    columns = jnp.arange(width, dtype=jnp.int32)
    frame_tiles = jnp.broadcast_to((frames // TT)[:, None, None], shape).reshape(-1)
    row_tiles = jnp.broadcast_to((rows // TH)[None, :, None], shape).reshape(-1)
    column_tiles = jnp.broadcast_to((columns // TW)[None, None, :], shape).reshape(-1)
    return (frame_tiles, row_tiles, column_tiles)


def per_device(tokens, mod_scale, mod_shift, w_qkv, q_gain, k_gain, window, valid):
    frame_count, row_count, width, features = tokens.shape
    token_count = frame_count * row_count * width
    modulated = modulate(tokens.reshape(token_count, features), mod_scale, mod_shift)
    band_weight = band_gather(w_qkv)
    full_weight = lax.all_gather(band_weight, "tm", axis=0, tiled=True)
    inner = full_weight.shape[1] // 3
    group_cols = inner // GROUPS
    tiled = (frame_count // TT, TT, row_count // TH, TH, width, group_cols)
    groups = []
    for group in range(GROUPS):
        start = group * group_cols
        stacked = project_kv(modulated, full_weight, start, group_cols, k_gain)
        stacked = stacked.reshape(2, *tiled)
        groups.append(with_halo(stacked, (("tm", 1), ("height", 3)), 1))
    query = project(modulated, full_weight, 0, inner, q_gain)
    frames_ext = frame_count + 2 * TT
    rows_ext = row_count + 2 * TH
    groups = [g.reshape(2, frames_ext, rows_ext, width, group_cols) for g in groups]
    frame_block = lax.axis_index("tm")
    row_block = lax.axis_index("height")
    first_frame = frame_block * frame_count
    first_row = row_block * row_count
    zero = jnp.int32(0)
    valid_pad = jnp.pad(valid, ((TT, TT), (TH, TH), (0, 0)))
    key_valid = lax.dynamic_slice(
        valid_pad, (first_frame, first_row, zero), (frames_ext, rows_ext, width)
    )
    query_valid = lax.dynamic_slice(
        valid, (first_frame, first_row, zero), (frame_count, row_count, width)
    )
    row_tiles = row_count // TH
    blocks = frame_count * row_tiles
    span_t = 2 * TT + 1
    span_h = 3 * TH
    query_n = TH * width
    key_n = span_t * span_h * width
    block_valid = jnp.stack(
        [
            key_valid[f : f + span_t, TH * rt : TH * rt + span_h].reshape(-1)
            for f in range(frame_count)
            for rt in range(row_tiles)
        ]
    )
    apart_t = jnp.abs(jnp.arange(span_t, dtype=jnp.int32) - TT)
    apart_h = jnp.abs(jnp.arange(span_h, dtype=jnp.int32) // TH - 1)
    near = (apart_t[None, :, None, None] <= window[:, 0, None, None, None]) & (
        apart_h[None, None, :, None] <= window[:, 1, None, None, None]
    )
    near = jnp.broadcast_to(near, (HEADS, span_t, span_h, width)).reshape(HEADS, 1, key_n)
    key_mask = (near & (block_valid[None] > 0)).astype(jnp.float32).reshape(HEADS, blocks, 1, key_n)
    column_tiles = jnp.arange(width, dtype=jnp.int32) // TW
    key_cols = jnp.tile(column_tiles, span_t * span_h).reshape(1, key_n)
    query_cols = jnp.tile(column_tiles, TH)
    query_lo = (query_cols[None, :] - window[:, 2, None]).reshape(HEADS, query_n, 1)
    query_hi = (query_cols[None, :] + window[:, 2, None]).reshape(HEADS, query_n, 1)
    query_ok = query_valid.reshape(blocks, query_n, 1).astype(jnp.float32)
    query_grid = query.reshape(frame_count, row_count, width, inner)
    out = None
    for group, extended in enumerate(groups):
        out = tile_attention(
            query_grid, extended, key_mask, query_lo, query_hi, key_cols, query_ok, group, out
        )
    return out


def attention_kernel(q_ref, k_ref, v_ref, km_ref, lo_ref, hi_ref, kc_ref, qv_ref, o_ref):
    block = pl.program_id(1)
    span_t = 2 * TT + 1
    span_h = 3 * TH
    frame = block // ROW_TILES
    row = (block % ROW_TILES) * TH
    width = q_ref.shape[2]
    query = q_ref[0].reshape(TH * width, HDIM)
    key = k_ref[0, pl.ds(frame, span_t), pl.ds(row, span_h)].reshape(-1, HDIM)
    value = v_ref[0, pl.ds(frame, span_t), pl.ds(row, span_h)].reshape(-1, HDIM)
    scores = lax.dot_general(
        query, key, (((1,), (1,)), ((), ())), preferred_element_type=jnp.float32
    ) * (1.0 / float(HDIM) ** 0.5)
    key_cols = kc_ref[...]
    allowed = (key_cols >= lo_ref[0]) & (key_cols <= hi_ref[0]) & (km_ref[0, 0] > 0.0)
    terms = jnp.where(allowed, jnp.exp(scores), jnp.float32(0.0))
    total = jnp.sum(terms, axis=-1, keepdims=True)
    seen = qv_ref[0] > 0.0
    total = jnp.where(seen, total, jnp.float32(1.0))
    weights = (terms / total).astype(jnp.bfloat16)
    result = jnp.dot(weights, value, preferred_element_type=jnp.float32)
    result = jnp.where(seen, result, jnp.float32(0.0)).astype(jnp.bfloat16)
    o_ref[0] = result.reshape(TH, width, HDIM)


ROW_TILES = 2


def tile_attention(query, extended, key_mask, query_lo, query_hi, key_cols, query_ok, group, out):
    frames, rows, width, inner = query.shape
    heads = extended.shape[-1] // HDIM
    first = group * heads
    row_tiles = rows // TH
    assert row_tiles == ROW_TILES
    blocks = frames * row_tiles
    _, frames_ext, rows_ext, _, _ = extended.shape
    key_n = key_mask.shape[-1]
    query_n = TH * width
    q_spec = pl.BlockSpec(
        (1, TH, width, HDIM), lambda h, b: (b // row_tiles, b % row_tiles, 0, first + h)
    )
    in_specs = [
        q_spec,
        pl.BlockSpec((1, frames_ext, rows_ext, width, HDIM), lambda h, b: (0, 0, 0, 0, h)),
        pl.BlockSpec((1, frames_ext, rows_ext, width, HDIM), lambda h, b: (1, 0, 0, 0, h)),
        pl.BlockSpec((1, 1, 1, key_n), lambda h, b: (first + h, b, 0, 0)),
        pl.BlockSpec((1, query_n, 1), lambda h, b: (first + h, 0, 0)),
        pl.BlockSpec((1, query_n, 1), lambda h, b: (first + h, 0, 0)),
        pl.BlockSpec((1, key_n), lambda h, b: (0, 0)),
        pl.BlockSpec((1, query_n, 1), lambda h, b: (b, 0, 0)),
    ]
    operands = [query, extended, extended, key_mask, query_lo, query_hi, key_cols, query_ok]
    aliases = {}
    kernel = attention_kernel
    if out is not None:
        in_specs.append(pl.BlockSpec(memory_space=pl.ANY))
        operands.append(out)
        aliases = {len(operands) - 1: 0}
        kernel = lambda *refs: attention_kernel(*refs[:8], refs[9])
    return pl.pallas_call(
        kernel,
        grid=(heads, blocks),
        in_specs=in_specs,
        out_specs=q_spec,
        out_shape=jax.ShapeDtypeStruct(query.shape, jnp.bfloat16),
        input_output_aliases=aliases,
    )(*operands)


PROJECT_COLS = 256


def projection_kernel(x_ref, w_ref, g_ref, o_ref, *, normalize):
    acc = jnp.dot(x_ref[...], w_ref[...], preferred_element_type=jnp.float32)
    for part in range(acc.shape[1] // HDIM):
        piece = acc[:, part * HDIM : (part + 1) * HDIM]
        if normalize:
            power = jnp.mean(piece * piece, axis=-1, keepdims=True)
            piece = piece * lax.rsqrt(power + EPS) * g_ref[...]
        o_ref[:, part * HDIM : (part + 1) * HDIM] = piece.astype(o_ref.dtype)


def project(x, w, start, count, gain):
    tokens, features = x.shape
    cols = PROJECT_COLS
    normalize = gain is not None
    gain = gain.reshape(1, HDIM) if normalize else jnp.ones((1, HDIM), jnp.float32)
    first = start // cols
    return pl.pallas_call(
        functools.partial(projection_kernel, normalize=normalize),
        grid=(count // cols,),
        in_specs=[
            pl.BlockSpec((tokens, features), lambda j: (0, 0)),
            pl.BlockSpec((features, cols), lambda j: (0, first + j)),
            pl.BlockSpec((1, HDIM), lambda j: (0, 0)),
        ],
        out_specs=pl.BlockSpec((tokens, cols), lambda j: (0, j)),
        out_shape=jax.ShapeDtypeStruct((tokens, count), jnp.bfloat16),
    )(x, w, gain)


MESH = pl.DeviceIdType.MESH


def band_gather_kernel(w_ref, out_ref, local_sem, send_sem, recv_sem):
    count = lax.axis_size("height")
    me = lax.axis_index("height")
    frame_block = lax.axis_index("tm")
    barrier = pltpu.get_barrier_semaphore()
    for step in range(1, count):
        peer = lax.rem(me + step, count)
        pl.semaphore_signal(barrier, inc=1, device_id=(frame_block, peer), device_id_type=MESH)
    pl.semaphore_wait(barrier, count - 1)
    own = pltpu.make_async_copy(w_ref, out_ref.at[me], local_sem)
    own.start()
    copies = []
    for step in range(1, count):
        peer = lax.rem(me + step, count)
        copy = pltpu.make_async_remote_copy(
            src_ref=w_ref,
            dst_ref=out_ref.at[me],
            send_sem=send_sem.at[step],
            recv_sem=recv_sem.at[me],
            device_id=(frame_block, peer),
            device_id_type=MESH,
        )
        copy.start()
        copies.append(copy)
    for copy in copies:
        copy.wait_send()
    for step in range(1, count):
        source = lax.rem(me + count - step, count)
        incoming = pltpu.make_async_remote_copy(
            src_ref=w_ref,
            dst_ref=out_ref.at[source],
            send_sem=send_sem.at[step],
            recv_sem=recv_sem.at[source],
            device_id=(frame_block, source),
            device_id_type=MESH,
        )
        incoming.wait_recv()
    own.wait()


def band_gather(w):
    rows, cols = w.shape
    count = lax.axis_size("height")
    gathered = pl.pallas_call(
        band_gather_kernel,
        in_specs=[pl.BlockSpec(memory_space=pl.ANY)],
        out_specs=pl.BlockSpec(memory_space=pl.ANY),
        out_shape=jax.ShapeDtypeStruct((count, rows, cols), w.dtype),
        scratch_shapes=[
            pltpu.SemaphoreType.DMA(()),
            pltpu.SemaphoreType.DMA((count,)),
            pltpu.SemaphoreType.DMA((count,)),
        ],
        compiler_params=pltpu.CompilerParams(collective_id=0, has_side_effects=True),
    )(w)
    return gathered.reshape(count * rows, cols)


def projection_kv_kernel(x_ref, w_ref, g_ref, o_ref):
    acc = jnp.dot(x_ref[...], w_ref[...], preferred_element_type=jnp.float32)
    is_key = pl.program_id(0) < pl.num_programs(0) // 2
    for part in range(acc.shape[1] // HDIM):
        piece = acc[:, part * HDIM : (part + 1) * HDIM]
        power = jnp.mean(piece * piece, axis=-1, keepdims=True)
        scale = jnp.where(is_key, lax.rsqrt(power + EPS), jnp.float32(1.0))
        gain = jnp.where(is_key, g_ref[...], jnp.float32(1.0))
        normed = jnp.where(is_key, piece * scale * gain, piece)
        o_ref[0, :, part * HDIM : (part + 1) * HDIM] = normed.astype(o_ref.dtype)


def project_kv(x, w, start, count, gain):
    tokens, features = x.shape
    cols = PROJECT_COLS
    inner = w.shape[1] // 3
    steps = count // cols
    key_first = (inner + start) // cols
    value_first = (2 * inner + start) // cols

    def weight_block(j):
        return (0, jnp.where(j < steps, key_first + j, value_first + j - steps))

    return pl.pallas_call(
        projection_kv_kernel,
        grid=(2 * steps,),
        in_specs=[
            pl.BlockSpec((tokens, features), lambda j: (0, 0)),
            pl.BlockSpec((features, cols), weight_block),
            pl.BlockSpec((1, HDIM), lambda j: (0, 0)),
        ],
        out_specs=pl.BlockSpec((1, tokens, cols), lambda j: (j // steps, 0, j % steps)),
        out_shape=jax.ShapeDtypeStruct((2, tokens, count), jnp.bfloat16),
    )(x, w, gain.reshape(1, HDIM))


def solution(mesh):
    in_specs = (
        P("tm", "height", None, None),
        P(),
        P(),
        P(("tm", "height"), None),
        P(),
        P(),
        P(),
        P(),
    )
    out_specs = P("tm", "height", None, None)
    return jax.shard_map(
        per_device, mesh=mesh, in_specs=in_specs, out_specs=out_specs, check_vma=False
    )
```

```python
import functools

import jax
import jax.numpy as jnp
from jax import lax
from jax.sharding import PartitionSpec as P
from jax.experimental import pallas as pl
from jax.experimental.pallas import tpu as pltpu

HDIM = 128
HEADS = 12
TT = 1
TH = 2
TW = 8
GROUPS = 2


EPS = 1e-06


def with_halo(cells, sides, width):
    for axis, dim in sides:
        count = lax.axis_size(axis)
        ends = count - 1
        head = lax.slice_in_dim(cells, 0, width, axis=dim)
        tail = lax.slice_in_dim(cells, cells.shape[dim] - width, cells.shape[dim], axis=dim)
        cells = jnp.concatenate(
            [
                lax.ppermute(tail, axis, [(i, (i + 1) % count) for i in range(ends)]),
                cells,
                lax.ppermute(head, axis, [((i + 1) % count, i) for i in range(ends)]),
            ],
            axis=dim,
        )
    return cells


def modulate(tokens, mod_scale, mod_shift):
    values = tokens.astype(jnp.float32)
    mean = jnp.mean(values, axis=-1, keepdims=True)
    centred = values - mean
    variance = jnp.mean(centred * centred, axis=-1, keepdims=True)
    normed = centred * lax.rsqrt(variance + EPS)
    return (normed * (1.0 + mod_scale) + mod_shift).astype(jnp.bfloat16)


def head_norm(values, gain):
    power = jnp.mean(values * values, axis=-1, keepdims=True)
    return (values * lax.rsqrt(power + EPS) * gain).astype(jnp.bfloat16)


def tile_coords(frames, rows, width):
    shape = (frames.shape[0], rows.shape[0], width)
    columns = jnp.arange(width, dtype=jnp.int32)
    frame_tiles = jnp.broadcast_to((frames // TT)[:, None, None], shape).reshape(-1)
    row_tiles = jnp.broadcast_to((rows // TH)[None, :, None], shape).reshape(-1)
    column_tiles = jnp.broadcast_to((columns // TW)[None, None, :], shape).reshape(-1)
    return (frame_tiles, row_tiles, column_tiles)


def per_device(tokens, mod_scale, mod_shift, w_qkv, q_gain, k_gain, window, valid):
    frame_count, row_count, width, features = tokens.shape
    token_count = frame_count * row_count * width
    modulated = modulate(tokens.reshape(token_count, features), mod_scale, mod_shift)
    band_weight = band_gather(w_qkv)
    full_weight = lax.all_gather(band_weight, "tm", axis=0, tiled=True)
    inner = full_weight.shape[1] // 3
    group_cols = inner // GROUPS
    tiled = (frame_count // TT, TT, row_count // TH, TH, width, group_cols)
    groups = []
    for group in range(GROUPS):
        start = group * group_cols
        stacked = project_kv(modulated, full_weight, start, group_cols, k_gain)
        stacked = stacked.reshape(2, *tiled)
        groups.append(with_halo(stacked, (("tm", 1), ("height", 3)), 1))
    query = project(modulated, full_weight, 0, inner, q_gain)
    frames_ext = frame_count + 2 * TT
    rows_ext = row_count + 2 * TH
    groups = [g.reshape(2, frames_ext, rows_ext, width, group_cols) for g in groups]
    frame_block = lax.axis_index("tm")
    row_block = lax.axis_index("height")
    first_frame = frame_block * frame_count
    first_row = row_block * row_count
    zero = jnp.int32(0)
    valid_pad = jnp.pad(valid, ((TT, TT), (TH, TH), (0, 0)))
    key_valid = lax.dynamic_slice(
        valid_pad, (first_frame, first_row, zero), (frames_ext, rows_ext, width)
    )
    query_valid = lax.dynamic_slice(
        valid, (first_frame, first_row, zero), (frame_count, row_count, width)
    )
    row_tiles = row_count // TH
    blocks = frame_count * row_tiles
    span_t = 2 * TT + 1
    span_h = 3 * TH
    query_n = TH * width
    key_n = span_t * span_h * width
    block_valid = jnp.stack(
        [
            key_valid[f : f + span_t, TH * rt : TH * rt + span_h].reshape(-1)
            for f in range(frame_count)
            for rt in range(row_tiles)
        ]
    )
    apart_t = jnp.abs(jnp.arange(span_t, dtype=jnp.int32) - TT)
    apart_h = jnp.abs(jnp.arange(span_h, dtype=jnp.int32) // TH - 1)
    near = (apart_t[None, :, None, None] <= window[:, 0, None, None, None]) & (
        apart_h[None, None, :, None] <= window[:, 1, None, None, None]
    )
    near = jnp.broadcast_to(near, (HEADS, span_t, span_h, width)).reshape(HEADS, 1, key_n)
    key_mask = (near & (block_valid[None] > 0)).astype(jnp.float32).reshape(HEADS, blocks, 1, key_n)
    column_tiles = jnp.arange(width, dtype=jnp.int32) // TW
    key_cols = jnp.tile(column_tiles, span_t * span_h).reshape(1, key_n)
    query_cols = jnp.tile(column_tiles, TH)
    query_lo = (query_cols[None, :] - window[:, 2, None]).reshape(HEADS, query_n, 1)
    query_hi = (query_cols[None, :] + window[:, 2, None]).reshape(HEADS, query_n, 1)
    query_ok = query_valid.reshape(blocks, query_n, 1).astype(jnp.float32)
    query_grid = query.reshape(frame_count, row_count, width, inner)
    out = None
    for group, extended in enumerate(groups):
        out = tile_attention(
            query_grid, extended, key_mask, query_lo, query_hi, key_cols, query_ok, group, out
        )
    return out


def attention_kernel(q_ref, k_ref, v_ref, km_ref, lo_ref, hi_ref, kc_ref, qv_ref, o_ref):
    block = pl.program_id(1)
    span_t = 2 * TT + 1
    span_h = 3 * TH
    frame = block // ROW_TILES
    row = (block % ROW_TILES) * TH
    width = q_ref.shape[2]
    query = q_ref[0].reshape(TH * width, HDIM)
    key = k_ref[0, pl.ds(frame, span_t), pl.ds(row, span_h)].reshape(-1, HDIM)
    value = v_ref[0, pl.ds(frame, span_t), pl.ds(row, span_h)].reshape(-1, HDIM)
    scores = lax.dot_general(
        query, key, (((1,), (1,)), ((), ())), preferred_element_type=jnp.float32
    ) * (1.0 / float(HDIM) ** 0.5)
    key_cols = kc_ref[...]
    allowed = (key_cols >= lo_ref[0]) & (key_cols <= hi_ref[0]) & (km_ref[0, 0] > 0.0)
    terms = jnp.where(allowed, jnp.exp(scores), jnp.float32(0.0))
    total = jnp.sum(terms, axis=-1, keepdims=True)
    seen = qv_ref[0] > 0.0
    total = jnp.where(seen, total, jnp.float32(1.0))
    weights = (terms * (1.0 / total)).astype(jnp.bfloat16)
    result = jnp.dot(weights, value, preferred_element_type=jnp.float32)
    result = jnp.where(seen, result, jnp.float32(0.0)).astype(jnp.bfloat16)
    o_ref[0] = result.reshape(TH, width, HDIM)


ROW_TILES = 2


def tile_attention(query, extended, key_mask, query_lo, query_hi, key_cols, query_ok, group, out):
    frames, rows, width, inner = query.shape
    heads = extended.shape[-1] // HDIM
    first = group * heads
    row_tiles = rows // TH
    assert row_tiles == ROW_TILES
    blocks = frames * row_tiles
    _, frames_ext, rows_ext, _, _ = extended.shape
    key_n = key_mask.shape[-1]
    query_n = TH * width
    q_spec = pl.BlockSpec(
        (1, TH, width, HDIM), lambda h, b: (b // row_tiles, b % row_tiles, 0, first + h)
    )
    in_specs = [
        q_spec,
        pl.BlockSpec((1, frames_ext, rows_ext, width, HDIM), lambda h, b: (0, 0, 0, 0, h)),
        pl.BlockSpec((1, frames_ext, rows_ext, width, HDIM), lambda h, b: (1, 0, 0, 0, h)),
        pl.BlockSpec((1, 1, 1, key_n), lambda h, b: (first + h, b, 0, 0)),
        pl.BlockSpec((1, query_n, 1), lambda h, b: (first + h, 0, 0)),
        pl.BlockSpec((1, query_n, 1), lambda h, b: (first + h, 0, 0)),
        pl.BlockSpec((1, key_n), lambda h, b: (0, 0)),
        pl.BlockSpec((1, query_n, 1), lambda h, b: (b, 0, 0)),
    ]
    operands = [query, extended, extended, key_mask, query_lo, query_hi, key_cols, query_ok]
    aliases = {}
    kernel = attention_kernel
    if out is not None:
        in_specs.append(pl.BlockSpec(memory_space=pl.ANY))
        operands.append(out)
        aliases = {len(operands) - 1: 0}
        kernel = lambda *refs: attention_kernel(*refs[:8], refs[9])
    return pl.pallas_call(
        kernel,
        grid=(heads, blocks),
        in_specs=in_specs,
        out_specs=q_spec,
        out_shape=jax.ShapeDtypeStruct(query.shape, jnp.bfloat16),
        input_output_aliases=aliases,
    )(*operands)


PROJECT_COLS = 256


def projection_kernel(x_ref, w_ref, g_ref, o_ref, *, normalize):
    acc = jnp.dot(x_ref[...], w_ref[...], preferred_element_type=jnp.float32)
    for part in range(acc.shape[1] // HDIM):
        piece = acc[:, part * HDIM : (part + 1) * HDIM]
        if normalize:
            power = jnp.mean(piece * piece, axis=-1, keepdims=True)
            piece = piece * lax.rsqrt(power + EPS) * g_ref[...]
        o_ref[:, part * HDIM : (part + 1) * HDIM] = piece.astype(o_ref.dtype)


def project(x, w, start, count, gain):
    tokens, features = x.shape
    cols = PROJECT_COLS
    normalize = gain is not None
    gain = gain.reshape(1, HDIM) if normalize else jnp.ones((1, HDIM), jnp.float32)
    first = start // cols
    return pl.pallas_call(
        functools.partial(projection_kernel, normalize=normalize),
        grid=(count // cols,),
        in_specs=[
            pl.BlockSpec((tokens, features), lambda j: (0, 0)),
            pl.BlockSpec((features, cols), lambda j: (0, first + j)),
            pl.BlockSpec((1, HDIM), lambda j: (0, 0)),
        ],
        out_specs=pl.BlockSpec((tokens, cols), lambda j: (0, j)),
        out_shape=jax.ShapeDtypeStruct((tokens, count), jnp.bfloat16),
    )(x, w, gain)


MESH = pl.DeviceIdType.MESH


def band_gather_kernel(w_ref, out_ref, local_sem, send_sem, recv_sem):
    count = lax.axis_size("height")
    me = lax.axis_index("height")
    frame_block = lax.axis_index("tm")
    barrier = pltpu.get_barrier_semaphore()
    for step in range(1, count):
        peer = lax.rem(me + step, count)
        pl.semaphore_signal(barrier, inc=1, device_id=(frame_block, peer), device_id_type=MESH)
    pl.semaphore_wait(barrier, count - 1)
    own = pltpu.make_async_copy(w_ref, out_ref.at[me], local_sem)
    own.start()
    copies = []
    for step in range(1, count):
        peer = lax.rem(me + step, count)
        copy = pltpu.make_async_remote_copy(
            src_ref=w_ref,
            dst_ref=out_ref.at[me],
            send_sem=send_sem.at[step],
            recv_sem=recv_sem.at[me],
            device_id=(frame_block, peer),
            device_id_type=MESH,
        )
        copy.start()
        copies.append(copy)
    for copy in copies:
        copy.wait_send()
    for step in range(1, count):
        source = lax.rem(me + count - step, count)
        incoming = pltpu.make_async_remote_copy(
            src_ref=w_ref,
            dst_ref=out_ref.at[source],
            send_sem=send_sem.at[step],
            recv_sem=recv_sem.at[source],
            device_id=(frame_block, source),
            device_id_type=MESH,
        )
        incoming.wait_recv()
    own.wait()


def band_gather(w):
    rows, cols = w.shape
    count = lax.axis_size("height")
    gathered = pl.pallas_call(
        band_gather_kernel,
        in_specs=[pl.BlockSpec(memory_space=pl.ANY)],
        out_specs=pl.BlockSpec(memory_space=pl.ANY),
        out_shape=jax.ShapeDtypeStruct((count, rows, cols), w.dtype),
        scratch_shapes=[
            pltpu.SemaphoreType.DMA(()),
            pltpu.SemaphoreType.DMA((count,)),
            pltpu.SemaphoreType.DMA((count,)),
        ],
        compiler_params=pltpu.CompilerParams(collective_id=0, has_side_effects=True),
    )(w)
    return gathered.reshape(count * rows, cols)


def projection_kv_kernel(x_ref, w_ref, g_ref, o_ref):
    acc = jnp.dot(x_ref[...], w_ref[...], preferred_element_type=jnp.float32)
    is_key = pl.program_id(0) < pl.num_programs(0) // 2
    for part in range(acc.shape[1] // HDIM):
        piece = acc[:, part * HDIM : (part + 1) * HDIM]
        power = jnp.mean(piece * piece, axis=-1, keepdims=True)
        scale = jnp.where(is_key, lax.rsqrt(power + EPS), jnp.float32(1.0))
        gain = jnp.where(is_key, g_ref[...], jnp.float32(1.0))
        normed = jnp.where(is_key, piece * scale * gain, piece)
        o_ref[0, :, part * HDIM : (part + 1) * HDIM] = normed.astype(o_ref.dtype)


def project_kv(x, w, start, count, gain):
    tokens, features = x.shape
    cols = PROJECT_COLS
    inner = w.shape[1] // 3
    steps = count // cols
    key_first = (inner + start) // cols
    value_first = (2 * inner + start) // cols

    def weight_block(j):
        return (0, jnp.where(j < steps, key_first + j, value_first + j - steps))

    return pl.pallas_call(
        projection_kv_kernel,
        grid=(2 * steps,),
        in_specs=[
            pl.BlockSpec((tokens, features), lambda j: (0, 0)),
            pl.BlockSpec((features, cols), weight_block),
            pl.BlockSpec((1, HDIM), lambda j: (0, 0)),
        ],
        out_specs=pl.BlockSpec((1, tokens, cols), lambda j: (j // steps, 0, j % steps)),
        out_shape=jax.ShapeDtypeStruct((2, tokens, count), jnp.bfloat16),
    )(x, w, gain.reshape(1, HDIM))


def solution(mesh):
    in_specs = (
        P("tm", "height", None, None),
        P(),
        P(),
        P(("tm", "height"), None),
        P(),
        P(),
        P(),
        P(),
    )
    out_specs = P("tm", "height", None, None)
    return jax.shard_map(
        per_device, mesh=mesh, in_specs=in_specs, out_specs=out_specs, check_vma=False
    )
```

```python
import functools

import jax
import jax.numpy as jnp
from jax import lax
from jax.sharding import PartitionSpec as P
from jax.experimental import pallas as pl
from jax.experimental.pallas import tpu as pltpu

HDIM = 128
HEADS = 12
TT = 1
TH = 2
TW = 8
GROUPS = 2


EPS = 1e-06


def with_halo(cells, sides, width):
    for axis, dim in sides:
        count = lax.axis_size(axis)
        ends = count - 1
        head = lax.slice_in_dim(cells, 0, width, axis=dim)
        tail = lax.slice_in_dim(cells, cells.shape[dim] - width, cells.shape[dim], axis=dim)
        cells = jnp.concatenate(
            [
                lax.ppermute(tail, axis, [(i, (i + 1) % count) for i in range(ends)]),
                cells,
                lax.ppermute(head, axis, [((i + 1) % count, i) for i in range(ends)]),
            ],
            axis=dim,
        )
    return cells


def modulate(tokens, mod_scale, mod_shift):
    values = tokens.astype(jnp.float32)
    mean = jnp.mean(values, axis=-1, keepdims=True)
    centred = values - mean
    variance = jnp.mean(centred * centred, axis=-1, keepdims=True)
    normed = centred * lax.rsqrt(variance + EPS)
    return (normed * (1.0 + mod_scale) + mod_shift).astype(jnp.bfloat16)


def head_norm(values, gain):
    power = jnp.mean(values * values, axis=-1, keepdims=True)
    return (values * lax.rsqrt(power + EPS) * gain).astype(jnp.bfloat16)


def tile_coords(frames, rows, width):
    shape = (frames.shape[0], rows.shape[0], width)
    columns = jnp.arange(width, dtype=jnp.int32)
    frame_tiles = jnp.broadcast_to((frames // TT)[:, None, None], shape).reshape(-1)
    row_tiles = jnp.broadcast_to((rows // TH)[None, :, None], shape).reshape(-1)
    column_tiles = jnp.broadcast_to((columns // TW)[None, None, :], shape).reshape(-1)
    return (frame_tiles, row_tiles, column_tiles)


def per_device(tokens, mod_scale, mod_shift, w_qkv, q_gain, k_gain, window, valid):
    frame_count, row_count, width, features = tokens.shape
    token_count = frame_count * row_count * width
    modulated = modulate(tokens.reshape(token_count, features), mod_scale, mod_shift)
    frames_ext = frame_count + 2 * TT
    rows_ext = row_count + 2 * TH
    token_tiles = (frame_count // TT, TT, row_count // TH, TH, width, features)
    halo_tokens = with_halo(modulated.reshape(token_tiles), (("tm", 0), ("height", 2)), 1)
    halo_tokens = halo_tokens.reshape(frames_ext * rows_ext * width, features)
    band_weight = band_gather(w_qkv)
    full_weight = lax.all_gather(band_weight, "tm", axis=0, tiled=True)
    inner = full_weight.shape[1] // 3
    group_cols = inner // GROUPS
    groups = []
    for group in range(GROUPS):
        start = group * group_cols
        stacked = project_kv(halo_tokens, full_weight, start, group_cols, k_gain)
        groups.append(stacked.reshape(2, frames_ext, rows_ext, width, group_cols))
    query = project(modulated, full_weight, 0, inner, q_gain)
    frame_block = lax.axis_index("tm")
    row_block = lax.axis_index("height")
    first_frame = frame_block * frame_count
    first_row = row_block * row_count
    zero = jnp.int32(0)
    valid_pad = jnp.pad(valid, ((TT, TT), (TH, TH), (0, 0)))
    key_valid = lax.dynamic_slice(
        valid_pad, (first_frame, first_row, zero), (frames_ext, rows_ext, width)
    )
    query_valid = lax.dynamic_slice(
        valid, (first_frame, first_row, zero), (frame_count, row_count, width)
    )
    row_tiles = row_count // TH
    blocks = frame_count * row_tiles
    span_t = 2 * TT + 1
    span_h = 3 * TH
    query_n = TH * width
    key_n = span_t * span_h * width
    block_valid = jnp.stack(
        [
            key_valid[f : f + span_t, TH * rt : TH * rt + span_h].reshape(-1)
            for f in range(frame_count)
            for rt in range(row_tiles)
        ]
    )
    apart_t = jnp.abs(jnp.arange(span_t, dtype=jnp.int32) - TT)
    apart_h = jnp.abs(jnp.arange(span_h, dtype=jnp.int32) // TH - 1)
    near = (apart_t[None, :, None, None] <= window[:, 0, None, None, None]) & (
        apart_h[None, None, :, None] <= window[:, 1, None, None, None]
    )
    near = jnp.broadcast_to(near, (HEADS, span_t, span_h, width)).reshape(HEADS, 1, key_n)
    key_mask = (near & (block_valid[None] > 0)).astype(jnp.float32).reshape(HEADS, blocks, 1, key_n)
    column_tiles = jnp.arange(width, dtype=jnp.int32) // TW
    key_cols = jnp.tile(column_tiles, span_t * span_h).reshape(1, key_n)
    query_cols = jnp.tile(column_tiles, TH)
    query_lo = (query_cols[None, :] - window[:, 2, None]).reshape(HEADS, query_n, 1)
    query_hi = (query_cols[None, :] + window[:, 2, None]).reshape(HEADS, query_n, 1)
    query_ok = query_valid.reshape(blocks, query_n, 1).astype(jnp.float32)
    query_grid = query.reshape(frame_count, row_count, width, inner)
    out = None
    for group, extended in enumerate(groups):
        out = tile_attention(
            query_grid, extended, key_mask, query_lo, query_hi, key_cols, query_ok, group, out
        )
    return out


def attention_kernel(q_ref, k_ref, v_ref, km_ref, lo_ref, hi_ref, kc_ref, qv_ref, o_ref):
    block = pl.program_id(1)
    span_t = 2 * TT + 1
    span_h = 3 * TH
    frame = block // ROW_TILES
    row = (block % ROW_TILES) * TH
    width = q_ref.shape[2]
    query = q_ref[0].reshape(TH * width, HDIM)
    key = k_ref[0, pl.ds(frame, span_t), pl.ds(row, span_h)].reshape(-1, HDIM)
    value = v_ref[0, pl.ds(frame, span_t), pl.ds(row, span_h)].reshape(-1, HDIM)
    scores = lax.dot_general(
        query, key, (((1,), (1,)), ((), ())), preferred_element_type=jnp.float32
    ) * (1.0 / float(HDIM) ** 0.5)
    key_cols = kc_ref[...]
    allowed = (key_cols >= lo_ref[0]) & (key_cols <= hi_ref[0]) & (km_ref[0, 0] > 0.0)
    terms = jnp.where(allowed, jnp.exp(scores), jnp.float32(0.0))
    total = jnp.sum(terms, axis=-1, keepdims=True)
    seen = qv_ref[0] > 0.0
    total = jnp.where(seen, total, jnp.float32(1.0))
    weights = (terms * (1.0 / total)).astype(jnp.bfloat16)
    result = jnp.dot(weights, value, preferred_element_type=jnp.float32)
    result = jnp.where(seen, result, jnp.float32(0.0)).astype(jnp.bfloat16)
    o_ref[0] = result.reshape(TH, width, HDIM)


ROW_TILES = 2


def tile_attention(query, extended, key_mask, query_lo, query_hi, key_cols, query_ok, group, out):
    frames, rows, width, inner = query.shape
    heads = extended.shape[-1] // HDIM
    first = group * heads
    row_tiles = rows // TH
    assert row_tiles == ROW_TILES
    blocks = frames * row_tiles
    _, frames_ext, rows_ext, _, _ = extended.shape
    key_n = key_mask.shape[-1]
    query_n = TH * width
    q_spec = pl.BlockSpec(
        (1, TH, width, HDIM), lambda h, b: (b // row_tiles, b % row_tiles, 0, first + h)
    )
    in_specs = [
        q_spec,
        pl.BlockSpec((1, frames_ext, rows_ext, width, HDIM), lambda h, b: (0, 0, 0, 0, h)),
        pl.BlockSpec((1, frames_ext, rows_ext, width, HDIM), lambda h, b: (1, 0, 0, 0, h)),
        pl.BlockSpec((1, 1, 1, key_n), lambda h, b: (first + h, b, 0, 0)),
        pl.BlockSpec((1, query_n, 1), lambda h, b: (first + h, 0, 0)),
        pl.BlockSpec((1, query_n, 1), lambda h, b: (first + h, 0, 0)),
        pl.BlockSpec((1, key_n), lambda h, b: (0, 0)),
        pl.BlockSpec((1, query_n, 1), lambda h, b: (b, 0, 0)),
    ]
    operands = [query, extended, extended, key_mask, query_lo, query_hi, key_cols, query_ok]
    aliases = {}
    kernel = attention_kernel
    if out is not None:
        in_specs.append(pl.BlockSpec(memory_space=pl.ANY))
        operands.append(out)
        aliases = {len(operands) - 1: 0}
        kernel = lambda *refs: attention_kernel(*refs[:8], refs[9])
    return pl.pallas_call(
        kernel,
        grid=(heads, blocks),
        in_specs=in_specs,
        out_specs=q_spec,
        out_shape=jax.ShapeDtypeStruct(query.shape, jnp.bfloat16),
        input_output_aliases=aliases,
    )(*operands)


PROJECT_COLS = 256
TOKEN_BLOCK = 640


def projection_kernel(x_ref, w_ref, g_ref, o_ref, *, normalize):
    acc = jnp.dot(x_ref[...], w_ref[...], preferred_element_type=jnp.float32)
    for part in range(acc.shape[1] // HDIM):
        piece = acc[:, part * HDIM : (part + 1) * HDIM]
        if normalize:
            power = jnp.mean(piece * piece, axis=-1, keepdims=True)
            piece = piece * lax.rsqrt(power + EPS) * g_ref[...]
        o_ref[:, part * HDIM : (part + 1) * HDIM] = piece.astype(o_ref.dtype)


def project(x, w, start, count, gain):
    tokens, features = x.shape
    cols = PROJECT_COLS
    normalize = gain is not None
    gain = gain.reshape(1, HDIM) if normalize else jnp.ones((1, HDIM), jnp.float32)
    first = start // cols
    return pl.pallas_call(
        functools.partial(projection_kernel, normalize=normalize),
        grid=(count // cols,),
        in_specs=[
            pl.BlockSpec((tokens, features), lambda j: (0, 0)),
            pl.BlockSpec((features, cols), lambda j: (0, first + j)),
            pl.BlockSpec((1, HDIM), lambda j: (0, 0)),
        ],
        out_specs=pl.BlockSpec((tokens, cols), lambda j: (0, j)),
        out_shape=jax.ShapeDtypeStruct((tokens, count), jnp.bfloat16),
    )(x, w, gain)


MESH = pl.DeviceIdType.MESH


def band_gather_kernel(w_ref, out_ref, local_sem, send_sem, recv_sem):
    count = lax.axis_size("height")
    me = lax.axis_index("height")
    frame_block = lax.axis_index("tm")
    barrier = pltpu.get_barrier_semaphore()
    for step in range(1, count):
        peer = lax.rem(me + step, count)
        pl.semaphore_signal(barrier, inc=1, device_id=(frame_block, peer), device_id_type=MESH)
    pl.semaphore_wait(barrier, count - 1)
    own = pltpu.make_async_copy(w_ref, out_ref.at[me], local_sem)
    own.start()
    copies = []
    for step in range(1, count):
        peer = lax.rem(me + step, count)
        copy = pltpu.make_async_remote_copy(
            src_ref=w_ref,
            dst_ref=out_ref.at[me],
            send_sem=send_sem.at[step],
            recv_sem=recv_sem.at[me],
            device_id=(frame_block, peer),
            device_id_type=MESH,
        )
        copy.start()
        copies.append(copy)
    for copy in copies:
        copy.wait_send()
    for step in range(1, count):
        source = lax.rem(me + count - step, count)
        incoming = pltpu.make_async_remote_copy(
            src_ref=w_ref,
            dst_ref=out_ref.at[source],
            send_sem=send_sem.at[step],
            recv_sem=recv_sem.at[source],
            device_id=(frame_block, source),
            device_id_type=MESH,
        )
        incoming.wait_recv()
    own.wait()


def band_gather(w):
    rows, cols = w.shape
    count = lax.axis_size("height")
    gathered = pl.pallas_call(
        band_gather_kernel,
        in_specs=[pl.BlockSpec(memory_space=pl.ANY)],
        out_specs=pl.BlockSpec(memory_space=pl.ANY),
        out_shape=jax.ShapeDtypeStruct((count, rows, cols), w.dtype),
        scratch_shapes=[
            pltpu.SemaphoreType.DMA(()),
            pltpu.SemaphoreType.DMA((count,)),
            pltpu.SemaphoreType.DMA((count,)),
        ],
        compiler_params=pltpu.CompilerParams(collective_id=0, has_side_effects=True),
    )(w)
    return gathered.reshape(count * rows, cols)


def projection_kv_kernel(x_ref, w_ref, g_ref, o_ref):
    acc = jnp.dot(x_ref[...], w_ref[...], preferred_element_type=jnp.float32)
    is_key = pl.program_id(1) < pl.num_programs(1) // 2
    for part in range(acc.shape[1] // HDIM):
        piece = acc[:, part * HDIM : (part + 1) * HDIM]
        power = jnp.mean(piece * piece, axis=-1, keepdims=True)
        scale = jnp.where(is_key, lax.rsqrt(power + EPS), jnp.float32(1.0))
        gain = jnp.where(is_key, g_ref[...], jnp.float32(1.0))
        normed = jnp.where(is_key, piece * scale * gain, piece)
        o_ref[0, :, part * HDIM : (part + 1) * HDIM] = normed.astype(o_ref.dtype)


def project_kv(x, w, start, count, gain):
    tokens, features = x.shape
    cols = PROJECT_COLS
    inner = w.shape[1] // 3
    steps = count // cols
    key_first = (inner + start) // cols
    value_first = (2 * inner + start) // cols

    def weight_block(j):
        return (0, jnp.where(j < steps, key_first + j, value_first + j - steps))

    block = TOKEN_BLOCK
    return pl.pallas_call(
        projection_kv_kernel,
        grid=(tokens // block, 2 * steps),
        in_specs=[
            pl.BlockSpec((block, features), lambda t, j: (t, 0)),
            pl.BlockSpec((features, cols), lambda t, j: weight_block(j)),
            pl.BlockSpec((1, HDIM), lambda t, j: (0, 0)),
        ],
        out_specs=pl.BlockSpec((1, block, cols), lambda t, j: (j // steps, t, j % steps)),
        out_shape=jax.ShapeDtypeStruct((2, tokens, count), jnp.bfloat16),
    )(x, w, gain.reshape(1, HDIM))


def solution(mesh):
    in_specs = (
        P("tm", "height", None, None),
        P(),
        P(),
        P(("tm", "height"), None),
        P(),
        P(),
        P(),
        P(),
    )
    out_specs = P("tm", "height", None, None)
    return jax.shard_map(
        per_device, mesh=mesh, in_specs=in_specs, out_specs=out_specs, check_vma=False
    )
```

```python
import functools

import jax
import jax.numpy as jnp
from jax import lax
from jax.sharding import PartitionSpec as P
from jax.experimental import pallas as pl
from jax.experimental.pallas import tpu as pltpu

HDIM = 128
HEADS = 12
TT = 1
TH = 2
TW = 8
GROUPS = 2


EPS = 1e-06


def with_halo(cells, sides, width):
    for axis, dim in sides:
        count = lax.axis_size(axis)
        ends = count - 1
        head = lax.slice_in_dim(cells, 0, width, axis=dim)
        tail = lax.slice_in_dim(cells, cells.shape[dim] - width, cells.shape[dim], axis=dim)
        cells = jnp.concatenate(
            [
                lax.ppermute(tail, axis, [(i, (i + 1) % count) for i in range(ends)]),
                cells,
                lax.ppermute(head, axis, [((i + 1) % count, i) for i in range(ends)]),
            ],
            axis=dim,
        )
    return cells


def modulate(tokens, mod_scale, mod_shift):
    values = tokens.astype(jnp.float32)
    mean = jnp.mean(values, axis=-1, keepdims=True)
    centred = values - mean
    variance = jnp.mean(centred * centred, axis=-1, keepdims=True)
    normed = centred * lax.rsqrt(variance + EPS)
    return (normed * (1.0 + mod_scale) + mod_shift).astype(jnp.bfloat16)


def head_norm(values, gain):
    power = jnp.mean(values * values, axis=-1, keepdims=True)
    return (values * lax.rsqrt(power + EPS) * gain).astype(jnp.bfloat16)


def tile_coords(frames, rows, width):
    shape = (frames.shape[0], rows.shape[0], width)
    columns = jnp.arange(width, dtype=jnp.int32)
    frame_tiles = jnp.broadcast_to((frames // TT)[:, None, None], shape).reshape(-1)
    row_tiles = jnp.broadcast_to((rows // TH)[None, :, None], shape).reshape(-1)
    column_tiles = jnp.broadcast_to((columns // TW)[None, None, :], shape).reshape(-1)
    return (frame_tiles, row_tiles, column_tiles)


def per_device(tokens, mod_scale, mod_shift, w_qkv, q_gain, k_gain, window, valid):
    frame_count, row_count, width, features = tokens.shape
    token_count = frame_count * row_count * width
    modulated = modulate(tokens.reshape(token_count, features), mod_scale, mod_shift)
    band_weight = band_gather(w_qkv)
    full_weight = lax.all_gather(band_weight, "tm", axis=0, tiled=True)
    inner = full_weight.shape[1] // 3
    group_cols = inner // GROUPS
    tiled = (frame_count // TT, TT, row_count // TH, TH, width, group_cols)
    groups = []
    for group in range(GROUPS):
        start = group * group_cols
        stacked = project_kv(modulated, full_weight, start, group_cols, k_gain)
        stacked = stacked.reshape(2, *tiled)
        groups.append(with_halo(stacked, (("tm", 1), ("height", 3)), 1))
    query = project(modulated, full_weight, 0, inner, q_gain)
    frames_ext = frame_count + 2 * TT
    rows_ext = row_count + 2 * TH
    groups = [g.reshape(2, frames_ext, rows_ext, width, group_cols) for g in groups]
    frame_block = lax.axis_index("tm")
    row_block = lax.axis_index("height")
    first_frame = frame_block * frame_count
    first_row = row_block * row_count
    zero = jnp.int32(0)
    valid_pad = jnp.pad(valid, ((TT, TT), (TH, TH), (0, 0)))
    key_valid = lax.dynamic_slice(
        valid_pad, (first_frame, first_row, zero), (frames_ext, rows_ext, width)
    )
    query_valid = lax.dynamic_slice(
        valid, (first_frame, first_row, zero), (frame_count, row_count, width)
    )
    row_tiles = row_count // TH
    blocks = frame_count * row_tiles
    span_t = 2 * TT + 1
    span_h = 3 * TH
    query_n = TH * width
    key_n = span_t * span_h * width
    block_valid = jnp.stack(
        [
            key_valid[f : f + span_t, TH * rt : TH * rt + span_h].reshape(-1)
            for f in range(frame_count)
            for rt in range(row_tiles)
        ]
    )
    apart_t = jnp.abs(jnp.arange(span_t, dtype=jnp.int32) - TT)
    apart_h = jnp.abs(jnp.arange(span_h, dtype=jnp.int32) // TH - 1)
    near = (apart_t[None, :, None, None] <= window[:, 0, None, None, None]) & (
        apart_h[None, None, :, None] <= window[:, 1, None, None, None]
    )
    near = jnp.broadcast_to(near, (HEADS, span_t, span_h, width)).reshape(HEADS, 1, key_n)
    key_mask = (near & (block_valid[None] > 0)).astype(jnp.float32).reshape(HEADS, blocks, 1, key_n)
    column_tiles = jnp.arange(width, dtype=jnp.int32) // TW
    key_cols = jnp.tile(column_tiles, span_t * span_h).reshape(1, key_n)
    query_cols = jnp.tile(column_tiles, TH)
    query_lo = (query_cols[None, :] - window[:, 2, None]).reshape(HEADS, query_n, 1)
    query_hi = (query_cols[None, :] + window[:, 2, None]).reshape(HEADS, query_n, 1)
    query_ok = query_valid.reshape(blocks, query_n, 1).astype(jnp.float32)
    query_grid = query.reshape(frame_count, row_count, width, inner)
    out = None
    for group, extended in enumerate(groups):
        out = tile_attention(
            query_grid, extended, key_mask, query_lo, query_hi, key_cols, query_ok, group, out
        )
    return out


def attention_kernel(q_ref, k_ref, v_ref, km_ref, lo_ref, hi_ref, kc_ref, qv_ref, o_ref):
    frame = pl.program_id(1)
    span_t = 2 * TT + 1
    span_h = 3 * TH
    width = q_ref.shape[2]
    key_cols = kc_ref[...]
    width_ok = (key_cols >= lo_ref[0]) & (key_cols <= hi_ref[0])
    for tile in range(ROW_TILES):
        row = tile * TH
        query = q_ref[0, row : row + TH].reshape(TH * width, HDIM)
        key = k_ref[0, pl.ds(frame, span_t), row : row + span_h].reshape(-1, HDIM)
        value = v_ref[0, pl.ds(frame, span_t), row : row + span_h].reshape(-1, HDIM)
        scores = lax.dot_general(
            query, key, (((1,), (1,)), ((), ())), preferred_element_type=jnp.float32
        ) * (1.0 / float(HDIM) ** 0.5)
        allowed = width_ok & (km_ref[0, tile] > 0.0)
        terms = jnp.where(allowed, jnp.exp(scores), jnp.float32(0.0))
        total = jnp.sum(terms, axis=-1, keepdims=True)
        seen = qv_ref[tile] > 0.0
        total = jnp.where(seen, total, jnp.float32(1.0))
        weights = (terms * (1.0 / total)).astype(jnp.bfloat16)
        result = jnp.dot(weights, value, preferred_element_type=jnp.float32)
        result = jnp.where(seen, result, jnp.float32(0.0)).astype(jnp.bfloat16)
        o_ref[0, row : row + TH] = result.reshape(TH, width, HDIM)


ROW_TILES = 2


def tile_attention(query, extended, key_mask, query_lo, query_hi, key_cols, query_ok, group, out):
    frames, rows, width, inner = query.shape
    heads = extended.shape[-1] // HDIM
    first = group * heads
    row_tiles = rows // TH
    assert row_tiles == ROW_TILES
    blocks = frames * row_tiles
    _, frames_ext, rows_ext, _, _ = extended.shape
    key_n = key_mask.shape[-1]
    query_n = TH * width
    q_spec = pl.BlockSpec((1, rows, width, HDIM), lambda h, f: (f, 0, 0, first + h))
    in_specs = [
        q_spec,
        pl.BlockSpec((1, frames_ext, rows_ext, width, HDIM), lambda h, b: (0, 0, 0, 0, h)),
        pl.BlockSpec((1, frames_ext, rows_ext, width, HDIM), lambda h, b: (1, 0, 0, 0, h)),
        pl.BlockSpec((1, row_tiles, 1, key_n), lambda h, f: (first + h, f, 0, 0)),
        pl.BlockSpec((1, query_n, 1), lambda h, b: (first + h, 0, 0)),
        pl.BlockSpec((1, query_n, 1), lambda h, b: (first + h, 0, 0)),
        pl.BlockSpec((1, key_n), lambda h, b: (0, 0)),
        pl.BlockSpec((row_tiles, query_n, 1), lambda h, f: (f, 0, 0)),
    ]
    operands = [query, extended, extended, key_mask, query_lo, query_hi, key_cols, query_ok]
    aliases = {}
    kernel = attention_kernel
    if out is not None:
        in_specs.append(pl.BlockSpec(memory_space=pl.ANY))
        operands.append(out)
        aliases = {len(operands) - 1: 0}
        kernel = lambda *refs: attention_kernel(*refs[:8], refs[9])
    return pl.pallas_call(
        kernel,
        grid=(heads, frames),
        in_specs=in_specs,
        out_specs=q_spec,
        out_shape=jax.ShapeDtypeStruct(query.shape, jnp.bfloat16),
        input_output_aliases=aliases,
    )(*operands)


PROJECT_COLS = 256


def projection_kernel(x_ref, w_ref, g_ref, o_ref, *, normalize):
    acc = jnp.dot(x_ref[...], w_ref[...], preferred_element_type=jnp.float32)
    for part in range(acc.shape[1] // HDIM):
        piece = acc[:, part * HDIM : (part + 1) * HDIM]
        if normalize:
            power = jnp.mean(piece * piece, axis=-1, keepdims=True)
            piece = piece * lax.rsqrt(power + EPS) * g_ref[...]
        o_ref[:, part * HDIM : (part + 1) * HDIM] = piece.astype(o_ref.dtype)


def project(x, w, start, count, gain):
    tokens, features = x.shape
    cols = PROJECT_COLS
    normalize = gain is not None
    gain = gain.reshape(1, HDIM) if normalize else jnp.ones((1, HDIM), jnp.float32)
    first = start // cols
    return pl.pallas_call(
        functools.partial(projection_kernel, normalize=normalize),
        grid=(count // cols,),
        in_specs=[
            pl.BlockSpec((tokens, features), lambda j: (0, 0)),
            pl.BlockSpec((features, cols), lambda j: (0, first + j)),
            pl.BlockSpec((1, HDIM), lambda j: (0, 0)),
        ],
        out_specs=pl.BlockSpec((tokens, cols), lambda j: (0, j)),
        out_shape=jax.ShapeDtypeStruct((tokens, count), jnp.bfloat16),
    )(x, w, gain)


MESH = pl.DeviceIdType.MESH


def band_gather_kernel(w_ref, out_ref, local_sem, send_sem, recv_sem):
    count = lax.axis_size("height")
    me = lax.axis_index("height")
    frame_block = lax.axis_index("tm")
    barrier = pltpu.get_barrier_semaphore()
    for step in range(1, count):
        peer = lax.rem(me + step, count)
        pl.semaphore_signal(barrier, inc=1, device_id=(frame_block, peer), device_id_type=MESH)
    pl.semaphore_wait(barrier, count - 1)
    own = pltpu.make_async_copy(w_ref, out_ref.at[me], local_sem)
    own.start()
    copies = []
    for step in range(1, count):
        peer = lax.rem(me + step, count)
        copy = pltpu.make_async_remote_copy(
            src_ref=w_ref,
            dst_ref=out_ref.at[me],
            send_sem=send_sem.at[step],
            recv_sem=recv_sem.at[me],
            device_id=(frame_block, peer),
            device_id_type=MESH,
        )
        copy.start()
        copies.append(copy)
    for copy in copies:
        copy.wait_send()
    for step in range(1, count):
        source = lax.rem(me + count - step, count)
        incoming = pltpu.make_async_remote_copy(
            src_ref=w_ref,
            dst_ref=out_ref.at[source],
            send_sem=send_sem.at[step],
            recv_sem=recv_sem.at[source],
            device_id=(frame_block, source),
            device_id_type=MESH,
        )
        incoming.wait_recv()
    own.wait()


def band_gather(w):
    rows, cols = w.shape
    count = lax.axis_size("height")
    gathered = pl.pallas_call(
        band_gather_kernel,
        in_specs=[pl.BlockSpec(memory_space=pl.ANY)],
        out_specs=pl.BlockSpec(memory_space=pl.ANY),
        out_shape=jax.ShapeDtypeStruct((count, rows, cols), w.dtype),
        scratch_shapes=[
            pltpu.SemaphoreType.DMA(()),
            pltpu.SemaphoreType.DMA((count,)),
            pltpu.SemaphoreType.DMA((count,)),
        ],
        compiler_params=pltpu.CompilerParams(collective_id=0, has_side_effects=True),
    )(w)
    return gathered.reshape(count * rows, cols)


def projection_kv_kernel(x_ref, w_ref, g_ref, o_ref):
    acc = jnp.dot(x_ref[...], w_ref[...], preferred_element_type=jnp.float32)
    is_key = pl.program_id(0) < pl.num_programs(0) // 2
    for part in range(acc.shape[1] // HDIM):
        piece = acc[:, part * HDIM : (part + 1) * HDIM]
        power = jnp.mean(piece * piece, axis=-1, keepdims=True)
        scale = jnp.where(is_key, lax.rsqrt(power + EPS), jnp.float32(1.0))
        gain = jnp.where(is_key, g_ref[...], jnp.float32(1.0))
        normed = jnp.where(is_key, piece * scale * gain, piece)
        o_ref[0, :, part * HDIM : (part + 1) * HDIM] = normed.astype(o_ref.dtype)


def project_kv(x, w, start, count, gain):
    tokens, features = x.shape
    cols = PROJECT_COLS
    inner = w.shape[1] // 3
    steps = count // cols
    key_first = (inner + start) // cols
    value_first = (2 * inner + start) // cols

    def weight_block(j):
        return (0, jnp.where(j < steps, key_first + j, value_first + j - steps))

    return pl.pallas_call(
        projection_kv_kernel,
        grid=(2 * steps,),
        in_specs=[
            pl.BlockSpec((tokens, features), lambda j: (0, 0)),
            pl.BlockSpec((features, cols), weight_block),
            pl.BlockSpec((1, HDIM), lambda j: (0, 0)),
        ],
        out_specs=pl.BlockSpec((1, tokens, cols), lambda j: (j // steps, 0, j % steps)),
        out_shape=jax.ShapeDtypeStruct((2, tokens, count), jnp.bfloat16),
    )(x, w, gain.reshape(1, HDIM))


def solution(mesh):
    in_specs = (
        P("tm", "height", None, None),
        P(),
        P(),
        P(("tm", "height"), None),
        P(),
        P(),
        P(),
        P(),
    )
    out_specs = P("tm", "height", None, None)
    return jax.shard_map(
        per_device, mesh=mesh, in_specs=in_specs, out_specs=out_specs, check_vma=False
    )
```

```python
import functools

import jax
import jax.numpy as jnp
from jax import lax
from jax.sharding import PartitionSpec as P
from jax.experimental import pallas as pl
from jax.experimental.pallas import tpu as pltpu

HDIM = 128
HEADS = 12
TT = 1
TH = 2
TW = 8
GROUPS = 2


EPS = 1e-06


def with_halo(cells, sides, width):
    for axis, dim in sides:
        count = lax.axis_size(axis)
        ends = count - 1
        head = lax.slice_in_dim(cells, 0, width, axis=dim)
        tail = lax.slice_in_dim(cells, cells.shape[dim] - width, cells.shape[dim], axis=dim)
        cells = jnp.concatenate(
            [
                lax.ppermute(tail, axis, [(i, (i + 1) % count) for i in range(ends)]),
                cells,
                lax.ppermute(head, axis, [((i + 1) % count, i) for i in range(ends)]),
            ],
            axis=dim,
        )
    return cells


def modulate(tokens, mod_scale, mod_shift):
    values = tokens.astype(jnp.float32)
    mean = jnp.mean(values, axis=-1, keepdims=True)
    centred = values - mean
    variance = jnp.mean(centred * centred, axis=-1, keepdims=True)
    normed = centred * lax.rsqrt(variance + EPS)
    return (normed * (1.0 + mod_scale) + mod_shift).astype(jnp.bfloat16)


def head_norm(values, gain):
    power = jnp.mean(values * values, axis=-1, keepdims=True)
    return (values * lax.rsqrt(power + EPS) * gain).astype(jnp.bfloat16)


def tile_coords(frames, rows, width):
    shape = (frames.shape[0], rows.shape[0], width)
    columns = jnp.arange(width, dtype=jnp.int32)
    frame_tiles = jnp.broadcast_to((frames // TT)[:, None, None], shape).reshape(-1)
    row_tiles = jnp.broadcast_to((rows // TH)[None, :, None], shape).reshape(-1)
    column_tiles = jnp.broadcast_to((columns // TW)[None, None, :], shape).reshape(-1)
    return (frame_tiles, row_tiles, column_tiles)


def per_device(tokens, mod_scale, mod_shift, w_qkv, q_gain, k_gain, window, valid):
    frame_count, row_count, width, features = tokens.shape
    token_count = frame_count * row_count * width
    modulated = modulate(tokens.reshape(token_count, features), mod_scale, mod_shift)
    band_weight = band_gather(w_qkv)
    full_weight = lax.all_gather(band_weight, "tm", axis=0, tiled=True)
    inner = full_weight.shape[1] // 3
    group_cols = inner // GROUPS
    tiled = (frame_count // TT, TT, row_count // TH, TH, width, group_cols)
    groups = []
    for group in range(GROUPS):
        start = group * group_cols
        stacked = project_kv(modulated, full_weight, start, group_cols, k_gain)
        stacked = stacked.reshape(2, *tiled)
        groups.append(with_halo(stacked, (("tm", 1), ("height", 3)), 1))
    query = project(modulated, full_weight, 0, inner, q_gain)
    frames_ext = frame_count + 2 * TT
    rows_ext = row_count + 2 * TH
    groups = [g.reshape(2, frames_ext, rows_ext, width, group_cols) for g in groups]
    frame_block = lax.axis_index("tm")
    row_block = lax.axis_index("height")
    first_frame = frame_block * frame_count
    first_row = row_block * row_count
    zero = jnp.int32(0)
    valid_pad = jnp.pad(valid, ((TT, TT), (TH, TH), (0, 0)))
    key_valid = lax.dynamic_slice(
        valid_pad, (first_frame, first_row, zero), (frames_ext, rows_ext, width)
    )
    query_valid = lax.dynamic_slice(
        valid, (first_frame, first_row, zero), (frame_count, row_count, width)
    )
    row_tiles = row_count // TH
    blocks = frame_count * row_tiles
    span_t = 2 * TT + 1
    span_h = 3 * TH
    query_n = TH * width
    key_n = span_t * span_h * width
    block_valid = jnp.stack(
        [
            key_valid[f : f + span_t, TH * rt : TH * rt + span_h].reshape(-1)
            for f in range(frame_count)
            for rt in range(row_tiles)
        ]
    )
    apart_t = jnp.abs(jnp.arange(span_t, dtype=jnp.int32) - TT)
    apart_h = jnp.abs(jnp.arange(span_h, dtype=jnp.int32) // TH - 1)
    near = (apart_t[None, :, None, None] <= window[:, 0, None, None, None]) & (
        apart_h[None, None, :, None] <= window[:, 1, None, None, None]
    )
    near = jnp.broadcast_to(near, (HEADS, span_t, span_h, width)).reshape(HEADS, 1, key_n)
    key_mask = (near & (block_valid[None] > 0)).astype(jnp.float32).reshape(HEADS, blocks, 1, key_n)
    column_tiles = jnp.arange(width, dtype=jnp.int32) // TW
    key_cols = jnp.tile(column_tiles, span_t * span_h).reshape(1, key_n)
    query_cols = jnp.tile(column_tiles, TH)
    query_lo = (query_cols[None, :] - window[:, 2, None]).reshape(HEADS, query_n, 1)
    query_hi = (query_cols[None, :] + window[:, 2, None]).reshape(HEADS, query_n, 1)
    query_ok = query_valid.reshape(blocks, query_n, 1).astype(jnp.float32)
    query_grid = query.reshape(frame_count, row_count, width, inner)
    out = None
    for group, extended in enumerate(groups):
        out = tile_attention(
            query_grid, extended, key_mask, query_lo, query_hi, key_cols, query_ok, group, out
        )
    return out


def attention_kernel(q_ref, k_ref, v_ref, km_ref, lo_ref, hi_ref, kc_ref, qv_ref, o_ref):
    span_t = 2 * TT + 1
    span_h = 3 * TH
    width = q_ref.shape[2]
    key_cols = kc_ref[...]
    width_ok = (key_cols >= lo_ref[0]) & (key_cols <= hi_ref[0])
    for block in range(q_ref.shape[0] * ROW_TILES):
        frame, tile = divmod(block, ROW_TILES)
        row = tile * TH
        query = q_ref[frame, row : row + TH].reshape(TH * width, HDIM)
        key = k_ref[0, frame : frame + span_t, row : row + span_h].reshape(-1, HDIM)
        value = v_ref[0, frame : frame + span_t, row : row + span_h].reshape(-1, HDIM)
        scores = lax.dot_general(
            query, key, (((1,), (1,)), ((), ())), preferred_element_type=jnp.float32
        ) * (1.0 / float(HDIM) ** 0.5)
        allowed = width_ok & (km_ref[0, block] > 0.0)
        terms = jnp.where(allowed, jnp.exp(scores), jnp.float32(0.0))
        total = jnp.sum(terms, axis=-1, keepdims=True)
        seen = qv_ref[block] > 0.0
        total = jnp.where(seen, total, jnp.float32(1.0))
        weights = (terms * (1.0 / total)).astype(jnp.bfloat16)
        result = jnp.dot(weights, value, preferred_element_type=jnp.float32)
        result = jnp.where(seen, result, jnp.float32(0.0)).astype(jnp.bfloat16)
        o_ref[frame, row : row + TH] = result.reshape(TH, width, HDIM)


ROW_TILES = 2


def tile_attention(query, extended, key_mask, query_lo, query_hi, key_cols, query_ok, group, out):
    frames, rows, width, inner = query.shape
    heads = extended.shape[-1] // HDIM
    first = group * heads
    row_tiles = rows // TH
    assert row_tiles == ROW_TILES
    blocks = frames * row_tiles
    _, frames_ext, rows_ext, _, _ = extended.shape
    key_n = key_mask.shape[-1]
    query_n = TH * width
    q_spec = pl.BlockSpec((frames, rows, width, HDIM), lambda h: (0, 0, 0, first + h))
    in_specs = [
        q_spec,
        pl.BlockSpec((1, frames_ext, rows_ext, width, HDIM), lambda h: (0, 0, 0, 0, h)),
        pl.BlockSpec((1, frames_ext, rows_ext, width, HDIM), lambda h: (1, 0, 0, 0, h)),
        pl.BlockSpec((1, blocks, 1, key_n), lambda h: (first + h, 0, 0, 0)),
        pl.BlockSpec((1, query_n, 1), lambda h: (first + h, 0, 0)),
        pl.BlockSpec((1, query_n, 1), lambda h: (first + h, 0, 0)),
        pl.BlockSpec((1, key_n), lambda h: (0, 0)),
        pl.BlockSpec((blocks, query_n, 1), lambda h: (0, 0, 0)),
    ]
    operands = [query, extended, extended, key_mask, query_lo, query_hi, key_cols, query_ok]
    aliases = {}
    kernel = attention_kernel
    if out is not None:
        in_specs.append(pl.BlockSpec(memory_space=pl.ANY))
        operands.append(out)
        aliases = {len(operands) - 1: 0}
        kernel = lambda *refs: attention_kernel(*refs[:8], refs[9])
    return pl.pallas_call(
        kernel,
        grid=(heads,),
        in_specs=in_specs,
        out_specs=q_spec,
        out_shape=jax.ShapeDtypeStruct(query.shape, jnp.bfloat16),
        input_output_aliases=aliases,
    )(*operands)


PROJECT_COLS = 256


def projection_kernel(x_ref, w_ref, g_ref, o_ref, *, normalize):
    acc = jnp.dot(x_ref[...], w_ref[...], preferred_element_type=jnp.float32)
    for part in range(acc.shape[1] // HDIM):
        piece = acc[:, part * HDIM : (part + 1) * HDIM]
        if normalize:
            power = jnp.mean(piece * piece, axis=-1, keepdims=True)
            piece = piece * lax.rsqrt(power + EPS) * g_ref[...]
        o_ref[:, part * HDIM : (part + 1) * HDIM] = piece.astype(o_ref.dtype)


def project(x, w, start, count, gain):
    tokens, features = x.shape
    cols = PROJECT_COLS
    normalize = gain is not None
    gain = gain.reshape(1, HDIM) if normalize else jnp.ones((1, HDIM), jnp.float32)
    first = start // cols
    return pl.pallas_call(
        functools.partial(projection_kernel, normalize=normalize),
        grid=(count // cols,),
        in_specs=[
            pl.BlockSpec((tokens, features), lambda j: (0, 0)),
            pl.BlockSpec((features, cols), lambda j: (0, first + j)),
            pl.BlockSpec((1, HDIM), lambda j: (0, 0)),
        ],
        out_specs=pl.BlockSpec((tokens, cols), lambda j: (0, j)),
        out_shape=jax.ShapeDtypeStruct((tokens, count), jnp.bfloat16),
    )(x, w, gain)


MESH = pl.DeviceIdType.MESH


def band_gather_kernel(w_ref, out_ref, local_sem, send_sem, recv_sem):
    count = lax.axis_size("height")
    me = lax.axis_index("height")
    frame_block = lax.axis_index("tm")
    barrier = pltpu.get_barrier_semaphore()
    for step in range(1, count):
        peer = lax.rem(me + step, count)
        pl.semaphore_signal(barrier, inc=1, device_id=(frame_block, peer), device_id_type=MESH)
    pl.semaphore_wait(barrier, count - 1)
    own = pltpu.make_async_copy(w_ref, out_ref.at[me], local_sem)
    own.start()
    copies = []
    for step in range(1, count):
        peer = lax.rem(me + step, count)
        copy = pltpu.make_async_remote_copy(
            src_ref=w_ref,
            dst_ref=out_ref.at[me],
            send_sem=send_sem.at[step],
            recv_sem=recv_sem.at[me],
            device_id=(frame_block, peer),
            device_id_type=MESH,
        )
        copy.start()
        copies.append(copy)
    for copy in copies:
        copy.wait_send()
    for step in range(1, count):
        source = lax.rem(me + count - step, count)
        incoming = pltpu.make_async_remote_copy(
            src_ref=w_ref,
            dst_ref=out_ref.at[source],
            send_sem=send_sem.at[step],
            recv_sem=recv_sem.at[source],
            device_id=(frame_block, source),
            device_id_type=MESH,
        )
        incoming.wait_recv()
    own.wait()


def band_gather(w):
    rows, cols = w.shape
    count = lax.axis_size("height")
    gathered = pl.pallas_call(
        band_gather_kernel,
        in_specs=[pl.BlockSpec(memory_space=pl.ANY)],
        out_specs=pl.BlockSpec(memory_space=pl.ANY),
        out_shape=jax.ShapeDtypeStruct((count, rows, cols), w.dtype),
        scratch_shapes=[
            pltpu.SemaphoreType.DMA(()),
            pltpu.SemaphoreType.DMA((count,)),
            pltpu.SemaphoreType.DMA((count,)),
        ],
        compiler_params=pltpu.CompilerParams(collective_id=0, has_side_effects=True),
    )(w)
    return gathered.reshape(count * rows, cols)


def projection_kv_kernel(x_ref, w_ref, g_ref, o_ref):
    acc = jnp.dot(x_ref[...], w_ref[...], preferred_element_type=jnp.float32)
    is_key = pl.program_id(0) < pl.num_programs(0) // 2
    for part in range(acc.shape[1] // HDIM):
        piece = acc[:, part * HDIM : (part + 1) * HDIM]
        power = jnp.mean(piece * piece, axis=-1, keepdims=True)
        scale = jnp.where(is_key, lax.rsqrt(power + EPS), jnp.float32(1.0))
        gain = jnp.where(is_key, g_ref[...], jnp.float32(1.0))
        normed = jnp.where(is_key, piece * scale * gain, piece)
        o_ref[0, :, part * HDIM : (part + 1) * HDIM] = normed.astype(o_ref.dtype)


def project_kv(x, w, start, count, gain):
    tokens, features = x.shape
    cols = PROJECT_COLS
    inner = w.shape[1] // 3
    steps = count // cols
    key_first = (inner + start) // cols
    value_first = (2 * inner + start) // cols

    def weight_block(j):
        return (0, jnp.where(j < steps, key_first + j, value_first + j - steps))

    return pl.pallas_call(
        projection_kv_kernel,
        grid=(2 * steps,),
        in_specs=[
            pl.BlockSpec((tokens, features), lambda j: (0, 0)),
            pl.BlockSpec((features, cols), weight_block),
            pl.BlockSpec((1, HDIM), lambda j: (0, 0)),
        ],
        out_specs=pl.BlockSpec((1, tokens, cols), lambda j: (j // steps, 0, j % steps)),
        out_shape=jax.ShapeDtypeStruct((2, tokens, count), jnp.bfloat16),
    )(x, w, gain.reshape(1, HDIM))


def solution(mesh):
    in_specs = (
        P("tm", "height", None, None),
        P(),
        P(),
        P(("tm", "height"), None),
        P(),
        P(),
        P(),
        P(),
    )
    out_specs = P("tm", "height", None, None)
    return jax.shard_map(
        per_device, mesh=mesh, in_specs=in_specs, out_specs=out_specs, check_vma=False
    )
```

```python
import functools

import jax
import jax.numpy as jnp
from jax import lax
from jax.sharding import PartitionSpec as P
from jax.experimental import pallas as pl
from jax.experimental.pallas import tpu as pltpu

HDIM = 128
HEADS = 12
TT = 1
TH = 2
TW = 8
GROUPS = 2


EPS = 1e-06


def with_halo(cells, sides, width):
    for axis, dim in sides:
        count = lax.axis_size(axis)
        ends = count - 1
        head = lax.slice_in_dim(cells, 0, width, axis=dim)
        tail = lax.slice_in_dim(cells, cells.shape[dim] - width, cells.shape[dim], axis=dim)
        cells = jnp.concatenate(
            [
                lax.ppermute(tail, axis, [(i, (i + 1) % count) for i in range(ends)]),
                cells,
                lax.ppermute(head, axis, [((i + 1) % count, i) for i in range(ends)]),
            ],
            axis=dim,
        )
    return cells


def modulate(tokens, mod_scale, mod_shift):
    values = tokens.astype(jnp.float32)
    mean = jnp.mean(values, axis=-1, keepdims=True)
    centred = values - mean
    variance = jnp.mean(centred * centred, axis=-1, keepdims=True)
    normed = centred * lax.rsqrt(variance + EPS)
    return (normed * (1.0 + mod_scale) + mod_shift).astype(jnp.bfloat16)


def head_norm(values, gain):
    power = jnp.mean(values * values, axis=-1, keepdims=True)
    return (values * lax.rsqrt(power + EPS) * gain).astype(jnp.bfloat16)


def tile_coords(frames, rows, width):
    shape = (frames.shape[0], rows.shape[0], width)
    columns = jnp.arange(width, dtype=jnp.int32)
    frame_tiles = jnp.broadcast_to((frames // TT)[:, None, None], shape).reshape(-1)
    row_tiles = jnp.broadcast_to((rows // TH)[None, :, None], shape).reshape(-1)
    column_tiles = jnp.broadcast_to((columns // TW)[None, None, :], shape).reshape(-1)
    return (frame_tiles, row_tiles, column_tiles)


def per_device(tokens, mod_scale, mod_shift, w_qkv, q_gain, k_gain, window, valid):
    frame_count, row_count, width, features = tokens.shape
    token_count = frame_count * row_count * width
    modulated = modulate(tokens.reshape(token_count, features), mod_scale, mod_shift)
    band_weight = band_gather(w_qkv)
    full_weight = lax.all_gather(band_weight, "tm", axis=0, tiled=True)
    inner = full_weight.shape[1] // 3
    group_cols = inner // GROUPS
    tiled = (frame_count // TT, TT, row_count // TH, TH, width, group_cols)
    groups = []
    for group in range(GROUPS):
        start = group * group_cols
        stacked = project_kv(modulated, full_weight, start, group_cols, k_gain)
        stacked = stacked.reshape(2, *tiled)
        groups.append(with_halo(stacked, (("tm", 1), ("height", 3)), 1))
    query = project(modulated, full_weight, 0, inner, q_gain)
    frames_ext = frame_count + 2 * TT
    rows_ext = row_count + 2 * TH
    groups = [g.reshape(2, frames_ext, rows_ext, width, group_cols) for g in groups]
    frame_block = lax.axis_index("tm")
    row_block = lax.axis_index("height")
    first_frame = frame_block * frame_count
    first_row = row_block * row_count
    zero = jnp.int32(0)
    valid_pad = jnp.pad(valid, ((TT, TT), (TH, TH), (0, 0)))
    key_valid = lax.dynamic_slice(
        valid_pad, (first_frame, first_row, zero), (frames_ext, rows_ext, width)
    )
    query_valid = lax.dynamic_slice(
        valid, (first_frame, first_row, zero), (frame_count, row_count, width)
    )
    row_tiles = row_count // TH
    blocks = frame_count * row_tiles
    span_t = 2 * TT + 1
    span_h = 3 * TH
    query_n = TH * width
    key_n = span_t * span_h * width
    block_valid = jnp.stack(
        [
            key_valid[f : f + span_t, TH * rt : TH * rt + span_h].reshape(-1)
            for f in range(frame_count)
            for rt in range(row_tiles)
        ]
    )
    apart_t = jnp.abs(jnp.arange(span_t, dtype=jnp.int32) - TT)
    apart_h = jnp.abs(jnp.arange(span_h, dtype=jnp.int32) // TH - 1)
    near = (apart_t[None, :, None, None] <= window[:, 0, None, None, None]) & (
        apart_h[None, None, :, None] <= window[:, 1, None, None, None]
    )
    near = jnp.broadcast_to(near, (HEADS, span_t, span_h, width)).reshape(HEADS, 1, key_n)
    key_mask = (near & (block_valid[None] > 0)).astype(jnp.float32).reshape(HEADS, blocks, 1, key_n)
    column_tiles = jnp.arange(width, dtype=jnp.int32) // TW
    key_cols = jnp.tile(column_tiles, span_t * span_h).reshape(1, key_n)
    query_cols = jnp.tile(column_tiles, TH)
    query_lo = (query_cols[None, :] - window[:, 2, None]).reshape(HEADS, query_n, 1)
    query_hi = (query_cols[None, :] + window[:, 2, None]).reshape(HEADS, query_n, 1)
    query_ok = query_valid.reshape(blocks, query_n, 1).astype(jnp.float32)
    query_grid = query.reshape(frame_count, row_count, width, inner)
    out = None
    for group, extended in enumerate(groups):
        out = tile_attention(
            query_grid, extended, key_mask, query_lo, query_hi, key_cols, query_ok, group, out
        )
    return out


def attention_kernel(q_ref, k_ref, v_ref, km_ref, lo_ref, hi_ref, kc_ref, qv_ref, o_ref):
    span_t = 2 * TT + 1
    span_h = 3 * TH
    width = q_ref.shape[2]
    key_cols = kc_ref[...]
    width_ok = (key_cols >= lo_ref[0]) & (key_cols <= hi_ref[0])
    for block in range(q_ref.shape[0] * ROW_TILES):
        frame, tile = divmod(block, ROW_TILES)
        row = tile * TH
        query = q_ref[frame, row : row + TH].reshape(TH * width, HDIM)
        key = k_ref[0, frame : frame + span_t, row : row + span_h].reshape(-1, HDIM)
        value = v_ref[0, frame : frame + span_t, row : row + span_h].reshape(-1, HDIM)
        scores = lax.dot_general(
            query, key, (((1,), (1,)), ((), ())), preferred_element_type=jnp.float32
        ) * (1.0 / float(HDIM) ** 0.5)
        allowed = width_ok & (km_ref[0, block] > 0.0)
        terms = jnp.where(allowed, jnp.exp(scores), jnp.float32(0.0))
        total = jnp.sum(terms, axis=-1, keepdims=True)
        seen = qv_ref[block] > 0.0
        total = jnp.where(seen, total, jnp.float32(1.0))
        weights = (terms * (1.0 / total)).astype(jnp.bfloat16)
        result = jnp.dot(weights, value, preferred_element_type=jnp.float32)
        result = jnp.where(seen, result, jnp.float32(0.0)).astype(jnp.bfloat16)
        o_ref[frame, row : row + TH] = result.reshape(TH, width, HDIM)


ROW_TILES = 2


def tile_attention(query, extended, key_mask, query_lo, query_hi, key_cols, query_ok, group, out):
    frames, rows, width, inner = query.shape
    heads = extended.shape[-1] // HDIM
    first = group * heads
    row_tiles = rows // TH
    assert row_tiles == ROW_TILES
    blocks = frames * row_tiles
    _, frames_ext, rows_ext, _, _ = extended.shape
    key_n = key_mask.shape[-1]
    query_n = TH * width
    q_spec = pl.BlockSpec((frames, rows, width, HDIM), lambda h: (0, 0, 0, first + h))
    in_specs = [
        q_spec,
        pl.BlockSpec((1, frames_ext, rows_ext, width, HDIM), lambda h: (0, 0, 0, 0, h)),
        pl.BlockSpec((1, frames_ext, rows_ext, width, HDIM), lambda h: (1, 0, 0, 0, h)),
        pl.BlockSpec((1, blocks, 1, key_n), lambda h: (first + h, 0, 0, 0)),
        pl.BlockSpec((1, query_n, 1), lambda h: (first + h, 0, 0)),
        pl.BlockSpec((1, query_n, 1), lambda h: (first + h, 0, 0)),
        pl.BlockSpec((1, key_n), lambda h: (0, 0)),
        pl.BlockSpec((blocks, query_n, 1), lambda h: (0, 0, 0)),
    ]
    operands = [query, extended, extended, key_mask, query_lo, query_hi, key_cols, query_ok]
    aliases = {}
    kernel = attention_kernel
    if out is not None:
        in_specs.append(pl.BlockSpec(memory_space=pl.ANY))
        operands.append(out)
        aliases = {len(operands) - 1: 0}
        kernel = lambda *refs: attention_kernel(*refs[:8], refs[9])
    return pl.pallas_call(
        kernel,
        grid=(heads,),
        in_specs=in_specs,
        out_specs=q_spec,
        out_shape=jax.ShapeDtypeStruct(query.shape, jnp.bfloat16),
        input_output_aliases=aliases,
    )(*operands)


PROJECT_COLS = 768


def projection_kernel(x_ref, w_ref, g_ref, o_ref, *, normalize):
    acc = jnp.dot(x_ref[...], w_ref[...], preferred_element_type=jnp.float32)
    for part in range(acc.shape[1] // HDIM):
        piece = acc[:, part * HDIM : (part + 1) * HDIM]
        if normalize:
            power = jnp.mean(piece * piece, axis=-1, keepdims=True)
            piece = piece * lax.rsqrt(power + EPS) * g_ref[...]
        o_ref[:, part * HDIM : (part + 1) * HDIM] = piece.astype(o_ref.dtype)


def project(x, w, start, count, gain):
    tokens, features = x.shape
    cols = PROJECT_COLS
    normalize = gain is not None
    gain = gain.reshape(1, HDIM) if normalize else jnp.ones((1, HDIM), jnp.float32)
    first = start // cols
    return pl.pallas_call(
        functools.partial(projection_kernel, normalize=normalize),
        grid=(count // cols,),
        in_specs=[
            pl.BlockSpec((tokens, features), lambda j: (0, 0)),
            pl.BlockSpec((features, cols), lambda j: (0, first + j)),
            pl.BlockSpec((1, HDIM), lambda j: (0, 0)),
        ],
        out_specs=pl.BlockSpec((tokens, cols), lambda j: (0, j)),
        out_shape=jax.ShapeDtypeStruct((tokens, count), jnp.bfloat16),
    )(x, w, gain)


MESH = pl.DeviceIdType.MESH


def band_gather_kernel(w_ref, out_ref, local_sem, send_sem, recv_sem):
    count = lax.axis_size("height")
    me = lax.axis_index("height")
    frame_block = lax.axis_index("tm")
    barrier = pltpu.get_barrier_semaphore()
    for step in range(1, count):
        peer = lax.rem(me + step, count)
        pl.semaphore_signal(barrier, inc=1, device_id=(frame_block, peer), device_id_type=MESH)
    pl.semaphore_wait(barrier, count - 1)
    own = pltpu.make_async_copy(w_ref, out_ref.at[me], local_sem)
    own.start()
    copies = []
    for step in range(1, count):
        peer = lax.rem(me + step, count)
        copy = pltpu.make_async_remote_copy(
            src_ref=w_ref,
            dst_ref=out_ref.at[me],
            send_sem=send_sem.at[step],
            recv_sem=recv_sem.at[me],
            device_id=(frame_block, peer),
            device_id_type=MESH,
        )
        copy.start()
        copies.append(copy)
    for copy in copies:
        copy.wait_send()
    for step in range(1, count):
        source = lax.rem(me + count - step, count)
        incoming = pltpu.make_async_remote_copy(
            src_ref=w_ref,
            dst_ref=out_ref.at[source],
            send_sem=send_sem.at[step],
            recv_sem=recv_sem.at[source],
            device_id=(frame_block, source),
            device_id_type=MESH,
        )
        incoming.wait_recv()
    own.wait()


def band_gather(w):
    rows, cols = w.shape
    count = lax.axis_size("height")
    gathered = pl.pallas_call(
        band_gather_kernel,
        in_specs=[pl.BlockSpec(memory_space=pl.ANY)],
        out_specs=pl.BlockSpec(memory_space=pl.ANY),
        out_shape=jax.ShapeDtypeStruct((count, rows, cols), w.dtype),
        scratch_shapes=[
            pltpu.SemaphoreType.DMA(()),
            pltpu.SemaphoreType.DMA((count,)),
            pltpu.SemaphoreType.DMA((count,)),
        ],
        compiler_params=pltpu.CompilerParams(collective_id=0, has_side_effects=True),
    )(w)
    return gathered.reshape(count * rows, cols)


def projection_kv_kernel(x_ref, w_ref, g_ref, o_ref):
    acc = jnp.dot(x_ref[...], w_ref[...], preferred_element_type=jnp.float32)
    is_key = pl.program_id(0) < pl.num_programs(0) // 2
    for part in range(acc.shape[1] // HDIM):
        piece = acc[:, part * HDIM : (part + 1) * HDIM]
        power = jnp.mean(piece * piece, axis=-1, keepdims=True)
        scale = jnp.where(is_key, lax.rsqrt(power + EPS), jnp.float32(1.0))
        gain = jnp.where(is_key, g_ref[...], jnp.float32(1.0))
        normed = jnp.where(is_key, piece * scale * gain, piece)
        o_ref[0, :, part * HDIM : (part + 1) * HDIM] = normed.astype(o_ref.dtype)


def project_kv(x, w, start, count, gain):
    tokens, features = x.shape
    cols = PROJECT_COLS
    inner = w.shape[1] // 3
    steps = count // cols
    key_first = (inner + start) // cols
    value_first = (2 * inner + start) // cols

    def weight_block(j):
        return (0, jnp.where(j < steps, key_first + j, value_first + j - steps))

    return pl.pallas_call(
        projection_kv_kernel,
        grid=(2 * steps,),
        in_specs=[
            pl.BlockSpec((tokens, features), lambda j: (0, 0)),
            pl.BlockSpec((features, cols), weight_block),
            pl.BlockSpec((1, HDIM), lambda j: (0, 0)),
        ],
        out_specs=pl.BlockSpec((1, tokens, cols), lambda j: (j // steps, 0, j % steps)),
        out_shape=jax.ShapeDtypeStruct((2, tokens, count), jnp.bfloat16),
    )(x, w, gain.reshape(1, HDIM))


def solution(mesh):
    in_specs = (
        P("tm", "height", None, None),
        P(),
        P(),
        P(("tm", "height"), None),
        P(),
        P(),
        P(),
        P(),
    )
    out_specs = P("tm", "height", None, None)
    return jax.shard_map(
        per_device, mesh=mesh, in_specs=in_specs, out_specs=out_specs, check_vma=False
    )
```

```python
import functools

import jax
import jax.numpy as jnp
from jax import lax
from jax.sharding import PartitionSpec as P
from jax.experimental import pallas as pl
from jax.experimental.pallas import tpu as pltpu

HDIM = 128
HEADS = 12
TT = 1
TH = 2
TW = 8
GROUPS = 2


EPS = 1e-06


def with_halo(cells, sides, width):
    for axis, dim in sides:
        count = lax.axis_size(axis)
        ends = count - 1
        head = lax.slice_in_dim(cells, 0, width, axis=dim)
        tail = lax.slice_in_dim(cells, cells.shape[dim] - width, cells.shape[dim], axis=dim)
        cells = jnp.concatenate(
            [
                lax.ppermute(tail, axis, [(i, (i + 1) % count) for i in range(ends)]),
                cells,
                lax.ppermute(head, axis, [((i + 1) % count, i) for i in range(ends)]),
            ],
            axis=dim,
        )
    return cells


def modulate(tokens, mod_scale, mod_shift):
    values = tokens.astype(jnp.float32)
    mean = jnp.mean(values, axis=-1, keepdims=True)
    centred = values - mean
    variance = jnp.mean(centred * centred, axis=-1, keepdims=True)
    normed = centred * lax.rsqrt(variance + EPS)
    return (normed * (1.0 + mod_scale) + mod_shift).astype(jnp.bfloat16)


def head_norm(values, gain):
    power = jnp.mean(values * values, axis=-1, keepdims=True)
    return (values * lax.rsqrt(power + EPS) * gain).astype(jnp.bfloat16)


def tile_coords(frames, rows, width):
    shape = (frames.shape[0], rows.shape[0], width)
    columns = jnp.arange(width, dtype=jnp.int32)
    frame_tiles = jnp.broadcast_to((frames // TT)[:, None, None], shape).reshape(-1)
    row_tiles = jnp.broadcast_to((rows // TH)[None, :, None], shape).reshape(-1)
    column_tiles = jnp.broadcast_to((columns // TW)[None, None, :], shape).reshape(-1)
    return (frame_tiles, row_tiles, column_tiles)


def per_device(tokens, mod_scale, mod_shift, w_qkv, q_gain, k_gain, window, valid):
    frame_count, row_count, width, features = tokens.shape
    token_count = frame_count * row_count * width
    modulated = modulate(tokens.reshape(token_count, features), mod_scale, mod_shift)
    band_weight = band_gather(w_qkv)
    full_weight = lax.all_gather(band_weight, "tm", axis=0, tiled=True)
    inner = full_weight.shape[1] // 3
    group_cols = inner // GROUPS
    tiled = (frame_count // TT, TT, row_count // TH, TH, width, group_cols)
    groups = []
    for group in range(GROUPS):
        start = group * group_cols
        stacked = project_kv(modulated, full_weight, start, group_cols, k_gain)
        stacked = stacked.reshape(2, *tiled)
        groups.append(with_halo(stacked, (("tm", 1), ("height", 3)), 1))
    frames_ext = frame_count + 2 * TT
    rows_ext = row_count + 2 * TH
    groups = [g.reshape(2, frames_ext, rows_ext, width, group_cols) for g in groups]
    frame_block = lax.axis_index("tm")
    row_block = lax.axis_index("height")
    first_frame = frame_block * frame_count
    first_row = row_block * row_count
    zero = jnp.int32(0)
    valid_pad = jnp.pad(valid, ((TT, TT), (TH, TH), (0, 0)))
    key_valid = lax.dynamic_slice(
        valid_pad, (first_frame, first_row, zero), (frames_ext, rows_ext, width)
    )
    query_valid = lax.dynamic_slice(
        valid, (first_frame, first_row, zero), (frame_count, row_count, width)
    )
    row_tiles = row_count // TH
    blocks = frame_count * row_tiles
    span_t = 2 * TT + 1
    span_h = 3 * TH
    query_n = TH * width
    key_n = span_t * span_h * width
    block_valid = jnp.stack(
        [
            key_valid[f : f + span_t, TH * rt : TH * rt + span_h].reshape(-1)
            for f in range(frame_count)
            for rt in range(row_tiles)
        ]
    )
    apart_t = jnp.abs(jnp.arange(span_t, dtype=jnp.int32) - TT)
    apart_h = jnp.abs(jnp.arange(span_h, dtype=jnp.int32) // TH - 1)
    near = (apart_t[None, :, None, None] <= window[:, 0, None, None, None]) & (
        apart_h[None, None, :, None] <= window[:, 1, None, None, None]
    )
    near = jnp.broadcast_to(near, (HEADS, span_t, span_h, width)).reshape(HEADS, 1, key_n)
    key_mask = (near & (block_valid[None] > 0)).astype(jnp.float32).reshape(HEADS, blocks, 1, key_n)
    column_tiles = jnp.arange(width, dtype=jnp.int32) // TW
    key_cols = jnp.tile(column_tiles, span_t * span_h).reshape(1, key_n)
    query_cols = jnp.tile(column_tiles, TH)
    query_lo = (query_cols[None, :] - window[:, 2, None]).reshape(HEADS, query_n, 1)
    query_hi = (query_cols[None, :] + window[:, 2, None]).reshape(HEADS, query_n, 1)
    query_ok = query_valid.reshape(blocks, query_n, 1).astype(jnp.float32)
    out = None
    for group, extended in enumerate(groups):
        source = modulated
        if out is not None:
            source, out = lax.optimization_barrier((modulated, out))
        query = project(source, full_weight, group * group_cols, group_cols, q_gain)
        query = query.reshape(frame_count, row_count, width, group_cols)
        out = tile_attention(
            query, extended, key_mask, query_lo, query_hi, key_cols, query_ok, group, out
        )
    return out


def attention_kernel(q_ref, k_ref, v_ref, km_ref, lo_ref, hi_ref, kc_ref, qv_ref, o_ref):
    span_t = 2 * TT + 1
    span_h = 3 * TH
    width = q_ref.shape[2]
    key_cols = kc_ref[...]
    width_ok = (key_cols >= lo_ref[0]) & (key_cols <= hi_ref[0])
    for block in range(q_ref.shape[0] * ROW_TILES):
        frame, tile = divmod(block, ROW_TILES)
        row = tile * TH
        query = q_ref[frame, row : row + TH].reshape(TH * width, HDIM)
        key = k_ref[0, frame : frame + span_t, row : row + span_h].reshape(-1, HDIM)
        value = v_ref[0, frame : frame + span_t, row : row + span_h].reshape(-1, HDIM)
        scores = lax.dot_general(
            query, key, (((1,), (1,)), ((), ())), preferred_element_type=jnp.float32
        ) * (1.0 / float(HDIM) ** 0.5)
        allowed = width_ok & (km_ref[0, block] > 0.0)
        terms = jnp.where(allowed, jnp.exp(scores), jnp.float32(0.0))
        total = jnp.sum(terms, axis=-1, keepdims=True)
        seen = qv_ref[block] > 0.0
        total = jnp.where(seen, total, jnp.float32(1.0))
        weights = (terms * (1.0 / total)).astype(jnp.bfloat16)
        result = jnp.dot(weights, value, preferred_element_type=jnp.float32)
        result = jnp.where(seen, result, jnp.float32(0.0)).astype(jnp.bfloat16)
        o_ref[frame, row : row + TH] = result.reshape(TH, width, HDIM)


ROW_TILES = 2


def tile_attention(query, extended, key_mask, query_lo, query_hi, key_cols, query_ok, group, out):
    frames, rows, width, group_cols = query.shape
    heads = group_cols // HDIM
    out_shape = (frames, rows, width, key_mask.shape[0] * HDIM)
    first = group * heads
    row_tiles = rows // TH
    assert row_tiles == ROW_TILES
    blocks = frames * row_tiles
    _, frames_ext, rows_ext, _, _ = extended.shape
    key_n = key_mask.shape[-1]
    query_n = TH * width
    q_spec = pl.BlockSpec((frames, rows, width, HDIM), lambda h: (0, 0, 0, h))
    o_spec = pl.BlockSpec((frames, rows, width, HDIM), lambda h: (0, 0, 0, first + h))
    in_specs = [
        q_spec,
        pl.BlockSpec((1, frames_ext, rows_ext, width, HDIM), lambda h: (0, 0, 0, 0, h)),
        pl.BlockSpec((1, frames_ext, rows_ext, width, HDIM), lambda h: (1, 0, 0, 0, h)),
        pl.BlockSpec((1, blocks, 1, key_n), lambda h: (first + h, 0, 0, 0)),
        pl.BlockSpec((1, query_n, 1), lambda h: (first + h, 0, 0)),
        pl.BlockSpec((1, query_n, 1), lambda h: (first + h, 0, 0)),
        pl.BlockSpec((1, key_n), lambda h: (0, 0)),
        pl.BlockSpec((blocks, query_n, 1), lambda h: (0, 0, 0)),
    ]
    operands = [query, extended, extended, key_mask, query_lo, query_hi, key_cols, query_ok]
    aliases = {}
    kernel = attention_kernel
    if out is not None:
        in_specs.append(pl.BlockSpec(memory_space=pl.ANY))
        operands.append(out)
        aliases = {len(operands) - 1: 0}
        kernel = lambda *refs: attention_kernel(*refs[:8], refs[9])
    return pl.pallas_call(
        kernel,
        grid=(heads,),
        in_specs=in_specs,
        out_specs=o_spec,
        out_shape=jax.ShapeDtypeStruct(out_shape, jnp.bfloat16),
        input_output_aliases=aliases,
    )(*operands)


PROJECT_COLS = 256


def projection_kernel(x_ref, w_ref, g_ref, o_ref, *, normalize):
    acc = jnp.dot(x_ref[...], w_ref[...], preferred_element_type=jnp.float32)
    for part in range(acc.shape[1] // HDIM):
        piece = acc[:, part * HDIM : (part + 1) * HDIM]
        if normalize:
            power = jnp.mean(piece * piece, axis=-1, keepdims=True)
            piece = piece * lax.rsqrt(power + EPS) * g_ref[...]
        o_ref[:, part * HDIM : (part + 1) * HDIM] = piece.astype(o_ref.dtype)


def project(x, w, start, count, gain):
    tokens, features = x.shape
    cols = PROJECT_COLS
    normalize = gain is not None
    gain = gain.reshape(1, HDIM) if normalize else jnp.ones((1, HDIM), jnp.float32)
    first = start // cols
    return pl.pallas_call(
        functools.partial(projection_kernel, normalize=normalize),
        grid=(count // cols,),
        in_specs=[
            pl.BlockSpec((tokens, features), lambda j: (0, 0)),
            pl.BlockSpec((features, cols), lambda j: (0, first + j)),
            pl.BlockSpec((1, HDIM), lambda j: (0, 0)),
        ],
        out_specs=pl.BlockSpec((tokens, cols), lambda j: (0, j)),
        out_shape=jax.ShapeDtypeStruct((tokens, count), jnp.bfloat16),
    )(x, w, gain)


MESH = pl.DeviceIdType.MESH


def band_gather_kernel(w_ref, out_ref, local_sem, send_sem, recv_sem):
    count = lax.axis_size("height")
    me = lax.axis_index("height")
    frame_block = lax.axis_index("tm")
    barrier = pltpu.get_barrier_semaphore()
    for step in range(1, count):
        peer = lax.rem(me + step, count)
        pl.semaphore_signal(barrier, inc=1, device_id=(frame_block, peer), device_id_type=MESH)
    pl.semaphore_wait(barrier, count - 1)
    own = pltpu.make_async_copy(w_ref, out_ref.at[me], local_sem)
    own.start()
    copies = []
    for step in range(1, count):
        peer = lax.rem(me + step, count)
        copy = pltpu.make_async_remote_copy(
            src_ref=w_ref,
            dst_ref=out_ref.at[me],
            send_sem=send_sem.at[step],
            recv_sem=recv_sem.at[me],
            device_id=(frame_block, peer),
            device_id_type=MESH,
        )
        copy.start()
        copies.append(copy)
    for copy in copies:
        copy.wait_send()
    for step in range(1, count):
        source = lax.rem(me + count - step, count)
        incoming = pltpu.make_async_remote_copy(
            src_ref=w_ref,
            dst_ref=out_ref.at[source],
            send_sem=send_sem.at[step],
            recv_sem=recv_sem.at[source],
            device_id=(frame_block, source),
            device_id_type=MESH,
        )
        incoming.wait_recv()
    own.wait()


def band_gather(w):
    rows, cols = w.shape
    count = lax.axis_size("height")
    gathered = pl.pallas_call(
        band_gather_kernel,
        in_specs=[pl.BlockSpec(memory_space=pl.ANY)],
        out_specs=pl.BlockSpec(memory_space=pl.ANY),
        out_shape=jax.ShapeDtypeStruct((count, rows, cols), w.dtype),
        scratch_shapes=[
            pltpu.SemaphoreType.DMA(()),
            pltpu.SemaphoreType.DMA((count,)),
            pltpu.SemaphoreType.DMA((count,)),
        ],
        compiler_params=pltpu.CompilerParams(collective_id=0, has_side_effects=True),
    )(w)
    return gathered.reshape(count * rows, cols)


def projection_kv_kernel(x_ref, w_ref, g_ref, o_ref):
    acc = jnp.dot(x_ref[...], w_ref[...], preferred_element_type=jnp.float32)
    is_key = pl.program_id(0) < pl.num_programs(0) // 2
    for part in range(acc.shape[1] // HDIM):
        piece = acc[:, part * HDIM : (part + 1) * HDIM]
        power = jnp.mean(piece * piece, axis=-1, keepdims=True)
        scale = jnp.where(is_key, lax.rsqrt(power + EPS), jnp.float32(1.0))
        gain = jnp.where(is_key, g_ref[...], jnp.float32(1.0))
        normed = jnp.where(is_key, piece * scale * gain, piece)
        o_ref[0, :, part * HDIM : (part + 1) * HDIM] = normed.astype(o_ref.dtype)


def project_kv(x, w, start, count, gain):
    tokens, features = x.shape
    cols = PROJECT_COLS
    inner = w.shape[1] // 3
    steps = count // cols
    key_first = (inner + start) // cols
    value_first = (2 * inner + start) // cols

    def weight_block(j):
        return (0, jnp.where(j < steps, key_first + j, value_first + j - steps))

    return pl.pallas_call(
        projection_kv_kernel,
        grid=(2 * steps,),
        in_specs=[
            pl.BlockSpec((tokens, features), lambda j: (0, 0)),
            pl.BlockSpec((features, cols), weight_block),
            pl.BlockSpec((1, HDIM), lambda j: (0, 0)),
        ],
        out_specs=pl.BlockSpec((1, tokens, cols), lambda j: (j // steps, 0, j % steps)),
        out_shape=jax.ShapeDtypeStruct((2, tokens, count), jnp.bfloat16),
    )(x, w, gain.reshape(1, HDIM))


def solution(mesh):
    in_specs = (
        P("tm", "height", None, None),
        P(),
        P(),
        P(("tm", "height"), None),
        P(),
        P(),
        P(),
        P(),
    )
    out_specs = P("tm", "height", None, None)
    return jax.shard_map(
        per_device, mesh=mesh, in_specs=in_specs, out_specs=out_specs, check_vma=False
    )
```

```python
import functools

import jax
import jax.numpy as jnp
from jax import lax
from jax.sharding import PartitionSpec as P
from jax.experimental import pallas as pl
from jax.experimental.pallas import tpu as pltpu

HDIM = 128
HEADS = 12
TT = 1
TH = 2
TW = 8
GROUPS = 2


EPS = 1e-06


def with_halo(cells, sides, width):
    for axis, dim in sides:
        count = lax.axis_size(axis)
        ends = count - 1
        head = lax.slice_in_dim(cells, 0, width, axis=dim)
        tail = lax.slice_in_dim(cells, cells.shape[dim] - width, cells.shape[dim], axis=dim)
        cells = jnp.concatenate(
            [
                lax.ppermute(tail, axis, [(i, (i + 1) % count) for i in range(ends)]),
                cells,
                lax.ppermute(head, axis, [((i + 1) % count, i) for i in range(ends)]),
            ],
            axis=dim,
        )
    return cells


def modulate(tokens, mod_scale, mod_shift):
    values = tokens.astype(jnp.float32)
    mean = jnp.mean(values, axis=-1, keepdims=True)
    centred = values - mean
    variance = jnp.mean(centred * centred, axis=-1, keepdims=True)
    normed = centred * lax.rsqrt(variance + EPS)
    return (normed * (1.0 + mod_scale) + mod_shift).astype(jnp.bfloat16)


def head_norm(values, gain):
    power = jnp.mean(values * values, axis=-1, keepdims=True)
    return (values * lax.rsqrt(power + EPS) * gain).astype(jnp.bfloat16)


def tile_coords(frames, rows, width):
    shape = (frames.shape[0], rows.shape[0], width)
    columns = jnp.arange(width, dtype=jnp.int32)
    frame_tiles = jnp.broadcast_to((frames // TT)[:, None, None], shape).reshape(-1)
    row_tiles = jnp.broadcast_to((rows // TH)[None, :, None], shape).reshape(-1)
    column_tiles = jnp.broadcast_to((columns // TW)[None, None, :], shape).reshape(-1)
    return (frame_tiles, row_tiles, column_tiles)


def per_device(tokens, mod_scale, mod_shift, w_qkv, q_gain, k_gain, window, valid):
    frame_count, row_count, width, features = tokens.shape
    token_count = frame_count * row_count * width
    modulated = modulate(tokens.reshape(token_count, features), mod_scale, mod_shift)
    band_weight = band_gather(w_qkv)
    full_weight = lax.all_gather(band_weight, "tm", axis=0, tiled=True)
    inner = full_weight.shape[1] // 3
    group_cols = inner // GROUPS
    tiled = (frame_count // TT, TT, row_count // TH, TH, width, group_cols)
    groups = []
    for group in range(GROUPS):
        start = group * group_cols
        stacked = project_kv(modulated, full_weight, start, group_cols, k_gain)
        stacked = stacked.reshape(2, *tiled)
        middle = with_halo(stacked, (("tm", 1),), 1)
        middle = middle.reshape(2, frame_count + 2 * TT, row_count, width, group_cols)
        count = lax.axis_size("height")
        top = lax.ppermute(
            middle[:, :, row_count - TH :], "height", [(i, i + 1) for i in range(count - 1)]
        )
        bottom = lax.ppermute(middle[:, :, :TH], "height", [(i + 1, i) for i in range(count - 1)])
        groups.append((middle, top, bottom))
    query = project(modulated, full_weight, 0, inner, q_gain)
    frames_ext = frame_count + 2 * TT
    rows_ext = row_count + 2 * TH
    frame_block = lax.axis_index("tm")
    row_block = lax.axis_index("height")
    first_frame = frame_block * frame_count
    first_row = row_block * row_count
    zero = jnp.int32(0)
    valid_pad = jnp.pad(valid, ((TT, TT), (TH, TH), (0, 0)))
    key_valid = lax.dynamic_slice(
        valid_pad, (first_frame, first_row, zero), (frames_ext, rows_ext, width)
    )
    query_valid = lax.dynamic_slice(
        valid, (first_frame, first_row, zero), (frame_count, row_count, width)
    )
    row_tiles = row_count // TH
    blocks = frame_count * row_tiles
    span_t = 2 * TT + 1
    span_h = 3 * TH
    query_n = TH * width
    key_n = span_t * span_h * width
    block_valid = jnp.stack(
        [
            key_valid[f : f + span_t, TH * rt : TH * rt + span_h].reshape(-1)
            for f in range(frame_count)
            for rt in range(row_tiles)
        ]
    )
    apart_t = jnp.abs(jnp.arange(span_t, dtype=jnp.int32) - TT)
    apart_h = jnp.abs(jnp.arange(span_h, dtype=jnp.int32) // TH - 1)
    near = (apart_t[None, :, None, None] <= window[:, 0, None, None, None]) & (
        apart_h[None, None, :, None] <= window[:, 1, None, None, None]
    )
    near = jnp.broadcast_to(near, (HEADS, span_t, span_h, width)).reshape(HEADS, 1, key_n)
    key_mask = (near & (block_valid[None] > 0)).astype(jnp.float32).reshape(HEADS, blocks, 1, key_n)
    column_tiles = jnp.arange(width, dtype=jnp.int32) // TW
    key_cols = jnp.tile(column_tiles, span_t * span_h).reshape(1, key_n)
    query_cols = jnp.tile(column_tiles, TH)
    query_lo = (query_cols[None, :] - window[:, 2, None]).reshape(HEADS, query_n, 1)
    query_hi = (query_cols[None, :] + window[:, 2, None]).reshape(HEADS, query_n, 1)
    query_ok = query_valid.reshape(blocks, query_n, 1).astype(jnp.float32)
    query_grid = query.reshape(frame_count, row_count, width, inner)
    assert row_count == 2 * TH
    mask_rows = key_mask.reshape(HEADS, blocks, span_t, span_h, width)
    halo_masks, own_masks = [], []
    for block in range(blocks):
        halo_rows = slice(0, TH) if block % row_tiles == 0 else slice(span_h - TH, span_h)
        own_rows = slice(TH, span_h) if block % row_tiles == 0 else slice(0, row_count)
        halo_masks.append(mask_rows[:, block, :, halo_rows].reshape(HEADS, 1, -1))
        own_masks.append(mask_rows[:, block, :, own_rows].reshape(HEADS, 1, -1))
    halo_mask = jnp.stack(halo_masks, axis=1)
    own_mask = jnp.stack(own_masks, axis=1)
    halo_cols = jnp.tile(column_tiles, span_t * TH).reshape(1, -1)
    own_cols = jnp.tile(column_tiles, span_t * row_count).reshape(1, -1)
    out = None
    for group, pieces in enumerate(groups):
        masks = (halo_mask, own_mask, query_lo, query_hi, halo_cols, own_cols, query_ok)
        out = tile_attention(query_grid, pieces, masks, group, out)
    return out


def attention_kernel(
    q_ref, mk_ref, mv_ref, tk_ref, tv_ref, bk_ref, bv_ref,
    hm_ref, om_ref, lo_ref, hi_ref, hc_ref, oc_ref, qv_ref, o_ref,
):
    span_t = 2 * TT + 1
    width = q_ref.shape[2]
    scale = 1.0 / float(HDIM) ** 0.5
    halo_ok = (hc_ref[...] >= lo_ref[0]) & (hc_ref[...] <= hi_ref[0])
    own_ok = (oc_ref[...] >= lo_ref[0]) & (oc_ref[...] <= hi_ref[0])
    for block in range(q_ref.shape[0] * ROW_TILES):
        frame, tile = divmod(block, ROW_TILES)
        row = tile * TH
        hk_ref, hv_ref = (tk_ref, tv_ref) if tile == 0 else (bk_ref, bv_ref)
        query = q_ref[frame, row : row + TH].reshape(TH * width, HDIM)
        pieces = (
            (hk_ref, hv_ref, halo_ok & (hm_ref[0, block] > 0.0)),
            (mk_ref, mv_ref, own_ok & (om_ref[0, block] > 0.0)),
        )
        terms, values = [], []
        for k_ref, v_ref, allowed in pieces:
            key = k_ref[0, frame : frame + span_t].reshape(-1, HDIM)
            values.append(v_ref[0, frame : frame + span_t].reshape(-1, HDIM))
            scores = lax.dot_general(
                query, key, (((1,), (1,)), ((), ())), preferred_element_type=jnp.float32
            ) * scale
            terms.append(jnp.where(allowed, jnp.exp(scores), jnp.float32(0.0)))
        total = jnp.sum(terms[0], axis=-1, keepdims=True) + jnp.sum(terms[1], axis=-1, keepdims=True)
        seen = qv_ref[block] > 0.0
        inverse = 1.0 / jnp.where(seen, total, jnp.float32(1.0))
        result = jnp.dot(
            (terms[0] * inverse).astype(jnp.bfloat16), values[0], preferred_element_type=jnp.float32
        ) + jnp.dot(
            (terms[1] * inverse).astype(jnp.bfloat16), values[1], preferred_element_type=jnp.float32
        )
        result = jnp.where(seen, result, jnp.float32(0.0)).astype(jnp.bfloat16)
        o_ref[frame, row : row + TH] = result.reshape(TH, width, HDIM)


ROW_TILES = 2


def tile_attention(query, pieces, masks, group, out):
    frames, rows, width, inner = query.shape
    middle, top, bottom = pieces
    heads = middle.shape[-1] // HDIM
    first = group * heads
    assert rows // TH == ROW_TILES
    blocks = frames * ROW_TILES
    halo_mask, own_mask, query_lo, query_hi, halo_cols, own_cols, query_ok = masks
    query_n = TH * width
    q_spec = pl.BlockSpec((frames, rows, width, HDIM), lambda h: (0, 0, 0, first + h))

    def piece_specs(piece):
        shape = (1, *piece.shape[1:-1], HDIM)
        return [
            pl.BlockSpec(shape, lambda h: (0, 0, 0, 0, h)),
            pl.BlockSpec(shape, lambda h: (1, 0, 0, 0, h)),
        ]

    in_specs = [q_spec] + piece_specs(middle) + piece_specs(top) + piece_specs(bottom) + [
        pl.BlockSpec((1, blocks, 1, halo_mask.shape[-1]), lambda h: (first + h, 0, 0, 0)),
        pl.BlockSpec((1, blocks, 1, own_mask.shape[-1]), lambda h: (first + h, 0, 0, 0)),
        pl.BlockSpec((1, query_n, 1), lambda h: (first + h, 0, 0)),
        pl.BlockSpec((1, query_n, 1), lambda h: (first + h, 0, 0)),
        pl.BlockSpec((1, halo_cols.shape[-1]), lambda h: (0, 0)),
        pl.BlockSpec((1, own_cols.shape[-1]), lambda h: (0, 0)),
        pl.BlockSpec((blocks, query_n, 1), lambda h: (0, 0, 0)),
    ]
    operands = [query, middle, middle, top, top, bottom, bottom, halo_mask, own_mask,
                query_lo, query_hi, halo_cols, own_cols, query_ok]
    aliases = {}
    kernel = attention_kernel
    if out is not None:
        count = len(operands)
        in_specs.append(pl.BlockSpec(memory_space=pl.ANY))
        operands.append(out)
        aliases = {count: 0}
        kernel = lambda *refs: attention_kernel(*refs[:count], refs[count + 1])
    return pl.pallas_call(
        kernel,
        grid=(heads,),
        in_specs=in_specs,
        out_specs=q_spec,
        out_shape=jax.ShapeDtypeStruct(query.shape, jnp.bfloat16),
        input_output_aliases=aliases,
    )(*operands)


PROJECT_COLS = 256


def projection_kernel(x_ref, w_ref, g_ref, o_ref, *, normalize):
    acc = jnp.dot(x_ref[...], w_ref[...], preferred_element_type=jnp.float32)
    for part in range(acc.shape[1] // HDIM):
        piece = acc[:, part * HDIM : (part + 1) * HDIM]
        if normalize:
            power = jnp.mean(piece * piece, axis=-1, keepdims=True)
            piece = piece * lax.rsqrt(power + EPS) * g_ref[...]
        o_ref[:, part * HDIM : (part + 1) * HDIM] = piece.astype(o_ref.dtype)


def project(x, w, start, count, gain):
    tokens, features = x.shape
    cols = PROJECT_COLS
    normalize = gain is not None
    gain = gain.reshape(1, HDIM) if normalize else jnp.ones((1, HDIM), jnp.float32)
    first = start // cols
    return pl.pallas_call(
        functools.partial(projection_kernel, normalize=normalize),
        grid=(count // cols,),
        in_specs=[
            pl.BlockSpec((tokens, features), lambda j: (0, 0)),
            pl.BlockSpec((features, cols), lambda j: (0, first + j)),
            pl.BlockSpec((1, HDIM), lambda j: (0, 0)),
        ],
        out_specs=pl.BlockSpec((tokens, cols), lambda j: (0, j)),
        out_shape=jax.ShapeDtypeStruct((tokens, count), jnp.bfloat16),
    )(x, w, gain)


MESH = pl.DeviceIdType.MESH


def band_gather_kernel(w_ref, out_ref, local_sem, send_sem, recv_sem):
    count = lax.axis_size("height")
    me = lax.axis_index("height")
    frame_block = lax.axis_index("tm")
    barrier = pltpu.get_barrier_semaphore()
    for step in range(1, count):
        peer = lax.rem(me + step, count)
        pl.semaphore_signal(barrier, inc=1, device_id=(frame_block, peer), device_id_type=MESH)
    pl.semaphore_wait(barrier, count - 1)
    own = pltpu.make_async_copy(w_ref, out_ref.at[me], local_sem)
    own.start()
    copies = []
    for step in range(1, count):
        peer = lax.rem(me + step, count)
        copy = pltpu.make_async_remote_copy(
            src_ref=w_ref,
            dst_ref=out_ref.at[me],
            send_sem=send_sem.at[step],
            recv_sem=recv_sem.at[me],
            device_id=(frame_block, peer),
            device_id_type=MESH,
        )
        copy.start()
        copies.append(copy)
    for copy in copies:
        copy.wait_send()
    for step in range(1, count):
        source = lax.rem(me + count - step, count)
        incoming = pltpu.make_async_remote_copy(
            src_ref=w_ref,
            dst_ref=out_ref.at[source],
            send_sem=send_sem.at[step],
            recv_sem=recv_sem.at[source],
            device_id=(frame_block, source),
            device_id_type=MESH,
        )
        incoming.wait_recv()
    own.wait()


def band_gather(w):
    rows, cols = w.shape
    count = lax.axis_size("height")
    gathered = pl.pallas_call(
        band_gather_kernel,
        in_specs=[pl.BlockSpec(memory_space=pl.ANY)],
        out_specs=pl.BlockSpec(memory_space=pl.ANY),
        out_shape=jax.ShapeDtypeStruct((count, rows, cols), w.dtype),
        scratch_shapes=[
            pltpu.SemaphoreType.DMA(()),
            pltpu.SemaphoreType.DMA((count,)),
            pltpu.SemaphoreType.DMA((count,)),
        ],
        compiler_params=pltpu.CompilerParams(collective_id=0, has_side_effects=True),
    )(w)
    return gathered.reshape(count * rows, cols)


def projection_kv_kernel(x_ref, w_ref, g_ref, o_ref):
    acc = jnp.dot(x_ref[...], w_ref[...], preferred_element_type=jnp.float32)
    is_key = pl.program_id(0) < pl.num_programs(0) // 2
    for part in range(acc.shape[1] // HDIM):
        piece = acc[:, part * HDIM : (part + 1) * HDIM]
        power = jnp.mean(piece * piece, axis=-1, keepdims=True)
        scale = jnp.where(is_key, lax.rsqrt(power + EPS), jnp.float32(1.0))
        gain = jnp.where(is_key, g_ref[...], jnp.float32(1.0))
        normed = jnp.where(is_key, piece * scale * gain, piece)
        o_ref[0, :, part * HDIM : (part + 1) * HDIM] = normed.astype(o_ref.dtype)


def project_kv(x, w, start, count, gain):
    tokens, features = x.shape
    cols = PROJECT_COLS
    inner = w.shape[1] // 3
    steps = count // cols
    key_first = (inner + start) // cols
    value_first = (2 * inner + start) // cols

    def weight_block(j):
        return (0, jnp.where(j < steps, key_first + j, value_first + j - steps))

    return pl.pallas_call(
        projection_kv_kernel,
        grid=(2 * steps,),
        in_specs=[
            pl.BlockSpec((tokens, features), lambda j: (0, 0)),
            pl.BlockSpec((features, cols), weight_block),
            pl.BlockSpec((1, HDIM), lambda j: (0, 0)),
        ],
        out_specs=pl.BlockSpec((1, tokens, cols), lambda j: (j // steps, 0, j % steps)),
        out_shape=jax.ShapeDtypeStruct((2, tokens, count), jnp.bfloat16),
    )(x, w, gain.reshape(1, HDIM))


def solution(mesh):
    in_specs = (
        P("tm", "height", None, None),
        P(),
        P(),
        P(("tm", "height"), None),
        P(),
        P(),
        P(),
        P(),
    )
    out_specs = P("tm", "height", None, None)
    return jax.shard_map(
        per_device, mesh=mesh, in_specs=in_specs, out_specs=out_specs, check_vma=False
    )
```

```python
import functools

import jax
import jax.numpy as jnp
from jax import lax
from jax.sharding import PartitionSpec as P
from jax.experimental import pallas as pl
from jax.experimental.pallas import tpu as pltpu

HDIM = 128
HEADS = 12
TT = 1
TH = 2
TW = 8
GROUPS = 3


EPS = 1e-06


def with_halo(cells, sides, width):
    for axis, dim in sides:
        count = lax.axis_size(axis)
        ends = count - 1
        head = lax.slice_in_dim(cells, 0, width, axis=dim)
        tail = lax.slice_in_dim(cells, cells.shape[dim] - width, cells.shape[dim], axis=dim)
        cells = jnp.concatenate(
            [
                lax.ppermute(tail, axis, [(i, (i + 1) % count) for i in range(ends)]),
                cells,
                lax.ppermute(head, axis, [((i + 1) % count, i) for i in range(ends)]),
            ],
            axis=dim,
        )
    return cells


def modulate(tokens, mod_scale, mod_shift):
    values = tokens.astype(jnp.float32)
    mean = jnp.mean(values, axis=-1, keepdims=True)
    centred = values - mean
    variance = jnp.mean(centred * centred, axis=-1, keepdims=True)
    normed = centred * lax.rsqrt(variance + EPS)
    return (normed * (1.0 + mod_scale) + mod_shift).astype(jnp.bfloat16)


def head_norm(values, gain):
    power = jnp.mean(values * values, axis=-1, keepdims=True)
    return (values * lax.rsqrt(power + EPS) * gain).astype(jnp.bfloat16)


def tile_coords(frames, rows, width):
    shape = (frames.shape[0], rows.shape[0], width)
    columns = jnp.arange(width, dtype=jnp.int32)
    frame_tiles = jnp.broadcast_to((frames // TT)[:, None, None], shape).reshape(-1)
    row_tiles = jnp.broadcast_to((rows // TH)[None, :, None], shape).reshape(-1)
    column_tiles = jnp.broadcast_to((columns // TW)[None, None, :], shape).reshape(-1)
    return (frame_tiles, row_tiles, column_tiles)


def per_device(tokens, mod_scale, mod_shift, w_qkv, q_gain, k_gain, window, valid):
    frame_count, row_count, width, features = tokens.shape
    token_count = frame_count * row_count * width
    modulated = modulate(tokens.reshape(token_count, features), mod_scale, mod_shift)
    band_weight = band_gather(w_qkv)
    full_weight = lax.all_gather(band_weight, "tm", axis=0, tiled=True)
    inner = full_weight.shape[1] // 3
    group_cols = inner // GROUPS
    tiled = (frame_count // TT, TT, row_count // TH, TH, width, group_cols)
    groups = []
    for group in range(GROUPS):
        start = group * group_cols
        stacked = project_kv(modulated, full_weight, start, group_cols, k_gain)
        stacked = stacked.reshape(2, *tiled)
        middle = with_halo(stacked, (("tm", 1),), 1)
        middle = middle.reshape(2, frame_count + 2 * TT, row_count, width, group_cols)
        count = lax.axis_size("height")
        top = lax.ppermute(
            middle[:, :, row_count - TH :], "height", [(i, i + 1) for i in range(count - 1)]
        )
        bottom = lax.ppermute(middle[:, :, :TH], "height", [(i + 1, i) for i in range(count - 1)])
        groups.append((middle, top, bottom))
    query = project(modulated, full_weight, 0, inner, q_gain)
    frames_ext = frame_count + 2 * TT
    rows_ext = row_count + 2 * TH
    frame_block = lax.axis_index("tm")
    row_block = lax.axis_index("height")
    first_frame = frame_block * frame_count
    first_row = row_block * row_count
    zero = jnp.int32(0)
    valid_pad = jnp.pad(valid, ((TT, TT), (TH, TH), (0, 0)))
    key_valid = lax.dynamic_slice(
        valid_pad, (first_frame, first_row, zero), (frames_ext, rows_ext, width)
    )
    query_valid = lax.dynamic_slice(
        valid, (first_frame, first_row, zero), (frame_count, row_count, width)
    )
    row_tiles = row_count // TH
    blocks = frame_count * row_tiles
    span_t = 2 * TT + 1
    span_h = 3 * TH
    query_n = TH * width
    key_n = span_t * span_h * width
    block_valid = jnp.stack(
        [
            key_valid[f : f + span_t, TH * rt : TH * rt + span_h].reshape(-1)
            for f in range(frame_count)
            for rt in range(row_tiles)
        ]
    )
    apart_t = jnp.abs(jnp.arange(span_t, dtype=jnp.int32) - TT)
    apart_h = jnp.abs(jnp.arange(span_h, dtype=jnp.int32) // TH - 1)
    near = (apart_t[None, :, None, None] <= window[:, 0, None, None, None]) & (
        apart_h[None, None, :, None] <= window[:, 1, None, None, None]
    )
    near = jnp.broadcast_to(near, (HEADS, span_t, span_h, width)).reshape(HEADS, 1, key_n)
    key_mask = (near & (block_valid[None] > 0)).astype(jnp.float32).reshape(HEADS, blocks, 1, key_n)
    column_tiles = jnp.arange(width, dtype=jnp.int32) // TW
    key_cols = jnp.tile(column_tiles, span_t * span_h).reshape(1, key_n)
    query_cols = jnp.tile(column_tiles, TH)
    query_lo = (query_cols[None, :] - window[:, 2, None]).reshape(HEADS, query_n, 1)
    query_hi = (query_cols[None, :] + window[:, 2, None]).reshape(HEADS, query_n, 1)
    query_ok = query_valid.reshape(blocks, query_n, 1).astype(jnp.float32)
    query_grid = query.reshape(frame_count, row_count, width, inner)
    assert row_count == 2 * TH
    mask_rows = key_mask.reshape(HEADS, blocks, span_t, span_h, width)
    halo_masks, own_masks = [], []
    for block in range(blocks):
        halo_rows = slice(0, TH) if block % row_tiles == 0 else slice(span_h - TH, span_h)
        own_rows = slice(TH, span_h) if block % row_tiles == 0 else slice(0, row_count)
        halo_masks.append(mask_rows[:, block, :, halo_rows].reshape(HEADS, 1, -1))
        own_masks.append(mask_rows[:, block, :, own_rows].reshape(HEADS, 1, -1))
    halo_mask = jnp.stack(halo_masks, axis=1)
    own_mask = jnp.stack(own_masks, axis=1)
    halo_cols = jnp.tile(column_tiles, span_t * TH).reshape(1, -1)
    own_cols = jnp.tile(column_tiles, span_t * row_count).reshape(1, -1)
    out = None
    for group, pieces in enumerate(groups):
        masks = (halo_mask, own_mask, query_lo, query_hi, halo_cols, own_cols, query_ok)
        out = tile_attention(query_grid, pieces, masks, group, out)
    return out


def attention_kernel(
    q_ref, mk_ref, mv_ref, tk_ref, tv_ref, bk_ref, bv_ref,
    hm_ref, om_ref, lo_ref, hi_ref, hc_ref, oc_ref, qv_ref, o_ref,
):
    span_t = 2 * TT + 1
    width = q_ref.shape[2]
    scale = 1.0 / float(HDIM) ** 0.5
    halo_ok = (hc_ref[...] >= lo_ref[0]) & (hc_ref[...] <= hi_ref[0])
    own_ok = (oc_ref[...] >= lo_ref[0]) & (oc_ref[...] <= hi_ref[0])
    for block in range(q_ref.shape[0] * ROW_TILES):
        frame, tile = divmod(block, ROW_TILES)
        row = tile * TH
        hk_ref, hv_ref = (tk_ref, tv_ref) if tile == 0 else (bk_ref, bv_ref)
        query = q_ref[frame, row : row + TH].reshape(TH * width, HDIM)
        pieces = (
            (hk_ref, hv_ref, halo_ok & (hm_ref[0, block] > 0.0)),
            (mk_ref, mv_ref, own_ok & (om_ref[0, block] > 0.0)),
        )
        terms, values = [], []
        for k_ref, v_ref, allowed in pieces:
            key = k_ref[0, frame : frame + span_t].reshape(-1, HDIM)
            values.append(v_ref[0, frame : frame + span_t].reshape(-1, HDIM))
            scores = lax.dot_general(
                query, key, (((1,), (1,)), ((), ())), preferred_element_type=jnp.float32
            ) * scale
            terms.append(jnp.where(allowed, jnp.exp(scores), jnp.float32(0.0)))
        total = jnp.sum(terms[0], axis=-1, keepdims=True) + jnp.sum(terms[1], axis=-1, keepdims=True)
        seen = qv_ref[block] > 0.0
        inverse = 1.0 / jnp.where(seen, total, jnp.float32(1.0))
        result = jnp.dot(
            (terms[0] * inverse).astype(jnp.bfloat16), values[0], preferred_element_type=jnp.float32
        ) + jnp.dot(
            (terms[1] * inverse).astype(jnp.bfloat16), values[1], preferred_element_type=jnp.float32
        )
        result = jnp.where(seen, result, jnp.float32(0.0)).astype(jnp.bfloat16)
        o_ref[frame, row : row + TH] = result.reshape(TH, width, HDIM)


ROW_TILES = 2


def tile_attention(query, pieces, masks, group, out):
    frames, rows, width, inner = query.shape
    middle, top, bottom = pieces
    heads = middle.shape[-1] // HDIM
    first = group * heads
    assert rows // TH == ROW_TILES
    blocks = frames * ROW_TILES
    halo_mask, own_mask, query_lo, query_hi, halo_cols, own_cols, query_ok = masks
    query_n = TH * width
    q_spec = pl.BlockSpec((frames, rows, width, HDIM), lambda h: (0, 0, 0, first + h))

    def piece_specs(piece):
        shape = (1, *piece.shape[1:-1], HDIM)
        return [
            pl.BlockSpec(shape, lambda h: (0, 0, 0, 0, h)),
            pl.BlockSpec(shape, lambda h: (1, 0, 0, 0, h)),
        ]

    in_specs = [q_spec] + piece_specs(middle) + piece_specs(top) + piece_specs(bottom) + [
        pl.BlockSpec((1, blocks, 1, halo_mask.shape[-1]), lambda h: (first + h, 0, 0, 0)),
        pl.BlockSpec((1, blocks, 1, own_mask.shape[-1]), lambda h: (first + h, 0, 0, 0)),
        pl.BlockSpec((1, query_n, 1), lambda h: (first + h, 0, 0)),
        pl.BlockSpec((1, query_n, 1), lambda h: (first + h, 0, 0)),
        pl.BlockSpec((1, halo_cols.shape[-1]), lambda h: (0, 0)),
        pl.BlockSpec((1, own_cols.shape[-1]), lambda h: (0, 0)),
        pl.BlockSpec((blocks, query_n, 1), lambda h: (0, 0, 0)),
    ]
    operands = [query, middle, middle, top, top, bottom, bottom, halo_mask, own_mask,
                query_lo, query_hi, halo_cols, own_cols, query_ok]
    aliases = {}
    kernel = attention_kernel
    if out is not None:
        count = len(operands)
        in_specs.append(pl.BlockSpec(memory_space=pl.ANY))
        operands.append(out)
        aliases = {count: 0}
        kernel = lambda *refs: attention_kernel(*refs[:count], refs[count + 1])
    return pl.pallas_call(
        kernel,
        grid=(heads,),
        in_specs=in_specs,
        out_specs=q_spec,
        out_shape=jax.ShapeDtypeStruct(query.shape, jnp.bfloat16),
        input_output_aliases=aliases,
    )(*operands)


PROJECT_COLS = 256


def projection_kernel(x_ref, w_ref, g_ref, o_ref, *, normalize):
    acc = jnp.dot(x_ref[...], w_ref[...], preferred_element_type=jnp.float32)
    for part in range(acc.shape[1] // HDIM):
        piece = acc[:, part * HDIM : (part + 1) * HDIM]
        if normalize:
            power = jnp.mean(piece * piece, axis=-1, keepdims=True)
            piece = piece * lax.rsqrt(power + EPS) * g_ref[...]
        o_ref[:, part * HDIM : (part + 1) * HDIM] = piece.astype(o_ref.dtype)


def project(x, w, start, count, gain):
    tokens, features = x.shape
    cols = PROJECT_COLS
    normalize = gain is not None
    gain = gain.reshape(1, HDIM) if normalize else jnp.ones((1, HDIM), jnp.float32)
    first = start // cols
    return pl.pallas_call(
        functools.partial(projection_kernel, normalize=normalize),
        grid=(count // cols,),
        in_specs=[
            pl.BlockSpec((tokens, features), lambda j: (0, 0)),
            pl.BlockSpec((features, cols), lambda j: (0, first + j)),
            pl.BlockSpec((1, HDIM), lambda j: (0, 0)),
        ],
        out_specs=pl.BlockSpec((tokens, cols), lambda j: (0, j)),
        out_shape=jax.ShapeDtypeStruct((tokens, count), jnp.bfloat16),
    )(x, w, gain)


MESH = pl.DeviceIdType.MESH


def band_gather_kernel(w_ref, out_ref, local_sem, send_sem, recv_sem):
    count = lax.axis_size("height")
    me = lax.axis_index("height")
    frame_block = lax.axis_index("tm")
    barrier = pltpu.get_barrier_semaphore()
    for step in range(1, count):
        peer = lax.rem(me + step, count)
        pl.semaphore_signal(barrier, inc=1, device_id=(frame_block, peer), device_id_type=MESH)
    pl.semaphore_wait(barrier, count - 1)
    own = pltpu.make_async_copy(w_ref, out_ref.at[me], local_sem)
    own.start()
    copies = []
    for step in range(1, count):
        peer = lax.rem(me + step, count)
        copy = pltpu.make_async_remote_copy(
            src_ref=w_ref,
            dst_ref=out_ref.at[me],
            send_sem=send_sem.at[step],
            recv_sem=recv_sem.at[me],
            device_id=(frame_block, peer),
            device_id_type=MESH,
        )
        copy.start()
        copies.append(copy)
    for copy in copies:
        copy.wait_send()
    for step in range(1, count):
        source = lax.rem(me + count - step, count)
        incoming = pltpu.make_async_remote_copy(
            src_ref=w_ref,
            dst_ref=out_ref.at[source],
            send_sem=send_sem.at[step],
            recv_sem=recv_sem.at[source],
            device_id=(frame_block, source),
            device_id_type=MESH,
        )
        incoming.wait_recv()
    own.wait()


def band_gather(w):
    rows, cols = w.shape
    count = lax.axis_size("height")
    gathered = pl.pallas_call(
        band_gather_kernel,
        in_specs=[pl.BlockSpec(memory_space=pl.ANY)],
        out_specs=pl.BlockSpec(memory_space=pl.ANY),
        out_shape=jax.ShapeDtypeStruct((count, rows, cols), w.dtype),
        scratch_shapes=[
            pltpu.SemaphoreType.DMA(()),
            pltpu.SemaphoreType.DMA((count,)),
            pltpu.SemaphoreType.DMA((count,)),
        ],
        compiler_params=pltpu.CompilerParams(collective_id=0, has_side_effects=True),
    )(w)
    return gathered.reshape(count * rows, cols)


def projection_kv_kernel(x_ref, w_ref, g_ref, o_ref):
    acc = jnp.dot(x_ref[...], w_ref[...], preferred_element_type=jnp.float32)
    is_key = pl.program_id(0) < pl.num_programs(0) // 2
    for part in range(acc.shape[1] // HDIM):
        piece = acc[:, part * HDIM : (part + 1) * HDIM]
        power = jnp.mean(piece * piece, axis=-1, keepdims=True)
        scale = jnp.where(is_key, lax.rsqrt(power + EPS), jnp.float32(1.0))
        gain = jnp.where(is_key, g_ref[...], jnp.float32(1.0))
        normed = jnp.where(is_key, piece * scale * gain, piece)
        o_ref[0, :, part * HDIM : (part + 1) * HDIM] = normed.astype(o_ref.dtype)


def project_kv(x, w, start, count, gain):
    tokens, features = x.shape
    cols = PROJECT_COLS
    inner = w.shape[1] // 3
    steps = count // cols
    key_first = (inner + start) // cols
    value_first = (2 * inner + start) // cols

    def weight_block(j):
        return (0, jnp.where(j < steps, key_first + j, value_first + j - steps))

    return pl.pallas_call(
        projection_kv_kernel,
        grid=(2 * steps,),
        in_specs=[
            pl.BlockSpec((tokens, features), lambda j: (0, 0)),
            pl.BlockSpec((features, cols), weight_block),
            pl.BlockSpec((1, HDIM), lambda j: (0, 0)),
        ],
        out_specs=pl.BlockSpec((1, tokens, cols), lambda j: (j // steps, 0, j % steps)),
        out_shape=jax.ShapeDtypeStruct((2, tokens, count), jnp.bfloat16),
    )(x, w, gain.reshape(1, HDIM))


def solution(mesh):
    in_specs = (
        P("tm", "height", None, None),
        P(),
        P(),
        P(("tm", "height"), None),
        P(),
        P(),
        P(),
        P(),
    )
    out_specs = P("tm", "height", None, None)
    return jax.shard_map(
        per_device, mesh=mesh, in_specs=in_specs, out_specs=out_specs, check_vma=False
    )
```

```python
import functools

import jax
import jax.numpy as jnp
from jax import lax
from jax.sharding import PartitionSpec as P
from jax.experimental import pallas as pl
from jax.experimental.pallas import tpu as pltpu

HDIM = 128
HEADS = 12
TT = 1
TH = 2
TW = 8
GROUPS = 2


EPS = 1e-06


def with_halo(cells, sides, width):
    for axis, dim in sides:
        count = lax.axis_size(axis)
        ends = count - 1
        head = lax.slice_in_dim(cells, 0, width, axis=dim)
        tail = lax.slice_in_dim(cells, cells.shape[dim] - width, cells.shape[dim], axis=dim)
        cells = jnp.concatenate(
            [
                lax.ppermute(tail, axis, [(i, (i + 1) % count) for i in range(ends)]),
                cells,
                lax.ppermute(head, axis, [((i + 1) % count, i) for i in range(ends)]),
            ],
            axis=dim,
        )
    return cells


def modulate(tokens, mod_scale, mod_shift):
    values = tokens.astype(jnp.float32)
    mean = jnp.mean(values, axis=-1, keepdims=True)
    centred = values - mean
    variance = jnp.mean(centred * centred, axis=-1, keepdims=True)
    normed = centred * lax.rsqrt(variance + EPS)
    return (normed * (1.0 + mod_scale) + mod_shift).astype(jnp.bfloat16)


def head_norm(values, gain):
    power = jnp.mean(values * values, axis=-1, keepdims=True)
    return (values * lax.rsqrt(power + EPS) * gain).astype(jnp.bfloat16)


def tile_coords(frames, rows, width):
    shape = (frames.shape[0], rows.shape[0], width)
    columns = jnp.arange(width, dtype=jnp.int32)
    frame_tiles = jnp.broadcast_to((frames // TT)[:, None, None], shape).reshape(-1)
    row_tiles = jnp.broadcast_to((rows // TH)[None, :, None], shape).reshape(-1)
    column_tiles = jnp.broadcast_to((columns // TW)[None, None, :], shape).reshape(-1)
    return (frame_tiles, row_tiles, column_tiles)


def per_device(tokens, mod_scale, mod_shift, w_qkv, q_gain, k_gain, window, valid):
    frame_count, row_count, width, features = tokens.shape
    token_count = frame_count * row_count * width
    modulated = modulate(tokens.reshape(token_count, features), mod_scale, mod_shift)
    band_weight = band_gather(w_qkv)
    full_weight = lax.all_gather(band_weight, "tm", axis=0, tiled=True)
    inner = full_weight.shape[1] // 3
    group_cols = inner // GROUPS
    tiled = (frame_count // TT, TT, row_count // TH, TH, width, group_cols)
    groups = []
    for group in range(GROUPS):
        start = group * group_cols
        stacked = project_kv(modulated, full_weight, start, group_cols, k_gain)
        stacked = stacked.reshape(2, *tiled)
        rows_done = with_halo(stacked, (("height", 3),), 1)
        rows_done = rows_done.reshape(2, frame_count, row_count + 2 * TH, width, group_cols)
        count = lax.axis_size("tm")
        before = lax.ppermute(
            rows_done[:, frame_count - TT :], "tm", [(i, i + 1) for i in range(count - 1)]
        )
        after = lax.ppermute(rows_done[:, :TT], "tm", [(i + 1, i) for i in range(count - 1)])
        groups.append((rows_done, before, after))
    query = project(modulated, full_weight, 0, inner, q_gain)
    frames_ext = frame_count + 2 * TT
    rows_ext = row_count + 2 * TH
    frame_block = lax.axis_index("tm")
    row_block = lax.axis_index("height")
    first_frame = frame_block * frame_count
    first_row = row_block * row_count
    zero = jnp.int32(0)
    valid_pad = jnp.pad(valid, ((TT, TT), (TH, TH), (0, 0)))
    key_valid = lax.dynamic_slice(
        valid_pad, (first_frame, first_row, zero), (frames_ext, rows_ext, width)
    )
    query_valid = lax.dynamic_slice(
        valid, (first_frame, first_row, zero), (frame_count, row_count, width)
    )
    row_tiles = row_count // TH
    blocks = frame_count * row_tiles
    span_t = 2 * TT + 1
    span_h = 3 * TH
    query_n = TH * width
    key_n = span_t * span_h * width
    block_valid = jnp.stack(
        [
            key_valid[f : f + span_t, TH * rt : TH * rt + span_h].reshape(-1)
            for f in range(frame_count)
            for rt in range(row_tiles)
        ]
    )
    apart_t = jnp.abs(jnp.arange(span_t, dtype=jnp.int32) - TT)
    apart_h = jnp.abs(jnp.arange(span_h, dtype=jnp.int32) // TH - 1)
    near = (apart_t[None, :, None, None] <= window[:, 0, None, None, None]) & (
        apart_h[None, None, :, None] <= window[:, 1, None, None, None]
    )
    near = jnp.broadcast_to(near, (HEADS, span_t, span_h, width)).reshape(HEADS, 1, key_n)
    key_mask = (near & (block_valid[None] > 0)).astype(jnp.float32).reshape(HEADS, blocks, 1, key_n)
    column_tiles = jnp.arange(width, dtype=jnp.int32) // TW
    key_cols = jnp.tile(column_tiles, span_t * span_h).reshape(1, key_n)
    query_cols = jnp.tile(column_tiles, TH)
    query_lo = (query_cols[None, :] - window[:, 2, None]).reshape(HEADS, query_n, 1)
    query_hi = (query_cols[None, :] + window[:, 2, None]).reshape(HEADS, query_n, 1)
    query_ok = query_valid.reshape(blocks, query_n, 1).astype(jnp.float32)
    query_grid = query.reshape(frame_count, row_count, width, inner)
    assert frame_count == 2 * TT
    mask_rows = key_mask.reshape(HEADS, blocks, span_t, span_h, width)
    halo_masks, own_masks = [], []
    for block in range(blocks):
        first_frame_block = block // row_tiles == 0
        halo_frames = slice(0, TT) if first_frame_block else slice(span_t - TT, span_t)
        own_frames = slice(TT, span_t) if first_frame_block else slice(0, frame_count)
        halo_masks.append(mask_rows[:, block, halo_frames].reshape(HEADS, 1, -1))
        own_masks.append(mask_rows[:, block, own_frames].reshape(HEADS, 1, -1))
    halo_mask = jnp.stack(halo_masks, axis=1)
    own_mask = jnp.stack(own_masks, axis=1)
    halo_cols = jnp.tile(column_tiles, TT * span_h).reshape(1, -1)
    own_cols = jnp.tile(column_tiles, frame_count * span_h).reshape(1, -1)
    out = None
    for group, pieces in enumerate(groups):
        masks = (halo_mask, own_mask, query_lo, query_hi, halo_cols, own_cols, query_ok)
        out = tile_attention(query_grid, pieces, masks, group, out)
    return out


def attention_kernel(
    q_ref, mk_ref, mv_ref, tk_ref, tv_ref, bk_ref, bv_ref,
    hm_ref, om_ref, lo_ref, hi_ref, hc_ref, oc_ref, qv_ref, o_ref,
):
    span_h = 3 * TH
    width = q_ref.shape[2]
    scale = 1.0 / float(HDIM) ** 0.5
    halo_ok = (hc_ref[...] >= lo_ref[0]) & (hc_ref[...] <= hi_ref[0])
    own_ok = (oc_ref[...] >= lo_ref[0]) & (oc_ref[...] <= hi_ref[0])
    for block in range(q_ref.shape[0] * ROW_TILES):
        frame, tile = divmod(block, ROW_TILES)
        row = tile * TH
        hk_ref, hv_ref = (tk_ref, tv_ref) if frame == 0 else (bk_ref, bv_ref)
        query = q_ref[frame, row : row + TH].reshape(TH * width, HDIM)
        pieces = (
            (hk_ref, hv_ref, halo_ok & (hm_ref[0, block] > 0.0)),
            (mk_ref, mv_ref, own_ok & (om_ref[0, block] > 0.0)),
        )
        terms, values = [], []
        for k_ref, v_ref, allowed in pieces:
            key = k_ref[0, :, row : row + span_h].reshape(-1, HDIM)
            values.append(v_ref[0, :, row : row + span_h].reshape(-1, HDIM))
            scores = lax.dot_general(
                query, key, (((1,), (1,)), ((), ())), preferred_element_type=jnp.float32
            ) * scale
            terms.append(jnp.where(allowed, jnp.exp(scores), jnp.float32(0.0)))
        total = jnp.sum(terms[0], axis=-1, keepdims=True) + jnp.sum(terms[1], axis=-1, keepdims=True)
        seen = qv_ref[block] > 0.0
        inverse = 1.0 / jnp.where(seen, total, jnp.float32(1.0))
        result = jnp.dot(
            (terms[0] * inverse).astype(jnp.bfloat16), values[0], preferred_element_type=jnp.float32
        ) + jnp.dot(
            (terms[1] * inverse).astype(jnp.bfloat16), values[1], preferred_element_type=jnp.float32
        )
        result = jnp.where(seen, result, jnp.float32(0.0)).astype(jnp.bfloat16)
        o_ref[frame, row : row + TH] = result.reshape(TH, width, HDIM)


ROW_TILES = 2


def tile_attention(query, pieces, masks, group, out):
    frames, rows, width, inner = query.shape
    middle, top, bottom = pieces
    heads = middle.shape[-1] // HDIM
    first = group * heads
    assert rows // TH == ROW_TILES
    blocks = frames * ROW_TILES
    halo_mask, own_mask, query_lo, query_hi, halo_cols, own_cols, query_ok = masks
    query_n = TH * width
    q_spec = pl.BlockSpec((frames, rows, width, HDIM), lambda h: (0, 0, 0, first + h))

    def piece_specs(piece):
        shape = (1, *piece.shape[1:-1], HDIM)
        return [
            pl.BlockSpec(shape, lambda h: (0, 0, 0, 0, h)),
            pl.BlockSpec(shape, lambda h: (1, 0, 0, 0, h)),
        ]

    in_specs = [q_spec] + piece_specs(middle) + piece_specs(top) + piece_specs(bottom) + [
        pl.BlockSpec((1, blocks, 1, halo_mask.shape[-1]), lambda h: (first + h, 0, 0, 0)),
        pl.BlockSpec((1, blocks, 1, own_mask.shape[-1]), lambda h: (first + h, 0, 0, 0)),
        pl.BlockSpec((1, query_n, 1), lambda h: (first + h, 0, 0)),
        pl.BlockSpec((1, query_n, 1), lambda h: (first + h, 0, 0)),
        pl.BlockSpec((1, halo_cols.shape[-1]), lambda h: (0, 0)),
        pl.BlockSpec((1, own_cols.shape[-1]), lambda h: (0, 0)),
        pl.BlockSpec((blocks, query_n, 1), lambda h: (0, 0, 0)),
    ]
    operands = [query, middle, middle, top, top, bottom, bottom, halo_mask, own_mask,
                query_lo, query_hi, halo_cols, own_cols, query_ok]
    aliases = {}
    kernel = attention_kernel
    if out is not None:
        count = len(operands)
        in_specs.append(pl.BlockSpec(memory_space=pl.ANY))
        operands.append(out)
        aliases = {count: 0}
        kernel = lambda *refs: attention_kernel(*refs[:count], refs[count + 1])
    return pl.pallas_call(
        kernel,
        grid=(heads,),
        in_specs=in_specs,
        out_specs=q_spec,
        out_shape=jax.ShapeDtypeStruct(query.shape, jnp.bfloat16),
        input_output_aliases=aliases,
    )(*operands)


PROJECT_COLS = 256


def projection_kernel(x_ref, w_ref, g_ref, o_ref, *, normalize):
    acc = jnp.dot(x_ref[...], w_ref[...], preferred_element_type=jnp.float32)
    for part in range(acc.shape[1] // HDIM):
        piece = acc[:, part * HDIM : (part + 1) * HDIM]
        if normalize:
            power = jnp.mean(piece * piece, axis=-1, keepdims=True)
            piece = piece * lax.rsqrt(power + EPS) * g_ref[...]
        o_ref[:, part * HDIM : (part + 1) * HDIM] = piece.astype(o_ref.dtype)


def project(x, w, start, count, gain):
    tokens, features = x.shape
    cols = PROJECT_COLS
    normalize = gain is not None
    gain = gain.reshape(1, HDIM) if normalize else jnp.ones((1, HDIM), jnp.float32)
    first = start // cols
    return pl.pallas_call(
        functools.partial(projection_kernel, normalize=normalize),
        grid=(count // cols,),
        in_specs=[
            pl.BlockSpec((tokens, features), lambda j: (0, 0)),
            pl.BlockSpec((features, cols), lambda j: (0, first + j)),
            pl.BlockSpec((1, HDIM), lambda j: (0, 0)),
        ],
        out_specs=pl.BlockSpec((tokens, cols), lambda j: (0, j)),
        out_shape=jax.ShapeDtypeStruct((tokens, count), jnp.bfloat16),
    )(x, w, gain)


MESH = pl.DeviceIdType.MESH


def band_gather_kernel(w_ref, out_ref, local_sem, send_sem, recv_sem):
    count = lax.axis_size("height")
    me = lax.axis_index("height")
    frame_block = lax.axis_index("tm")
    barrier = pltpu.get_barrier_semaphore()
    for step in range(1, count):
        peer = lax.rem(me + step, count)
        pl.semaphore_signal(barrier, inc=1, device_id=(frame_block, peer), device_id_type=MESH)
    pl.semaphore_wait(barrier, count - 1)
    own = pltpu.make_async_copy(w_ref, out_ref.at[me], local_sem)
    own.start()
    copies = []
    for step in range(1, count):
        peer = lax.rem(me + step, count)
        copy = pltpu.make_async_remote_copy(
            src_ref=w_ref,
            dst_ref=out_ref.at[me],
            send_sem=send_sem.at[step],
            recv_sem=recv_sem.at[me],
            device_id=(frame_block, peer),
            device_id_type=MESH,
        )
        copy.start()
        copies.append(copy)
    for copy in copies:
        copy.wait_send()
    for step in range(1, count):
        source = lax.rem(me + count - step, count)
        incoming = pltpu.make_async_remote_copy(
            src_ref=w_ref,
            dst_ref=out_ref.at[source],
            send_sem=send_sem.at[step],
            recv_sem=recv_sem.at[source],
            device_id=(frame_block, source),
            device_id_type=MESH,
        )
        incoming.wait_recv()
    own.wait()


def band_gather(w):
    rows, cols = w.shape
    count = lax.axis_size("height")
    gathered = pl.pallas_call(
        band_gather_kernel,
        in_specs=[pl.BlockSpec(memory_space=pl.ANY)],
        out_specs=pl.BlockSpec(memory_space=pl.ANY),
        out_shape=jax.ShapeDtypeStruct((count, rows, cols), w.dtype),
        scratch_shapes=[
            pltpu.SemaphoreType.DMA(()),
            pltpu.SemaphoreType.DMA((count,)),
            pltpu.SemaphoreType.DMA((count,)),
        ],
        compiler_params=pltpu.CompilerParams(collective_id=0, has_side_effects=True),
    )(w)
    return gathered.reshape(count * rows, cols)


def projection_kv_kernel(x_ref, w_ref, g_ref, o_ref):
    acc = jnp.dot(x_ref[...], w_ref[...], preferred_element_type=jnp.float32)
    is_key = pl.program_id(0) < pl.num_programs(0) // 2
    for part in range(acc.shape[1] // HDIM):
        piece = acc[:, part * HDIM : (part + 1) * HDIM]
        power = jnp.mean(piece * piece, axis=-1, keepdims=True)
        scale = jnp.where(is_key, lax.rsqrt(power + EPS), jnp.float32(1.0))
        gain = jnp.where(is_key, g_ref[...], jnp.float32(1.0))
        normed = jnp.where(is_key, piece * scale * gain, piece)
        o_ref[0, :, part * HDIM : (part + 1) * HDIM] = normed.astype(o_ref.dtype)


def project_kv(x, w, start, count, gain):
    tokens, features = x.shape
    cols = PROJECT_COLS
    inner = w.shape[1] // 3
    steps = count // cols
    key_first = (inner + start) // cols
    value_first = (2 * inner + start) // cols

    def weight_block(j):
        return (0, jnp.where(j < steps, key_first + j, value_first + j - steps))

    return pl.pallas_call(
        projection_kv_kernel,
        grid=(2 * steps,),
        in_specs=[
            pl.BlockSpec((tokens, features), lambda j: (0, 0)),
            pl.BlockSpec((features, cols), weight_block),
            pl.BlockSpec((1, HDIM), lambda j: (0, 0)),
        ],
        out_specs=pl.BlockSpec((1, tokens, cols), lambda j: (j // steps, 0, j % steps)),
        out_shape=jax.ShapeDtypeStruct((2, tokens, count), jnp.bfloat16),
    )(x, w, gain.reshape(1, HDIM))


def solution(mesh):
    in_specs = (
        P("tm", "height", None, None),
        P(),
        P(),
        P(("tm", "height"), None),
        P(),
        P(),
        P(),
        P(),
    )
    out_specs = P("tm", "height", None, None)
    return jax.shard_map(
        per_device, mesh=mesh, in_specs=in_specs, out_specs=out_specs, check_vma=False
    )
```

```python
import functools

import jax
import jax.numpy as jnp
from jax import lax
from jax.sharding import PartitionSpec as P
from jax.experimental import pallas as pl
from jax.experimental.pallas import tpu as pltpu

HDIM = 128
HEADS = 12
TT = 1
TH = 2
TW = 8
GROUPS = 2


EPS = 1e-06


def with_halo(cells, sides, width):
    for axis, dim in sides:
        count = lax.axis_size(axis)
        ends = count - 1
        head = lax.slice_in_dim(cells, 0, width, axis=dim)
        tail = lax.slice_in_dim(cells, cells.shape[dim] - width, cells.shape[dim], axis=dim)
        cells = jnp.concatenate(
            [
                lax.ppermute(tail, axis, [(i, (i + 1) % count) for i in range(ends)]),
                cells,
                lax.ppermute(head, axis, [((i + 1) % count, i) for i in range(ends)]),
            ],
            axis=dim,
        )
    return cells


def modulate(tokens, mod_scale, mod_shift):
    values = tokens.astype(jnp.float32)
    mean = jnp.mean(values, axis=-1, keepdims=True)
    centred = values - mean
    variance = jnp.mean(centred * centred, axis=-1, keepdims=True)
    normed = centred * lax.rsqrt(variance + EPS)
    return (normed * (1.0 + mod_scale) + mod_shift).astype(jnp.bfloat16)


def head_norm(values, gain):
    power = jnp.mean(values * values, axis=-1, keepdims=True)
    return (values * lax.rsqrt(power + EPS) * gain).astype(jnp.bfloat16)


def tile_coords(frames, rows, width):
    shape = (frames.shape[0], rows.shape[0], width)
    columns = jnp.arange(width, dtype=jnp.int32)
    frame_tiles = jnp.broadcast_to((frames // TT)[:, None, None], shape).reshape(-1)
    row_tiles = jnp.broadcast_to((rows // TH)[None, :, None], shape).reshape(-1)
    column_tiles = jnp.broadcast_to((columns // TW)[None, None, :], shape).reshape(-1)
    return (frame_tiles, row_tiles, column_tiles)


def per_device(tokens, mod_scale, mod_shift, w_qkv, q_gain, k_gain, window, valid):
    frame_count, row_count, width, features = tokens.shape
    token_count = frame_count * row_count * width
    modulated = modulate(tokens.reshape(token_count, features), mod_scale, mod_shift)
    band_weight = band_gather(w_qkv)
    full_weight = lax.all_gather(band_weight, "tm", axis=0, tiled=True)
    inner = full_weight.shape[1] // 3
    group_cols = inner // GROUPS
    tiled = (frame_count // TT, TT, row_count // TH, TH, width, group_cols)
    groups = []
    queries = []
    for group in range(GROUPS):
        start = group * group_cols
        projected = project_qkv(modulated, full_weight, start, group_cols, q_gain, k_gain)
        queries.append(projected[0].reshape(frame_count, row_count, width, group_cols))
        stacked = projected[1:].reshape(2, *tiled)
        rows_done = with_halo(stacked, (("height", 3),), 1)
        rows_done = rows_done.reshape(2, frame_count, row_count + 2 * TH, width, group_cols)
        count = lax.axis_size("tm")
        before = lax.ppermute(
            rows_done[:, frame_count - TT :], "tm", [(i, i + 1) for i in range(count - 1)]
        )
        after = lax.ppermute(rows_done[:, :TT], "tm", [(i + 1, i) for i in range(count - 1)])
        groups.append((rows_done, before, after))
    frames_ext = frame_count + 2 * TT
    rows_ext = row_count + 2 * TH
    frame_block = lax.axis_index("tm")
    row_block = lax.axis_index("height")
    first_frame = frame_block * frame_count
    first_row = row_block * row_count
    zero = jnp.int32(0)
    valid_pad = jnp.pad(valid, ((TT, TT), (TH, TH), (0, 0)))
    key_valid = lax.dynamic_slice(
        valid_pad, (first_frame, first_row, zero), (frames_ext, rows_ext, width)
    )
    query_valid = lax.dynamic_slice(
        valid, (first_frame, first_row, zero), (frame_count, row_count, width)
    )
    row_tiles = row_count // TH
    blocks = frame_count * row_tiles
    span_t = 2 * TT + 1
    span_h = 3 * TH
    query_n = TH * width
    key_n = span_t * span_h * width
    block_valid = jnp.stack(
        [
            key_valid[f : f + span_t, TH * rt : TH * rt + span_h].reshape(-1)
            for f in range(frame_count)
            for rt in range(row_tiles)
        ]
    )
    apart_t = jnp.abs(jnp.arange(span_t, dtype=jnp.int32) - TT)
    apart_h = jnp.abs(jnp.arange(span_h, dtype=jnp.int32) // TH - 1)
    near = (apart_t[None, :, None, None] <= window[:, 0, None, None, None]) & (
        apart_h[None, None, :, None] <= window[:, 1, None, None, None]
    )
    near = jnp.broadcast_to(near, (HEADS, span_t, span_h, width)).reshape(HEADS, 1, key_n)
    key_mask = (near & (block_valid[None] > 0)).astype(jnp.float32).reshape(HEADS, blocks, 1, key_n)
    column_tiles = jnp.arange(width, dtype=jnp.int32) // TW
    key_cols = jnp.tile(column_tiles, span_t * span_h).reshape(1, key_n)
    query_cols = jnp.tile(column_tiles, TH)
    query_lo = (query_cols[None, :] - window[:, 2, None]).reshape(HEADS, query_n, 1)
    query_hi = (query_cols[None, :] + window[:, 2, None]).reshape(HEADS, query_n, 1)
    query_ok = query_valid.reshape(blocks, query_n, 1).astype(jnp.float32)
    assert frame_count == 2 * TT
    mask_rows = key_mask.reshape(HEADS, blocks, span_t, span_h, width)
    halo_masks, own_masks = [], []
    for block in range(blocks):
        first_frame_block = block // row_tiles == 0
        halo_frames = slice(0, TT) if first_frame_block else slice(span_t - TT, span_t)
        own_frames = slice(TT, span_t) if first_frame_block else slice(0, frame_count)
        halo_masks.append(mask_rows[:, block, halo_frames].reshape(HEADS, 1, -1))
        own_masks.append(mask_rows[:, block, own_frames].reshape(HEADS, 1, -1))
    halo_mask = jnp.stack(halo_masks, axis=1)
    own_mask = jnp.stack(own_masks, axis=1)
    halo_cols = jnp.tile(column_tiles, TT * span_h).reshape(1, -1)
    own_cols = jnp.tile(column_tiles, frame_count * span_h).reshape(1, -1)
    out = None
    for group, pieces in enumerate(groups):
        masks = (halo_mask, own_mask, query_lo, query_hi, halo_cols, own_cols, query_ok)
        out = tile_attention(queries[group], pieces, masks, group, out)
    return out


def attention_kernel(
    q_ref, mk_ref, mv_ref, tk_ref, tv_ref, bk_ref, bv_ref,
    hm_ref, om_ref, lo_ref, hi_ref, hc_ref, oc_ref, qv_ref, o_ref,
):
    span_h = 3 * TH
    width = q_ref.shape[2]
    scale = 1.0 / float(HDIM) ** 0.5
    halo_ok = (hc_ref[...] >= lo_ref[0]) & (hc_ref[...] <= hi_ref[0])
    own_ok = (oc_ref[...] >= lo_ref[0]) & (oc_ref[...] <= hi_ref[0])
    for block in range(q_ref.shape[0] * ROW_TILES):
        frame, tile = divmod(block, ROW_TILES)
        row = tile * TH
        hk_ref, hv_ref = (tk_ref, tv_ref) if frame == 0 else (bk_ref, bv_ref)
        query = q_ref[frame, row : row + TH].reshape(TH * width, HDIM)
        pieces = (
            (hk_ref, hv_ref, halo_ok & (hm_ref[0, block] > 0.0)),
            (mk_ref, mv_ref, own_ok & (om_ref[0, block] > 0.0)),
        )
        terms, values = [], []
        for k_ref, v_ref, allowed in pieces:
            key = k_ref[0, :, row : row + span_h].reshape(-1, HDIM)
            values.append(v_ref[0, :, row : row + span_h].reshape(-1, HDIM))
            scores = lax.dot_general(
                query, key, (((1,), (1,)), ((), ())), preferred_element_type=jnp.float32
            ) * scale
            terms.append(jnp.where(allowed, jnp.exp(scores), jnp.float32(0.0)))
        total = jnp.sum(terms[0], axis=-1, keepdims=True) + jnp.sum(terms[1], axis=-1, keepdims=True)
        seen = qv_ref[block] > 0.0
        inverse = 1.0 / jnp.where(seen, total, jnp.float32(1.0))
        result = jnp.dot(
            (terms[0] * inverse).astype(jnp.bfloat16), values[0], preferred_element_type=jnp.float32
        ) + jnp.dot(
            (terms[1] * inverse).astype(jnp.bfloat16), values[1], preferred_element_type=jnp.float32
        )
        result = jnp.where(seen, result, jnp.float32(0.0)).astype(jnp.bfloat16)
        o_ref[frame, row : row + TH] = result.reshape(TH, width, HDIM)


ROW_TILES = 2


def tile_attention(query, pieces, masks, group, out):
    frames, rows, width, group_cols = query.shape
    middle, top, bottom = pieces
    heads = group_cols // HDIM
    out_shape = (frames, rows, width, masks[2].shape[0] * HDIM)
    first = group * heads
    assert rows // TH == ROW_TILES
    blocks = frames * ROW_TILES
    halo_mask, own_mask, query_lo, query_hi, halo_cols, own_cols, query_ok = masks
    query_n = TH * width
    q_spec = pl.BlockSpec((frames, rows, width, HDIM), lambda h: (0, 0, 0, h))
    o_spec = pl.BlockSpec((frames, rows, width, HDIM), lambda h: (0, 0, 0, first + h))

    def piece_specs(piece):
        shape = (1, *piece.shape[1:-1], HDIM)
        return [
            pl.BlockSpec(shape, lambda h: (0, 0, 0, 0, h)),
            pl.BlockSpec(shape, lambda h: (1, 0, 0, 0, h)),
        ]

    in_specs = [q_spec] + piece_specs(middle) + piece_specs(top) + piece_specs(bottom) + [
        pl.BlockSpec((1, blocks, 1, halo_mask.shape[-1]), lambda h: (first + h, 0, 0, 0)),
        pl.BlockSpec((1, blocks, 1, own_mask.shape[-1]), lambda h: (first + h, 0, 0, 0)),
        pl.BlockSpec((1, query_n, 1), lambda h: (first + h, 0, 0)),
        pl.BlockSpec((1, query_n, 1), lambda h: (first + h, 0, 0)),
        pl.BlockSpec((1, halo_cols.shape[-1]), lambda h: (0, 0)),
        pl.BlockSpec((1, own_cols.shape[-1]), lambda h: (0, 0)),
        pl.BlockSpec((blocks, query_n, 1), lambda h: (0, 0, 0)),
    ]
    operands = [query, middle, middle, top, top, bottom, bottom, halo_mask, own_mask,
                query_lo, query_hi, halo_cols, own_cols, query_ok]
    aliases = {}
    kernel = attention_kernel
    if out is not None:
        count = len(operands)
        in_specs.append(pl.BlockSpec(memory_space=pl.ANY))
        operands.append(out)
        aliases = {count: 0}
        kernel = lambda *refs: attention_kernel(*refs[:count], refs[count + 1])
    return pl.pallas_call(
        kernel,
        grid=(heads,),
        in_specs=in_specs,
        out_specs=o_spec,
        out_shape=jax.ShapeDtypeStruct(out_shape, jnp.bfloat16),
        input_output_aliases=aliases,
    )(*operands)


PROJECT_COLS = 256


def projection_kernel(x_ref, w_ref, g_ref, o_ref, *, normalize):
    acc = jnp.dot(x_ref[...], w_ref[...], preferred_element_type=jnp.float32)
    for part in range(acc.shape[1] // HDIM):
        piece = acc[:, part * HDIM : (part + 1) * HDIM]
        if normalize:
            power = jnp.mean(piece * piece, axis=-1, keepdims=True)
            piece = piece * lax.rsqrt(power + EPS) * g_ref[...]
        o_ref[:, part * HDIM : (part + 1) * HDIM] = piece.astype(o_ref.dtype)


def project(x, w, start, count, gain):
    tokens, features = x.shape
    cols = PROJECT_COLS
    normalize = gain is not None
    gain = gain.reshape(1, HDIM) if normalize else jnp.ones((1, HDIM), jnp.float32)
    first = start // cols
    return pl.pallas_call(
        functools.partial(projection_kernel, normalize=normalize),
        grid=(count // cols,),
        in_specs=[
            pl.BlockSpec((tokens, features), lambda j: (0, 0)),
            pl.BlockSpec((features, cols), lambda j: (0, first + j)),
            pl.BlockSpec((1, HDIM), lambda j: (0, 0)),
        ],
        out_specs=pl.BlockSpec((tokens, cols), lambda j: (0, j)),
        out_shape=jax.ShapeDtypeStruct((tokens, count), jnp.bfloat16),
    )(x, w, gain)


MESH = pl.DeviceIdType.MESH


def band_gather_kernel(w_ref, out_ref, local_sem, send_sem, recv_sem):
    count = lax.axis_size("height")
    me = lax.axis_index("height")
    frame_block = lax.axis_index("tm")
    barrier = pltpu.get_barrier_semaphore()
    for step in range(1, count):
        peer = lax.rem(me + step, count)
        pl.semaphore_signal(barrier, inc=1, device_id=(frame_block, peer), device_id_type=MESH)
    pl.semaphore_wait(barrier, count - 1)
    own = pltpu.make_async_copy(w_ref, out_ref.at[me], local_sem)
    own.start()
    copies = []
    for step in range(1, count):
        peer = lax.rem(me + step, count)
        copy = pltpu.make_async_remote_copy(
            src_ref=w_ref,
            dst_ref=out_ref.at[me],
            send_sem=send_sem.at[step],
            recv_sem=recv_sem.at[me],
            device_id=(frame_block, peer),
            device_id_type=MESH,
        )
        copy.start()
        copies.append(copy)
    for copy in copies:
        copy.wait_send()
    for step in range(1, count):
        source = lax.rem(me + count - step, count)
        incoming = pltpu.make_async_remote_copy(
            src_ref=w_ref,
            dst_ref=out_ref.at[source],
            send_sem=send_sem.at[step],
            recv_sem=recv_sem.at[source],
            device_id=(frame_block, source),
            device_id_type=MESH,
        )
        incoming.wait_recv()
    own.wait()


def band_gather(w):
    rows, cols = w.shape
    count = lax.axis_size("height")
    gathered = pl.pallas_call(
        band_gather_kernel,
        in_specs=[pl.BlockSpec(memory_space=pl.ANY)],
        out_specs=pl.BlockSpec(memory_space=pl.ANY),
        out_shape=jax.ShapeDtypeStruct((count, rows, cols), w.dtype),
        scratch_shapes=[
            pltpu.SemaphoreType.DMA(()),
            pltpu.SemaphoreType.DMA((count,)),
            pltpu.SemaphoreType.DMA((count,)),
        ],
        compiler_params=pltpu.CompilerParams(collective_id=0, has_side_effects=True),
    )(w)
    return gathered.reshape(count * rows, cols)


def projection_kv_kernel(x_ref, w_ref, g_ref, o_ref):
    acc = jnp.dot(x_ref[...], w_ref[...], preferred_element_type=jnp.float32)
    is_key = pl.program_id(0) < pl.num_programs(0) // 2
    for part in range(acc.shape[1] // HDIM):
        piece = acc[:, part * HDIM : (part + 1) * HDIM]
        power = jnp.mean(piece * piece, axis=-1, keepdims=True)
        scale = jnp.where(is_key, lax.rsqrt(power + EPS), jnp.float32(1.0))
        gain = jnp.where(is_key, g_ref[...], jnp.float32(1.0))
        normed = jnp.where(is_key, piece * scale * gain, piece)
        o_ref[0, :, part * HDIM : (part + 1) * HDIM] = normed.astype(o_ref.dtype)


def project_kv(x, w, start, count, gain):
    tokens, features = x.shape
    cols = PROJECT_COLS
    inner = w.shape[1] // 3
    steps = count // cols
    key_first = (inner + start) // cols
    value_first = (2 * inner + start) // cols

    def weight_block(j):
        return (0, jnp.where(j < steps, key_first + j, value_first + j - steps))

    return pl.pallas_call(
        projection_kv_kernel,
        grid=(2 * steps,),
        in_specs=[
            pl.BlockSpec((tokens, features), lambda j: (0, 0)),
            pl.BlockSpec((features, cols), weight_block),
            pl.BlockSpec((1, HDIM), lambda j: (0, 0)),
        ],
        out_specs=pl.BlockSpec((1, tokens, cols), lambda j: (j // steps, 0, j % steps)),
        out_shape=jax.ShapeDtypeStruct((2, tokens, count), jnp.bfloat16),
    )(x, w, gain.reshape(1, HDIM))


def projection_qkv_kernel(x_ref, w_ref, qg_ref, kg_ref, o_ref):
    acc = jnp.dot(x_ref[...], w_ref[...], preferred_element_type=jnp.float32)
    third = pl.program_id(0) // (pl.num_programs(0) // 3)
    normalize = third < 2
    gain = jnp.where(third == 0, qg_ref[...], kg_ref[...])
    for part in range(acc.shape[1] // HDIM):
        piece = acc[:, part * HDIM : (part + 1) * HDIM]
        power = jnp.mean(piece * piece, axis=-1, keepdims=True)
        normed = jnp.where(normalize, piece * lax.rsqrt(power + EPS) * gain, piece)
        o_ref[0, :, part * HDIM : (part + 1) * HDIM] = normed.astype(o_ref.dtype)


def project_qkv(x, w, start, count, q_gain, k_gain):
    tokens, features = x.shape
    cols = PROJECT_COLS
    inner = w.shape[1] // 3
    steps = count // cols

    def weight_block(j):
        return (0, (j // steps) * (inner // cols) + start // cols + j % steps)

    return pl.pallas_call(
        projection_qkv_kernel,
        grid=(3 * steps,),
        in_specs=[
            pl.BlockSpec((tokens, features), lambda j: (0, 0)),
            pl.BlockSpec((features, cols), weight_block),
            pl.BlockSpec((1, HDIM), lambda j: (0, 0)),
            pl.BlockSpec((1, HDIM), lambda j: (0, 0)),
        ],
        out_specs=pl.BlockSpec((1, tokens, cols), lambda j: (j // steps, 0, j % steps)),
        out_shape=jax.ShapeDtypeStruct((3, tokens, count), jnp.bfloat16),
    )(x, w, q_gain.reshape(1, HDIM), k_gain.reshape(1, HDIM))


def solution(mesh):
    in_specs = (
        P("tm", "height", None, None),
        P(),
        P(),
        P(("tm", "height"), None),
        P(),
        P(),
        P(),
        P(),
    )
    out_specs = P("tm", "height", None, None)
    return jax.shard_map(
        per_device, mesh=mesh, in_specs=in_specs, out_specs=out_specs, check_vma=False
    )
```

```python
import functools

import jax
import jax.numpy as jnp
from jax import lax
from jax.sharding import PartitionSpec as P
from jax.experimental import pallas as pl
from jax.experimental.pallas import tpu as pltpu

HDIM = 128
HEADS = 12
TT = 1
TH = 2
TW = 8
GROUPS = 2


EPS = 1e-06


def with_halo(cells, sides, width):
    for axis, dim in sides:
        count = lax.axis_size(axis)
        ends = count - 1
        head = lax.slice_in_dim(cells, 0, width, axis=dim)
        tail = lax.slice_in_dim(cells, cells.shape[dim] - width, cells.shape[dim], axis=dim)
        cells = jnp.concatenate(
            [
                lax.ppermute(tail, axis, [(i, (i + 1) % count) for i in range(ends)]),
                cells,
                lax.ppermute(head, axis, [((i + 1) % count, i) for i in range(ends)]),
            ],
            axis=dim,
        )
    return cells


def modulate(tokens, mod_scale, mod_shift):
    values = tokens.astype(jnp.float32)
    mean = jnp.mean(values, axis=-1, keepdims=True)
    centred = values - mean
    variance = jnp.mean(centred * centred, axis=-1, keepdims=True)
    normed = centred * lax.rsqrt(variance + EPS)
    return (normed * (1.0 + mod_scale) + mod_shift).astype(jnp.bfloat16)


def head_norm(values, gain):
    power = jnp.mean(values * values, axis=-1, keepdims=True)
    return (values * lax.rsqrt(power + EPS) * gain).astype(jnp.bfloat16)


def tile_coords(frames, rows, width):
    shape = (frames.shape[0], rows.shape[0], width)
    columns = jnp.arange(width, dtype=jnp.int32)
    frame_tiles = jnp.broadcast_to((frames // TT)[:, None, None], shape).reshape(-1)
    row_tiles = jnp.broadcast_to((rows // TH)[None, :, None], shape).reshape(-1)
    column_tiles = jnp.broadcast_to((columns // TW)[None, None, :], shape).reshape(-1)
    return (frame_tiles, row_tiles, column_tiles)


def per_device(tokens, mod_scale, mod_shift, w_qkv, q_gain, k_gain, window, valid):
    frame_count, row_count, width, features = tokens.shape
    token_count = frame_count * row_count * width
    modulated = modulate(tokens.reshape(token_count, features), mod_scale, mod_shift)
    band_weight = band_gather(w_qkv)
    full_weight = lax.all_gather(band_weight, "tm", axis=0, tiled=True)
    inner = full_weight.shape[1] // 3
    group_cols = inner // GROUPS
    tiled = (frame_count // TT, TT, row_count // TH, TH, width, group_cols)
    groups = []
    for group in range(GROUPS):
        start = group * group_cols
        stacked = project_kv(modulated, full_weight, start, group_cols, k_gain)
        stacked = stacked.reshape(2, *tiled)
        rows_done = with_halo(stacked, (("height", 3),), 1)
        rows_done = rows_done.reshape(2, frame_count, row_count + 2 * TH, width, group_cols)
        count = lax.axis_size("tm")
        before = lax.ppermute(
            rows_done[:, frame_count - TT :], "tm", [(i, i + 1) for i in range(count - 1)]
        )
        after = lax.ppermute(rows_done[:, :TT], "tm", [(i + 1, i) for i in range(count - 1)])
        groups.append((rows_done, before, after))
    frames_ext = frame_count + 2 * TT
    rows_ext = row_count + 2 * TH
    frame_block = lax.axis_index("tm")
    row_block = lax.axis_index("height")
    first_frame = frame_block * frame_count
    first_row = row_block * row_count
    zero = jnp.int32(0)
    valid_pad = jnp.pad(valid, ((TT, TT), (TH, TH), (0, 0)))
    key_valid = lax.dynamic_slice(
        valid_pad, (first_frame, first_row, zero), (frames_ext, rows_ext, width)
    )
    query_valid = lax.dynamic_slice(
        valid, (first_frame, first_row, zero), (frame_count, row_count, width)
    )
    row_tiles = row_count // TH
    blocks = frame_count * row_tiles
    span_t = 2 * TT + 1
    span_h = 3 * TH
    query_n = TH * width
    key_n = span_t * span_h * width
    block_valid = jnp.stack(
        [
            key_valid[f : f + span_t, TH * rt : TH * rt + span_h].reshape(-1)
            for f in range(frame_count)
            for rt in range(row_tiles)
        ]
    )
    apart_t = jnp.abs(jnp.arange(span_t, dtype=jnp.int32) - TT)
    apart_h = jnp.abs(jnp.arange(span_h, dtype=jnp.int32) // TH - 1)
    near = (apart_t[None, :, None, None] <= window[:, 0, None, None, None]) & (
        apart_h[None, None, :, None] <= window[:, 1, None, None, None]
    )
    near = jnp.broadcast_to(near, (HEADS, span_t, span_h, width)).reshape(HEADS, 1, key_n)
    key_mask = (near & (block_valid[None] > 0)).astype(jnp.float32).reshape(HEADS, blocks, 1, key_n)
    column_tiles = jnp.arange(width, dtype=jnp.int32) // TW
    key_cols = jnp.tile(column_tiles, span_t * span_h).reshape(1, key_n)
    query_cols = jnp.tile(column_tiles, TH)
    query_lo = (query_cols[None, :] - window[:, 2, None]).reshape(HEADS, query_n, 1)
    query_hi = (query_cols[None, :] + window[:, 2, None]).reshape(HEADS, query_n, 1)
    query_ok = query_valid.reshape(blocks, query_n, 1).astype(jnp.float32)
    assert frame_count == 2 * TT
    mask_rows = key_mask.reshape(HEADS, blocks, span_t, span_h, width)
    halo_masks, own_masks = [], []
    for block in range(blocks):
        first_frame_block = block // row_tiles == 0
        halo_frames = slice(0, TT) if first_frame_block else slice(span_t - TT, span_t)
        own_frames = slice(TT, span_t) if first_frame_block else slice(0, frame_count)
        halo_masks.append(mask_rows[:, block, halo_frames].reshape(HEADS, 1, -1))
        own_masks.append(mask_rows[:, block, own_frames].reshape(HEADS, 1, -1))
    halo_mask = jnp.stack(halo_masks, axis=1)
    own_mask = jnp.stack(own_masks, axis=1)
    halo_cols = jnp.tile(column_tiles, TT * span_h).reshape(1, -1)
    own_cols = jnp.tile(column_tiles, frame_count * span_h).reshape(1, -1)
    out = None
    for group, pieces in enumerate(groups):
        masks = (halo_mask, own_mask, query_lo, query_hi, halo_cols, own_cols, query_ok)
        query = project(modulated, full_weight, group * group_cols, group_cols, q_gain)
        query = query.reshape(frame_count, row_count, width, group_cols)
        out = tile_attention(query, pieces, masks, group, out)
    return out


def attention_kernel(
    q_ref, mk_ref, mv_ref, tk_ref, tv_ref, bk_ref, bv_ref,
    hm_ref, om_ref, lo_ref, hi_ref, hc_ref, oc_ref, qv_ref, o_ref,
):
    span_h = 3 * TH
    width = q_ref.shape[2]
    scale = 1.0 / float(HDIM) ** 0.5
    halo_ok = (hc_ref[...] >= lo_ref[0]) & (hc_ref[...] <= hi_ref[0])
    own_ok = (oc_ref[...] >= lo_ref[0]) & (oc_ref[...] <= hi_ref[0])
    for block in range(q_ref.shape[0] * ROW_TILES):
        frame, tile = divmod(block, ROW_TILES)
        row = tile * TH
        hk_ref, hv_ref = (tk_ref, tv_ref) if frame == 0 else (bk_ref, bv_ref)
        query = q_ref[frame, row : row + TH].reshape(TH * width, HDIM)
        pieces = (
            (hk_ref, hv_ref, halo_ok & (hm_ref[0, block] > 0.0)),
            (mk_ref, mv_ref, own_ok & (om_ref[0, block] > 0.0)),
        )
        terms, values = [], []
        for k_ref, v_ref, allowed in pieces:
            key = k_ref[0, :, row : row + span_h].reshape(-1, HDIM)
            values.append(v_ref[0, :, row : row + span_h].reshape(-1, HDIM))
            scores = lax.dot_general(
                query, key, (((1,), (1,)), ((), ())), preferred_element_type=jnp.float32
            ) * scale
            terms.append(jnp.where(allowed, jnp.exp(scores), jnp.float32(0.0)))
        total = jnp.sum(terms[0], axis=-1, keepdims=True) + jnp.sum(terms[1], axis=-1, keepdims=True)
        seen = qv_ref[block] > 0.0
        inverse = 1.0 / jnp.where(seen, total, jnp.float32(1.0))
        result = jnp.dot(
            (terms[0] * inverse).astype(jnp.bfloat16), values[0], preferred_element_type=jnp.float32
        ) + jnp.dot(
            (terms[1] * inverse).astype(jnp.bfloat16), values[1], preferred_element_type=jnp.float32
        )
        result = jnp.where(seen, result, jnp.float32(0.0)).astype(jnp.bfloat16)
        o_ref[frame, row : row + TH] = result.reshape(TH, width, HDIM)


ROW_TILES = 2


def tile_attention(query, pieces, masks, group, out):
    frames, rows, width, group_cols = query.shape
    middle, top, bottom = pieces
    heads = group_cols // HDIM
    out_shape = (frames, rows, width, masks[2].shape[0] * HDIM)
    first = group * heads
    assert rows // TH == ROW_TILES
    blocks = frames * ROW_TILES
    halo_mask, own_mask, query_lo, query_hi, halo_cols, own_cols, query_ok = masks
    query_n = TH * width
    q_spec = pl.BlockSpec((frames, rows, width, HDIM), lambda h: (0, 0, 0, h))
    o_spec = pl.BlockSpec((frames, rows, width, HDIM), lambda h: (0, 0, 0, first + h))

    def piece_specs(piece):
        shape = (1, *piece.shape[1:-1], HDIM)
        return [
            pl.BlockSpec(shape, lambda h: (0, 0, 0, 0, h)),
            pl.BlockSpec(shape, lambda h: (1, 0, 0, 0, h)),
        ]

    in_specs = [q_spec] + piece_specs(middle) + piece_specs(top) + piece_specs(bottom) + [
        pl.BlockSpec((1, blocks, 1, halo_mask.shape[-1]), lambda h: (first + h, 0, 0, 0)),
        pl.BlockSpec((1, blocks, 1, own_mask.shape[-1]), lambda h: (first + h, 0, 0, 0)),
        pl.BlockSpec((1, query_n, 1), lambda h: (first + h, 0, 0)),
        pl.BlockSpec((1, query_n, 1), lambda h: (first + h, 0, 0)),
        pl.BlockSpec((1, halo_cols.shape[-1]), lambda h: (0, 0)),
        pl.BlockSpec((1, own_cols.shape[-1]), lambda h: (0, 0)),
        pl.BlockSpec((blocks, query_n, 1), lambda h: (0, 0, 0)),
    ]
    operands = [query, middle, middle, top, top, bottom, bottom, halo_mask, own_mask,
                query_lo, query_hi, halo_cols, own_cols, query_ok]
    aliases = {}
    kernel = attention_kernel
    if out is not None:
        count = len(operands)
        in_specs.append(pl.BlockSpec(memory_space=pl.ANY))
        operands.append(out)
        aliases = {count: 0}
        kernel = lambda *refs: attention_kernel(*refs[:count], refs[count + 1])
    return pl.pallas_call(
        kernel,
        grid=(heads,),
        in_specs=in_specs,
        out_specs=o_spec,
        out_shape=jax.ShapeDtypeStruct(out_shape, jnp.bfloat16),
        input_output_aliases=aliases,
    )(*operands)


PROJECT_COLS = 256


def projection_kernel(x_ref, w_ref, g_ref, o_ref, *, normalize):
    acc = jnp.dot(x_ref[...], w_ref[...], preferred_element_type=jnp.float32)
    for part in range(acc.shape[1] // HDIM):
        piece = acc[:, part * HDIM : (part + 1) * HDIM]
        if normalize:
            power = jnp.mean(piece * piece, axis=-1, keepdims=True)
            piece = piece * lax.rsqrt(power + EPS) * g_ref[...]
        o_ref[:, part * HDIM : (part + 1) * HDIM] = piece.astype(o_ref.dtype)


def project(x, w, start, count, gain):
    tokens, features = x.shape
    cols = PROJECT_COLS
    normalize = gain is not None
    gain = gain.reshape(1, HDIM) if normalize else jnp.ones((1, HDIM), jnp.float32)
    first = start // cols
    return pl.pallas_call(
        functools.partial(projection_kernel, normalize=normalize),
        grid=(count // cols,),
        in_specs=[
            pl.BlockSpec((tokens, features), lambda j: (0, 0)),
            pl.BlockSpec((features, cols), lambda j: (0, first + j)),
            pl.BlockSpec((1, HDIM), lambda j: (0, 0)),
        ],
        out_specs=pl.BlockSpec((tokens, cols), lambda j: (0, j)),
        out_shape=jax.ShapeDtypeStruct((tokens, count), jnp.bfloat16),
    )(x, w, gain)


MESH = pl.DeviceIdType.MESH


def band_gather_kernel(w_ref, out_ref, local_sem, send_sem, recv_sem):
    count = lax.axis_size("height")
    me = lax.axis_index("height")
    frame_block = lax.axis_index("tm")
    barrier = pltpu.get_barrier_semaphore()
    for step in range(1, count):
        peer = lax.rem(me + step, count)
        pl.semaphore_signal(barrier, inc=1, device_id=(frame_block, peer), device_id_type=MESH)
    pl.semaphore_wait(barrier, count - 1)
    own = pltpu.make_async_copy(w_ref, out_ref.at[me], local_sem)
    own.start()
    copies = []
    for step in range(1, count):
        peer = lax.rem(me + step, count)
        copy = pltpu.make_async_remote_copy(
            src_ref=w_ref,
            dst_ref=out_ref.at[me],
            send_sem=send_sem.at[step],
            recv_sem=recv_sem.at[me],
            device_id=(frame_block, peer),
            device_id_type=MESH,
        )
        copy.start()
        copies.append(copy)
    for copy in copies:
        copy.wait_send()
    for step in range(1, count):
        source = lax.rem(me + count - step, count)
        incoming = pltpu.make_async_remote_copy(
            src_ref=w_ref,
            dst_ref=out_ref.at[source],
            send_sem=send_sem.at[step],
            recv_sem=recv_sem.at[source],
            device_id=(frame_block, source),
            device_id_type=MESH,
        )
        incoming.wait_recv()
    own.wait()


def band_gather(w):
    rows, cols = w.shape
    count = lax.axis_size("height")
    gathered = pl.pallas_call(
        band_gather_kernel,
        in_specs=[pl.BlockSpec(memory_space=pl.ANY)],
        out_specs=pl.BlockSpec(memory_space=pl.ANY),
        out_shape=jax.ShapeDtypeStruct((count, rows, cols), w.dtype),
        scratch_shapes=[
            pltpu.SemaphoreType.DMA(()),
            pltpu.SemaphoreType.DMA((count,)),
            pltpu.SemaphoreType.DMA((count,)),
        ],
        compiler_params=pltpu.CompilerParams(collective_id=0, has_side_effects=True),
    )(w)
    return gathered.reshape(count * rows, cols)


def projection_kv_kernel(x_ref, w_ref, g_ref, o_ref):
    acc = jnp.dot(x_ref[...], w_ref[...], preferred_element_type=jnp.float32)
    is_key = pl.program_id(0) < pl.num_programs(0) // 2
    for part in range(acc.shape[1] // HDIM):
        piece = acc[:, part * HDIM : (part + 1) * HDIM]
        power = jnp.mean(piece * piece, axis=-1, keepdims=True)
        scale = jnp.where(is_key, lax.rsqrt(power + EPS), jnp.float32(1.0))
        gain = jnp.where(is_key, g_ref[...], jnp.float32(1.0))
        normed = jnp.where(is_key, piece * scale * gain, piece)
        o_ref[0, :, part * HDIM : (part + 1) * HDIM] = normed.astype(o_ref.dtype)


def project_kv(x, w, start, count, gain):
    tokens, features = x.shape
    cols = PROJECT_COLS
    inner = w.shape[1] // 3
    steps = count // cols
    key_first = (inner + start) // cols
    value_first = (2 * inner + start) // cols

    def weight_block(j):
        return (0, jnp.where(j < steps, key_first + j, value_first + j - steps))

    return pl.pallas_call(
        projection_kv_kernel,
        grid=(2 * steps,),
        in_specs=[
            pl.BlockSpec((tokens, features), lambda j: (0, 0)),
            pl.BlockSpec((features, cols), weight_block),
            pl.BlockSpec((1, HDIM), lambda j: (0, 0)),
        ],
        out_specs=pl.BlockSpec((1, tokens, cols), lambda j: (j // steps, 0, j % steps)),
        out_shape=jax.ShapeDtypeStruct((2, tokens, count), jnp.bfloat16),
    )(x, w, gain.reshape(1, HDIM))


def solution(mesh):
    in_specs = (
        P("tm", "height", None, None),
        P(),
        P(),
        P(("tm", "height"), None),
        P(),
        P(),
        P(),
        P(),
    )
    out_specs = P("tm", "height", None, None)
    return jax.shard_map(
        per_device, mesh=mesh, in_specs=in_specs, out_specs=out_specs, check_vma=False
    )
```

```python
import functools

import jax
import jax.numpy as jnp
from jax import lax
from jax.sharding import PartitionSpec as P
from jax.experimental import pallas as pl
from jax.experimental.pallas import tpu as pltpu

HDIM = 128
HEADS = 12
TT = 1
TH = 2
TW = 8
GROUPS = 2


EPS = 1e-06


def with_halo(cells, sides, width):
    for axis, dim in sides:
        count = lax.axis_size(axis)
        ends = count - 1
        head = lax.slice_in_dim(cells, 0, width, axis=dim)
        tail = lax.slice_in_dim(cells, cells.shape[dim] - width, cells.shape[dim], axis=dim)
        cells = jnp.concatenate(
            [
                lax.ppermute(tail, axis, [(i, (i + 1) % count) for i in range(ends)]),
                cells,
                lax.ppermute(head, axis, [((i + 1) % count, i) for i in range(ends)]),
            ],
            axis=dim,
        )
    return cells


def modulate(tokens, mod_scale, mod_shift):
    values = tokens.astype(jnp.float32)
    mean = jnp.mean(values, axis=-1, keepdims=True)
    centred = values - mean
    variance = jnp.mean(centred * centred, axis=-1, keepdims=True)
    normed = centred * lax.rsqrt(variance + EPS)
    return (normed * (1.0 + mod_scale) + mod_shift).astype(jnp.bfloat16)


def head_norm(values, gain):
    power = jnp.mean(values * values, axis=-1, keepdims=True)
    return (values * lax.rsqrt(power + EPS) * gain).astype(jnp.bfloat16)


def tile_coords(frames, rows, width):
    shape = (frames.shape[0], rows.shape[0], width)
    columns = jnp.arange(width, dtype=jnp.int32)
    frame_tiles = jnp.broadcast_to((frames // TT)[:, None, None], shape).reshape(-1)
    row_tiles = jnp.broadcast_to((rows // TH)[None, :, None], shape).reshape(-1)
    column_tiles = jnp.broadcast_to((columns // TW)[None, None, :], shape).reshape(-1)
    return (frame_tiles, row_tiles, column_tiles)


def per_device(tokens, mod_scale, mod_shift, w_qkv, q_gain, k_gain, window, valid):
    frame_count, row_count, width, features = tokens.shape
    token_count = frame_count * row_count * width
    modulated = modulate(tokens.reshape(token_count, features), mod_scale, mod_shift)
    band_weight = band_gather(w_qkv)
    full_weight = lax.all_gather(band_weight, "tm", axis=0, tiled=True)
    inner = full_weight.shape[1] // 3
    group_cols = inner // GROUPS
    tiled = (frame_count // TT, TT, row_count // TH, TH, width, group_cols)
    groups = []
    query = project(modulated, full_weight, 0, inner, q_gain)
    for group in range(GROUPS):
        start = group * group_cols
        stacked = project_kv(modulated, full_weight, start, group_cols, k_gain)
        stacked = stacked.reshape(2, *tiled)
        rows_done = with_halo(stacked, (("height", 3),), 1)
        rows_done = rows_done.reshape(2, frame_count, row_count + 2 * TH, width, group_cols)
        if group == 0:
            rows_done, query = lax.optimization_barrier((rows_done, query))
        count = lax.axis_size("tm")
        before = lax.ppermute(
            rows_done[:, frame_count - TT :], "tm", [(i, i + 1) for i in range(count - 1)]
        )
        after = lax.ppermute(rows_done[:, :TT], "tm", [(i + 1, i) for i in range(count - 1)])
        groups.append((rows_done, before, after))
    frames_ext = frame_count + 2 * TT
    rows_ext = row_count + 2 * TH
    frame_block = lax.axis_index("tm")
    row_block = lax.axis_index("height")
    first_frame = frame_block * frame_count
    first_row = row_block * row_count
    zero = jnp.int32(0)
    valid_pad = jnp.pad(valid, ((TT, TT), (TH, TH), (0, 0)))
    key_valid = lax.dynamic_slice(
        valid_pad, (first_frame, first_row, zero), (frames_ext, rows_ext, width)
    )
    query_valid = lax.dynamic_slice(
        valid, (first_frame, first_row, zero), (frame_count, row_count, width)
    )
    row_tiles = row_count // TH
    blocks = frame_count * row_tiles
    span_t = 2 * TT + 1
    span_h = 3 * TH
    query_n = TH * width
    key_n = span_t * span_h * width
    block_valid = jnp.stack(
        [
            key_valid[f : f + span_t, TH * rt : TH * rt + span_h].reshape(-1)
            for f in range(frame_count)
            for rt in range(row_tiles)
        ]
    )
    apart_t = jnp.abs(jnp.arange(span_t, dtype=jnp.int32) - TT)
    apart_h = jnp.abs(jnp.arange(span_h, dtype=jnp.int32) // TH - 1)
    near = (apart_t[None, :, None, None] <= window[:, 0, None, None, None]) & (
        apart_h[None, None, :, None] <= window[:, 1, None, None, None]
    )
    near = jnp.broadcast_to(near, (HEADS, span_t, span_h, width)).reshape(HEADS, 1, key_n)
    key_mask = (near & (block_valid[None] > 0)).astype(jnp.float32).reshape(HEADS, blocks, 1, key_n)
    column_tiles = jnp.arange(width, dtype=jnp.int32) // TW
    key_cols = jnp.tile(column_tiles, span_t * span_h).reshape(1, key_n)
    query_cols = jnp.tile(column_tiles, TH)
    query_lo = (query_cols[None, :] - window[:, 2, None]).reshape(HEADS, query_n, 1)
    query_hi = (query_cols[None, :] + window[:, 2, None]).reshape(HEADS, query_n, 1)
    query_ok = query_valid.reshape(blocks, query_n, 1).astype(jnp.float32)
    query_grid = query.reshape(frame_count, row_count, width, inner)
    assert frame_count == 2 * TT
    mask_rows = key_mask.reshape(HEADS, blocks, span_t, span_h, width)
    halo_masks, own_masks = [], []
    for block in range(blocks):
        first_frame_block = block // row_tiles == 0
        halo_frames = slice(0, TT) if first_frame_block else slice(span_t - TT, span_t)
        own_frames = slice(TT, span_t) if first_frame_block else slice(0, frame_count)
        halo_masks.append(mask_rows[:, block, halo_frames].reshape(HEADS, 1, -1))
        own_masks.append(mask_rows[:, block, own_frames].reshape(HEADS, 1, -1))
    halo_mask = jnp.stack(halo_masks, axis=1)
    own_mask = jnp.stack(own_masks, axis=1)
    halo_cols = jnp.tile(column_tiles, TT * span_h).reshape(1, -1)
    own_cols = jnp.tile(column_tiles, frame_count * span_h).reshape(1, -1)
    out = None
    for group, pieces in enumerate(groups):
        masks = (halo_mask, own_mask, query_lo, query_hi, halo_cols, own_cols, query_ok)
        out = tile_attention(query_grid, pieces, masks, group, out)
    return out


def attention_kernel(
    q_ref, mk_ref, mv_ref, tk_ref, tv_ref, bk_ref, bv_ref,
    hm_ref, om_ref, lo_ref, hi_ref, hc_ref, oc_ref, qv_ref, o_ref,
):
    span_h = 3 * TH
    width = q_ref.shape[2]
    scale = 1.0 / float(HDIM) ** 0.5
    halo_ok = (hc_ref[...] >= lo_ref[0]) & (hc_ref[...] <= hi_ref[0])
    own_ok = (oc_ref[...] >= lo_ref[0]) & (oc_ref[...] <= hi_ref[0])
    for block in range(q_ref.shape[0] * ROW_TILES):
        frame, tile = divmod(block, ROW_TILES)
        row = tile * TH
        hk_ref, hv_ref = (tk_ref, tv_ref) if frame == 0 else (bk_ref, bv_ref)
        query = q_ref[frame, row : row + TH].reshape(TH * width, HDIM)
        pieces = (
            (hk_ref, hv_ref, halo_ok & (hm_ref[0, block] > 0.0)),
            (mk_ref, mv_ref, own_ok & (om_ref[0, block] > 0.0)),
        )
        terms, values = [], []
        for k_ref, v_ref, allowed in pieces:
            key = k_ref[0, :, row : row + span_h].reshape(-1, HDIM)
            values.append(v_ref[0, :, row : row + span_h].reshape(-1, HDIM))
            scores = lax.dot_general(
                query, key, (((1,), (1,)), ((), ())), preferred_element_type=jnp.float32
            ) * scale
            terms.append(jnp.where(allowed, jnp.exp(scores), jnp.float32(0.0)))
        total = jnp.sum(terms[0], axis=-1, keepdims=True) + jnp.sum(terms[1], axis=-1, keepdims=True)
        seen = qv_ref[block] > 0.0
        inverse = 1.0 / jnp.where(seen, total, jnp.float32(1.0))
        result = jnp.dot(
            (terms[0] * inverse).astype(jnp.bfloat16), values[0], preferred_element_type=jnp.float32
        ) + jnp.dot(
            (terms[1] * inverse).astype(jnp.bfloat16), values[1], preferred_element_type=jnp.float32
        )
        result = jnp.where(seen, result, jnp.float32(0.0)).astype(jnp.bfloat16)
        o_ref[frame, row : row + TH] = result.reshape(TH, width, HDIM)


ROW_TILES = 2


def tile_attention(query, pieces, masks, group, out):
    frames, rows, width, inner = query.shape
    middle, top, bottom = pieces
    heads = middle.shape[-1] // HDIM
    first = group * heads
    assert rows // TH == ROW_TILES
    blocks = frames * ROW_TILES
    halo_mask, own_mask, query_lo, query_hi, halo_cols, own_cols, query_ok = masks
    query_n = TH * width
    q_spec = pl.BlockSpec((frames, rows, width, HDIM), lambda h: (0, 0, 0, first + h))

    def piece_specs(piece):
        shape = (1, *piece.shape[1:-1], HDIM)
        return [
            pl.BlockSpec(shape, lambda h: (0, 0, 0, 0, h)),
            pl.BlockSpec(shape, lambda h: (1, 0, 0, 0, h)),
        ]

    in_specs = [q_spec] + piece_specs(middle) + piece_specs(top) + piece_specs(bottom) + [
        pl.BlockSpec((1, blocks, 1, halo_mask.shape[-1]), lambda h: (first + h, 0, 0, 0)),
        pl.BlockSpec((1, blocks, 1, own_mask.shape[-1]), lambda h: (first + h, 0, 0, 0)),
        pl.BlockSpec((1, query_n, 1), lambda h: (first + h, 0, 0)),
        pl.BlockSpec((1, query_n, 1), lambda h: (first + h, 0, 0)),
        pl.BlockSpec((1, halo_cols.shape[-1]), lambda h: (0, 0)),
        pl.BlockSpec((1, own_cols.shape[-1]), lambda h: (0, 0)),
        pl.BlockSpec((blocks, query_n, 1), lambda h: (0, 0, 0)),
    ]
    operands = [query, middle, middle, top, top, bottom, bottom, halo_mask, own_mask,
                query_lo, query_hi, halo_cols, own_cols, query_ok]
    aliases = {}
    kernel = attention_kernel
    if out is not None:
        count = len(operands)
        in_specs.append(pl.BlockSpec(memory_space=pl.ANY))
        operands.append(out)
        aliases = {count: 0}
        kernel = lambda *refs: attention_kernel(*refs[:count], refs[count + 1])
    return pl.pallas_call(
        kernel,
        grid=(heads,),
        in_specs=in_specs,
        out_specs=q_spec,
        out_shape=jax.ShapeDtypeStruct(query.shape, jnp.bfloat16),
        input_output_aliases=aliases,
    )(*operands)


PROJECT_COLS = 256


def projection_kernel(x_ref, w_ref, g_ref, o_ref, *, normalize):
    acc = jnp.dot(x_ref[...], w_ref[...], preferred_element_type=jnp.float32)
    for part in range(acc.shape[1] // HDIM):
        piece = acc[:, part * HDIM : (part + 1) * HDIM]
        if normalize:
            power = jnp.mean(piece * piece, axis=-1, keepdims=True)
            piece = piece * lax.rsqrt(power + EPS) * g_ref[...]
        o_ref[:, part * HDIM : (part + 1) * HDIM] = piece.astype(o_ref.dtype)


def project(x, w, start, count, gain):
    tokens, features = x.shape
    cols = PROJECT_COLS
    normalize = gain is not None
    gain = gain.reshape(1, HDIM) if normalize else jnp.ones((1, HDIM), jnp.float32)
    first = start // cols
    return pl.pallas_call(
        functools.partial(projection_kernel, normalize=normalize),
        grid=(count // cols,),
        in_specs=[
            pl.BlockSpec((tokens, features), lambda j: (0, 0)),
            pl.BlockSpec((features, cols), lambda j: (0, first + j)),
            pl.BlockSpec((1, HDIM), lambda j: (0, 0)),
        ],
        out_specs=pl.BlockSpec((tokens, cols), lambda j: (0, j)),
        out_shape=jax.ShapeDtypeStruct((tokens, count), jnp.bfloat16),
    )(x, w, gain)


MESH = pl.DeviceIdType.MESH


def band_gather_kernel(w_ref, out_ref, local_sem, send_sem, recv_sem):
    count = lax.axis_size("height")
    me = lax.axis_index("height")
    frame_block = lax.axis_index("tm")
    barrier = pltpu.get_barrier_semaphore()
    for step in range(1, count):
        peer = lax.rem(me + step, count)
        pl.semaphore_signal(barrier, inc=1, device_id=(frame_block, peer), device_id_type=MESH)
    pl.semaphore_wait(barrier, count - 1)
    own = pltpu.make_async_copy(w_ref, out_ref.at[me], local_sem)
    own.start()
    copies = []
    for step in range(1, count):
        peer = lax.rem(me + step, count)
        copy = pltpu.make_async_remote_copy(
            src_ref=w_ref,
            dst_ref=out_ref.at[me],
            send_sem=send_sem.at[step],
            recv_sem=recv_sem.at[me],
            device_id=(frame_block, peer),
            device_id_type=MESH,
        )
        copy.start()
        copies.append(copy)
    for copy in copies:
        copy.wait_send()
    for step in range(1, count):
        source = lax.rem(me + count - step, count)
        incoming = pltpu.make_async_remote_copy(
            src_ref=w_ref,
            dst_ref=out_ref.at[source],
            send_sem=send_sem.at[step],
            recv_sem=recv_sem.at[source],
            device_id=(frame_block, source),
            device_id_type=MESH,
        )
        incoming.wait_recv()
    own.wait()


def band_gather(w):
    rows, cols = w.shape
    count = lax.axis_size("height")
    gathered = pl.pallas_call(
        band_gather_kernel,
        in_specs=[pl.BlockSpec(memory_space=pl.ANY)],
        out_specs=pl.BlockSpec(memory_space=pl.ANY),
        out_shape=jax.ShapeDtypeStruct((count, rows, cols), w.dtype),
        scratch_shapes=[
            pltpu.SemaphoreType.DMA(()),
            pltpu.SemaphoreType.DMA((count,)),
            pltpu.SemaphoreType.DMA((count,)),
        ],
        compiler_params=pltpu.CompilerParams(collective_id=0, has_side_effects=True),
    )(w)
    return gathered.reshape(count * rows, cols)


def projection_kv_kernel(x_ref, w_ref, g_ref, o_ref):
    acc = jnp.dot(x_ref[...], w_ref[...], preferred_element_type=jnp.float32)
    is_key = pl.program_id(0) < pl.num_programs(0) // 2
    for part in range(acc.shape[1] // HDIM):
        piece = acc[:, part * HDIM : (part + 1) * HDIM]
        power = jnp.mean(piece * piece, axis=-1, keepdims=True)
        scale = jnp.where(is_key, lax.rsqrt(power + EPS), jnp.float32(1.0))
        gain = jnp.where(is_key, g_ref[...], jnp.float32(1.0))
        normed = jnp.where(is_key, piece * scale * gain, piece)
        o_ref[0, :, part * HDIM : (part + 1) * HDIM] = normed.astype(o_ref.dtype)


def project_kv(x, w, start, count, gain):
    tokens, features = x.shape
    cols = PROJECT_COLS
    inner = w.shape[1] // 3
    steps = count // cols
    key_first = (inner + start) // cols
    value_first = (2 * inner + start) // cols

    def weight_block(j):
        return (0, jnp.where(j < steps, key_first + j, value_first + j - steps))

    return pl.pallas_call(
        projection_kv_kernel,
        grid=(2 * steps,),
        in_specs=[
            pl.BlockSpec((tokens, features), lambda j: (0, 0)),
            pl.BlockSpec((features, cols), weight_block),
            pl.BlockSpec((1, HDIM), lambda j: (0, 0)),
        ],
        out_specs=pl.BlockSpec((1, tokens, cols), lambda j: (j // steps, 0, j % steps)),
        out_shape=jax.ShapeDtypeStruct((2, tokens, count), jnp.bfloat16),
    )(x, w, gain.reshape(1, HDIM))


def solution(mesh):
    in_specs = (
        P("tm", "height", None, None),
        P(),
        P(),
        P(("tm", "height"), None),
        P(),
        P(),
        P(),
        P(),
    )
    out_specs = P("tm", "height", None, None)
    return jax.shard_map(
        per_device, mesh=mesh, in_specs=in_specs, out_specs=out_specs, check_vma=False
    )
```
